32 devices in a mesh: dp: 8 (over y, x, core), tensor: 4 (over z).
Axes of the slice: x: 2, y: 2, z: 4, core: 2. Of those that a mesh axis runs over, the one named last changes fastest.
Arguments:
- features: bfloat16 [528, 32, 768], P(None, 'dp'), may hold values from -6 to 6
- mask_starts: int32 [32, 8], P('dp'), may hold values from -10 to 518, as said below
- mask_vector: float32 [768], replicated, may hold values from -6 to 6
- query_weight: bfloat16 [768, 768], P(None, 'tensor'), may hold values from -0.3125 to 0.3125
- query_bias: float32 [768], P('tensor'), may hold values from -2 to 2
- key_weight: bfloat16 [768, 768], P(None, 'tensor'), may hold values from -0.3125 to 0.3125
- value_weight: bfloat16 [768, 768], P(None, 'tensor'), may hold values from -0.21875 to 0.21875
- value_bias: float32 [768], P('tensor'), may hold values from -2 to 2
- output_weight: bfloat16 [768, 768], P('tensor'), may hold values from -1.75 to 1.75
- output_bias: float32 [768], replicated, may hold values from -2 to 2
- attn_gain: float32 [768], replicated, may hold values from 0.5 to 1.5
- attn_shift: float32 [768], replicated, may hold values from -2 to 2
- up_weight: bfloat16 [768, 3072], P(None, 'tensor'), may hold values from -0.21875 to 0.21875
- up_bias: float32 [3072], P('tensor'), may hold values from -2 to 2
- down_weight: bfloat16 [3072, 768], P('tensor'), may hold values from -0.15625 to 0.15625
- down_bias: float32 [768], replicated, may hold values from -2 to 2
- final_gain: float32 [768], replicated, may hold values from 0.5 to 1.5
- final_shift: float32 [768], replicated, may hold values from -2 to 2
- grad_output: bfloat16 [528, 32, 768], P('tensor', 'dp'), may hold values from -6 to 6
Outputs:
- layer_output: bfloat16 [528, 32, 768], P('tensor', 'dp')
- input_grad: bfloat16 [528, 32, 768], P('tensor', 'dp')
- grad_mask_vector: float32 [768], replicated
- grad_query_weight: float32 [768, 768], P(None, 'tensor')
- grad_query_bias: float32 [768], P('tensor')
- grad_key_weight: float32 [768, 768], P(None, 'tensor')
- grad_value_weight: float32 [768, 768], P(None, 'tensor')
- grad_value_bias: float32 [768], P('tensor')
- grad_output_weight: float32 [768, 768], P('tensor')
- grad_output_bias: float32 [768], replicated
- grad_attn_gain: float32 [768], replicated
- grad_attn_shift: float32 [768], replicated
- grad_up_weight: float32 [768, 3072], P(None, 'tensor')
- grad_up_bias: float32 [3072], P('tensor')
- grad_down_weight: float32 [3072, 768], P('tensor')
- grad_down_bias: float32 [768], replicated
- grad_final_gain: float32 [768], replicated
- grad_final_shift: float32 [768], replicated
The draws below stay inside these ranges and needn't reach their ends.
Inputs may be any that keep to these rules, and one draw needn't show every extreme that they name: `mask_starts`: each item's used span slots come first; a start of -10 marks an unused slot; spans may intersect; the number of spans differs from item to item.
All inputs are finite; a program needn't handle non-finite values.
Results may differ from the reference program's by a relative error of at most 0.023.
Values may be sent and summed in bfloat16 or wider, within the bound.
A program may use at most 192 MiB of HBM per device.

```python
import jax
import jax.numpy as jnp
from jax import lax

D = 768
HEAD = 64
HEAD_SLOTS_DEV = 3
FF_DEV = 768
FRAMES = 528
SPAN = 10
MAXSPANS = 8
ITEMS_DEV = 4
HEADS = 10
FF = 2688
ITEMS = 32
N_DP = 8
N_TENSOR = 4


def draw_mask_starts(key, part):
    count_key, start_key = jax.random.split(jax.random.fold_in(key, 11))
    span_counts = jax.random.randint(count_key, (ITEMS,), 1, MAXSPANS + 1)
    span_counts = jnp.where(jnp.arange(ITEMS) == 0, 1, span_counts)
    raw_starts = jax.random.randint(start_key, (ITEMS, MAXSPANS), 0, FRAMES - SPAN + 1)
    used_slots = jnp.arange(MAXSPANS)[None, :] < span_counts[:, None]
    return jnp.where(used_slots, raw_starts, -SPAN).astype(jnp.int32)


def block_levels(stream_key, shape, cuts, least, high):
    gain = 1.0
    for axis_at, shards_of in cuts:
        steps = jax.random.uniform(jax.random.fold_in(jax.random.fold_in(stream_key, 6), axis_at), (shards_of,), jnp.float32, least / len(cuts), high / len(cuts))
        gain = gain * jnp.repeat(jnp.exp(steps), shape[axis_at] // shards_of).reshape((-1,) + (1,) * (len(shape) - 1 - axis_at))
    return gain


def scatter_about(rng, dims, scale, most, shards=(), kind=jnp.bfloat16):
    gain = block_levels(rng, dims, shards, -0.22, 0.18) if shards else 1.0
    values = jax.random.normal(rng, dims, jnp.float32) * scale * gain
    return jnp.minimum(jnp.maximum(values, -most), most).astype(kind)


def setup_inputs(seed: int = 0) -> dict:
    seeds = jax.random.split(jax.random.key(seed), 20)
    return {
        "features": scatter_about(seeds[0], (FRAMES, ITEMS, D), 1.0, 6.0, ((1, 8),)),
        "mask_starts": draw_mask_starts(jax.random.fold_in(seeds[19], 71), 0),
        "mask_vector": scatter_about(seeds[2], (D,), 1.0, 6.0, (), jnp.float32),
        "query_weight": scatter_about(seeds[3], (D, N_TENSOR * HEAD_SLOTS_DEV * HEAD), (D // 2) ** -0.5, 0.3125, ((1, 4),)),
        "query_bias": scatter_about(seeds[4], (N_TENSOR * HEAD_SLOTS_DEV * HEAD,), 0.3, 2.0, ((0, 4),), jnp.float32),
        "key_weight": scatter_about(seeds[5], (D, N_TENSOR * HEAD_SLOTS_DEV * HEAD), (D // 2) ** -0.5, 0.3125, ((1, 4),)),
        "value_weight": scatter_about(seeds[6], (D, N_TENSOR * HEAD_SLOTS_DEV * HEAD), D ** -0.5, 0.21875, ((1, 4),)),
        "value_bias": scatter_about(seeds[7], (N_TENSOR * HEAD_SLOTS_DEV * HEAD,), 0.3, 2.0, ((0, 4),), jnp.float32),
        "output_weight": scatter_about(seeds[8], (N_TENSOR * HEAD_SLOTS_DEV * HEAD, D), (HEADS * HEAD // 48) ** -0.5, 1.75, ((0, 4),)),
        "output_bias": scatter_about(seeds[9], (D,), 0.3, 2.0, (), jnp.float32),
        "attn_gain": jnp.clip(1.0 + 0.1 * jax.random.normal(seeds[10], (D,), jnp.float32), 0.5, 1.5),
        "attn_shift": scatter_about(seeds[11], (D,), 0.3, 2.0, (), jnp.float32),
        "up_weight": scatter_about(seeds[12], (D, N_TENSOR * FF_DEV), D ** -0.5, 0.21875, ((1, 4),)),
        "up_bias": scatter_about(seeds[13], (N_TENSOR * FF_DEV,), 0.3, 2.0, ((0, 4),), jnp.float32),
        "down_weight": scatter_about(seeds[14], (N_TENSOR * FF_DEV, D), (FF // 2) ** -0.5, 0.15625, ((0, 4),)),
        "down_bias": scatter_about(seeds[15], (D,), 0.3, 2.0, (), jnp.float32),
        "final_gain": jnp.clip(1.0 + 0.1 * jax.random.normal(seeds[16], (D,), jnp.float32), 0.5, 1.5),
        "final_shift": scatter_about(seeds[17], (D,), 0.3, 2.0, (), jnp.float32),
        "grad_output": scatter_about(seeds[18], (FRAMES, ITEMS, D), 1.0, 6.0, ((0, 4), (1, 8))),
    }


EPS = 1e-05
HIGH = lax.Precision.HIGHEST

@jax.custom_vjp
def low(v):
    return lax.optimization_barrier(v.astype(jnp.bfloat16)).astype(jnp.float32)

@jax.custom_vjp
def low_back(v):
    return v

def low_keep(v):
    return (low(v), None)

def low_pass(kept, grad):
    return (grad,)

def back_keep(v):
    return (v, None)

def back_low(kept, grad):
    return (low(grad),)
low.defvjp(low_keep, low_pass)
low_back.defvjp(back_keep, back_low)

def normalize(values):
    center = values - lax.optimization_barrier(jnp.mean(values, axis=-1, keepdims=True))
    scaled = lax.rsqrt(lax.optimization_barrier(jnp.mean(center * center, axis=-1, keepdims=True)) + EPS)
    return center * scaled

def project(left, right):
    return jnp.einsum('fid,de->fie', left, right, precision=HIGH)

def live_heads(slot_count):
    column = jnp.arange(slot_count * HEAD, dtype=jnp.int32) // HEAD
    owner_rank = column // HEAD_SLOTS_DEV
    within = column % HEAD_SLOTS_DEV
    keep_mask = within < HEAD_SLOTS_DEV - jnp.where(owner_rank * 2 >= N_TENSOR, 1, 0)
    return jnp.where(keep_mask, 1.0, 0.0).astype(jnp.float32)

def live_hidden(unit_count):
    column = jnp.arange(unit_count, dtype=jnp.int32)
    owner_rank = column // FF_DEV
    within = column % FF_DEV
    keep_mask = within < jnp.where(owner_rank > 0, FF_DEV * 5 // 6, FF_DEV)
    return jnp.where(keep_mask, 1.0, 0.0).astype(jnp.float32)

def masked_frames(starts):
    position = jnp.arange(FRAMES, dtype=jnp.int32)[:, None, None]
    span_hits = (starts[None] <= position) & (position < starts[None] + SPAN)
    return jnp.any(span_hits, axis=2)

def layer(feat_float, starts, params):
    mask_vector, query_weight, query_bias, key_weight, value_weight, value_bias, output_weight, output_bias, attn_gain, attn_shift, up_weight, up_bias, down_weight, down_bias, final_gain, final_shift = params
    item_count = feat_float.shape[1]
    slot_count = query_weight.shape[1] // HEAD
    covered = masked_frames(starts)
    hidden_in = jnp.where(covered[:, :, None], mask_vector[None, None, :], feat_float)
    hidden_low = low(hidden_in)
    query_low = low(low_back(project(hidden_low, query_weight) + query_bias))
    key_low = low(low_back(project(hidden_low, key_weight)))
    value_low = low(low_back(project(hidden_low, value_weight) + value_bias))
    head_shape = (FRAMES, item_count, slot_count, HEAD)
    scores = jnp.einsum('fine,gine->infg', query_low.reshape(head_shape), key_low.reshape(head_shape), precision=HIGH) * 0.125
    scores = low_back(scores)
    prob_low = low(jax.nn.softmax(scores, axis=-1))
    context = jnp.einsum('infg,gine->fine', prob_low, value_low.reshape(head_shape), precision=HIGH)
    context = context.reshape(FRAMES, item_count, slot_count * HEAD)
    context = low(low_back(context * live_heads(slot_count)))
    attended = low_back(project(context, output_weight))
    resid_one = hidden_in + attended + output_bias
    mid_rows = normalize(resid_one) * attn_gain + attn_shift
    pre_up = low_back(project(low(mid_rows), up_weight)) + up_bias
    active = jax.nn.gelu(pre_up, approximate=False) * live_hidden(up_weight.shape[1])
    branch_out = low_back(project(low(active), down_weight))
    resid_two = mid_rows + branch_out + down_bias
    return normalize(resid_two) * final_gain + final_shift

def reference(features, mask_starts, mask_vector, query_weight, query_bias, key_weight, value_weight, value_bias, output_weight, output_bias, attn_gain, attn_shift, up_weight, up_bias, down_weight, down_bias, final_gain, final_shift, grad_output):
    params = (mask_vector.astype(jnp.float32), query_weight.astype(jnp.float32), query_bias.astype(jnp.float32), key_weight.astype(jnp.float32), value_weight.astype(jnp.float32), value_bias.astype(jnp.float32), output_weight.astype(jnp.float32), output_bias.astype(jnp.float32), attn_gain.astype(jnp.float32), attn_shift.astype(jnp.float32), up_weight.astype(jnp.float32), up_bias.astype(jnp.float32), down_weight.astype(jnp.float32), down_bias.astype(jnp.float32), final_gain.astype(jnp.float32), final_shift.astype(jnp.float32))
    feat_groups = features.astype(jnp.float32).reshape(FRAMES, N_DP, ITEMS_DEV, D).transpose(1, 0, 2, 3)
    start_groups = mask_starts.reshape(N_DP, ITEMS_DEV, MAXSPANS)
    grad_groups = grad_output.astype(jnp.float32).reshape(FRAMES, N_DP, ITEMS_DEV, D).transpose(1, 0, 2, 3)

    def one_group(running, group_data):
        feat_float, starts, upstream = group_data
        output, pull_back = jax.vjp(lambda inputs, weights: layer(inputs, starts, weights), feat_float, params)
        input_part, weight_parts = pull_back(upstream)
        running = jax.tree.map(lambda total_sum, addend: total_sum + addend, running, weight_parts)
        return (running, (output, input_part))
    totals, (outputs, input_parts) = lax.scan(one_group, jax.tree.map(jnp.zeros_like, params), (feat_groups, start_groups, grad_groups))
    layer_output = outputs.transpose(1, 0, 2, 3).reshape(FRAMES, ITEMS, D).astype(jnp.bfloat16)
    input_grad = (0.1 * input_parts).transpose(1, 0, 2, 3).reshape(FRAMES, ITEMS, D).astype(jnp.bfloat16)
    return (layer_output, input_grad, totals[0], totals[1], totals[2], totals[3], totals[4], totals[5], totals[6], totals[7], totals[8], totals[9], totals[10], totals[11], totals[12], totals[13], totals[14], totals[15])
```

```python
import jax
import jax.numpy as jnp
from jax import lax
from jax.sharding import PartitionSpec as P

HEAD = 64
SPAN = 10
EPS = 1e-05
BF = jnp.bfloat16
F32 = jnp.float32


def normalize(values):
    center = values - jnp.mean(values, axis=-1, keepdims=True)
    scaled = lax.rsqrt(jnp.mean(center * center, axis=-1, keepdims=True) + EPS)
    return (center * scaled, scaled)


def norm_back(upstream, normed, scaled):
    row_mean = jnp.mean(upstream, axis=-1, keepdims=True)
    row_proj = jnp.mean(upstream * normed, axis=-1, keepdims=True)
    return scaled * (upstream - row_mean - normed * row_proj)


def mm(a, b):
    return jnp.dot(a, b, preferred_element_type=F32)


def mm_rows(a, b):
    return lax.dot_general(a, b, (((0,), (0,)), ((), ())), preferred_element_type=F32)


def mm_cols(a, b):
    return lax.dot_general(a, b, (((1,), (1,)), ((), ())), preferred_element_type=F32)


def gelu_slope(values):
    normal_cdf = 0.5 * (1.0 + jax.scipy.special.erf(values * 0.7071067811865476))
    normal_pdf = jnp.exp(-0.5 * values * values) * 0.3989422804014327
    return normal_cdf + values * normal_pdf


def body(features, mask_starts, mask_vector, query_weight, query_bias, key_weight, value_weight,
         value_bias, output_weight, output_bias, attn_gain, attn_shift, up_weight, up_bias,
         down_weight, down_bias, final_gain, final_shift, grad_output):
    frames, item_count, width = features.shape
    n_t = lax.axis_size("tensor")
    n_d = lax.axis_size("dp")
    rank = lax.axis_index("tensor")
    dpi = lax.axis_index("dp")
    per = item_count // n_t
    slots = query_weight.shape[1] // HEAD
    units = up_weight.shape[1]
    head_live = [slots if 2 * r < n_t else slots - 1 for r in range(n_t)]
    unit_live = [units if r == 0 else units * 5 // 6 for r in range(n_t)]
    rows = width // n_d

    def mine(a):
        step = a.shape[0] // n_d
        return lax.dynamic_slice_in_dim(a, dpi * step, step, 0)

    def gather(a):
        got = lax.all_gather(mine(a), ("tensor", "dp"), axis=0, tiled=True)
        return got.reshape((n_t,) + a.shape)

    qkv_all = gather(jnp.concatenate([query_weight, key_weight, value_weight], axis=1))
    bias_all = lax.all_gather(
        jnp.concatenate([query_bias, value_bias, up_bias]), "tensor", axis=0, tiled=False
    )
    out_all = gather(output_weight)
    up_all = gather(up_weight)
    down_all = gather(down_weight)
    hs = slots * HEAD

    def cols_of(r, which):
        return qkv_all[r, :, which * hs : which * hs + head_live[r] * HEAD]

    wq = jnp.concatenate([cols_of(r, 0) for r in range(n_t)], axis=1)
    wk = jnp.concatenate([cols_of(r, 1) for r in range(n_t)], axis=1)
    wv = jnp.concatenate([cols_of(r, 2) for r in range(n_t)], axis=1)
    bq = jnp.concatenate([bias_all[r, : head_live[r] * HEAD] for r in range(n_t)])
    bv = jnp.concatenate([bias_all[r, hs : hs + head_live[r] * HEAD] for r in range(n_t)])
    bu = jnp.concatenate([bias_all[r, 2 * hs : 2 * hs + unit_live[r]] for r in range(n_t)])
    wo = jnp.concatenate([out_all[r, : head_live[r] * HEAD] for r in range(n_t)], axis=0)
    wu = jnp.concatenate([up_all[r, :, : unit_live[r]] for r in range(n_t)], axis=1)
    wd = jnp.concatenate([down_all[r, : unit_live[r]] for r in range(n_t)], axis=0)
    heads = sum(head_live)

    feat = lax.dynamic_slice_in_dim(features, rank * per, per, 1).transpose(1, 0, 2)
    starts = lax.dynamic_slice_in_dim(mask_starts, rank * per, per, 0)
    all_rows = per * frames
    upstream = lax.all_to_all(
        grad_output.reshape(frames // n_t, n_t, per, width), "tensor", 1, 0, tiled=False
    )
    upstream = upstream.transpose(2, 0, 1, 3).reshape(all_rows, width).astype(F32)
    position = jnp.arange(frames, dtype=jnp.int32)[None, :, None]
    hits = (starts[:, None, :] <= position) & (position < starts[:, None, :] + SPAN)
    covered = jnp.any(hits, axis=2).reshape(all_rows)
    hidden_in = jnp.where(
        covered[:, None], mask_vector[None, :], feat.reshape(all_rows, width).astype(F32)
    )
    x = hidden_in.astype(BF)

    def split(a):
        return a.reshape(per, frames, heads, HEAD).transpose(0, 2, 1, 3)

    def join(a):
        return a.transpose(0, 2, 1, 3).reshape(all_rows, heads * HEAD)

    q = split((mm(x, wq) + bq).astype(BF))
    k = split(mm(x, wk).astype(BF))
    v = split((mm(x, wv) + bv).astype(BF))
    scores = jnp.einsum("infe,inge->infg", q, k, preferred_element_type=F32) * 0.125
    top = jnp.max(scores, axis=-1, keepdims=True)
    shifted = jnp.exp(scores - top)
    total = jnp.sum(shifted, axis=-1, keepdims=True)
    prob_low = (shifted / total).astype(BF)
    log_total = top + jnp.log(total)
    context = join(
        jnp.einsum("infg,inge->infe", prob_low, v, preferred_element_type=F32).astype(BF)
    )
    normed_one, scale_one = normalize(hidden_in + mm(context, wo) + output_bias)
    mid = normed_one * attn_gain + attn_shift
    mid_low = mid.astype(BF)
    pre_up = mm(mid_low, wu) + bu
    active = jax.nn.gelu(pre_up, approximate=False).astype(BF)
    normed_two, scale_two = normalize(mid + mm(active, wd) + down_bias)
    layer_output = (normed_two * final_gain + final_shift).astype(BF)

    def give(a):
        a = a.reshape(per, n_t, frames // n_t, width)
        a = lax.all_to_all(a, "tensor", 1, 0, tiled=False)
        return a.transpose(2, 0, 1, 3).reshape(frames // n_t, item_count, width)

    layer_output = give(layer_output)

    grad_final_gain = jnp.sum(upstream * normed_two, axis=0)
    grad_final_shift = jnp.sum(upstream, axis=0)
    grad_two = norm_back(upstream * final_gain, normed_two, scale_two)
    grad_down_bias = jnp.sum(grad_two, axis=0)
    g2 = grad_two.astype(BF)
    gwd = mm_rows(active, g2)
    grad_pre = mm_cols(g2, wd) * gelu_slope(pre_up)
    grad_up_bias = jnp.sum(grad_pre, axis=0)
    gp = grad_pre.astype(BF)
    gwu = mm_rows(mid_low, gp)
    grad_mid = mm_cols(gp, wu) + grad_two
    grad_attn_gain = jnp.sum(grad_mid * normed_one, axis=0)
    grad_attn_shift = jnp.sum(grad_mid, axis=0)
    grad_one = norm_back(grad_mid * attn_gain, normed_one, scale_one)
    grad_output_bias = jnp.sum(grad_one, axis=0)
    g1 = grad_one.astype(BF)
    gwo = mm_rows(context, g1)

    def spread_rows(a, live, full):
        parts, at = [], 0
        for n in live:
            parts.append(jnp.pad(a[at : at + n], ((0, full - n), (0, 0))))
            at += n
        return jnp.stack(parts)

    def spread_cols(a, live, full):
        parts, at = [], 0
        for n in live:
            parts.append(jnp.pad(a[:, at : at + n], ((0, 0), (0, full - n))))
            at += n
        return jnp.stack(parts)

    def reduce(a):
        a = lax.psum_scatter(a.astype(BF), "dp", scatter_dimension=1, tiled=True)
        a = lax.psum_scatter(a, "tensor", scatter_dimension=0, tiled=True)[0]
        return lax.all_gather(a, "dp", axis=0, tiled=True).astype(F32)

    hl = [n * HEAD for n in head_live]
    ff_grads = reduce(
        jnp.concatenate([spread_rows(gwd, unit_live, units), spread_cols(gwu, unit_live, units)], axis=2)
    )
    grad_down_weight, grad_up_weight = ff_grads[:, :width], ff_grads[:, width:]
    grad_output_weight = reduce(spread_rows(gwo, hl, hs))

    gc = split(mm_cols(g1, wo).astype(BF))
    scores = jnp.einsum("infe,inge->infg", q, k, preferred_element_type=F32) * 0.125
    prob = jnp.exp(scores - log_total)
    gprob = jnp.einsum("infe,inge->infg", gc, v, preferred_element_type=F32)
    row_dot = jnp.sum(gprob * prob, axis=-1, keepdims=True)
    gs = (prob * (gprob - row_dot)).astype(BF)
    gq = join((jnp.einsum("infg,inge->infe", gs, k, preferred_element_type=F32) * 0.125).astype(BF))
    gk = join((jnp.einsum("infg,infe->inge", gs, q, preferred_element_type=F32) * 0.125).astype(BF))
    gv = join(jnp.einsum("infg,infe->inge", prob.astype(BF), gc, preferred_element_type=F32).astype(BF))
    grad_query_bias = jnp.sum(gq.astype(F32), axis=0)
    grad_value_bias = jnp.sum(gv.astype(F32), axis=0)
    qkv_grads = reduce(
        jnp.concatenate(
            [spread_cols(mm_rows(x, g), hl, hs) for g in (gq, gk, gv)], axis=2
        )
    )
    grad_query_weight = qkv_grads[:, :hs]
    grad_key_weight = qkv_grads[:, hs : 2 * hs]
    grad_value_weight = qkv_grads[:, 2 * hs :]
    grad_in = mm_cols(gq, wq) + mm_cols(gk, wk) + mm_cols(gv, wv) + grad_one
    grad_mask_vector = jnp.sum(jnp.where(covered[:, None], grad_in, 0.0), axis=0)
    input_grad = give((0.1 * jnp.where(covered[:, None], 0.0, grad_in)).astype(BF))

    def spread_vec(a, live, full):
        parts, at = [], 0
        for n in live:
            parts.append(jnp.pad(a[at : at + n], (0, full - n)))
            at += n
        return jnp.concatenate(parts)

    small = [grad_mask_vector, grad_output_bias, grad_attn_gain, grad_attn_shift, grad_down_bias,
             grad_final_gain, grad_final_shift]
    packed = jnp.concatenate(
        small + [spread_vec(grad_query_bias, hl, hs), spread_vec(grad_value_bias, hl, hs),
                 spread_vec(grad_up_bias, unit_live, units)])
    packed = lax.psum(packed, ("dp", "tensor"))
    at = 0
    outs = []
    for a in small:
        outs.append(packed[at : at + width])
        at += width

    def own(n):
        nonlocal at
        got = lax.dynamic_slice_in_dim(packed[at : at + n * n_t], rank * n, n, 0)
        at += n * n_t
        return got

    grad_query_bias = own(hs)
    grad_value_bias = own(hs)
    grad_up_bias = own(units)
    (grad_mask_vector, grad_output_bias, grad_attn_gain, grad_attn_shift, grad_down_bias,
     grad_final_gain, grad_final_shift) = outs
    return (layer_output, input_grad, grad_mask_vector, grad_query_weight, grad_query_bias,
            grad_key_weight, grad_value_weight, grad_value_bias, grad_output_weight,
            grad_output_bias, grad_attn_gain, grad_attn_shift, grad_up_weight, grad_up_bias,
            grad_down_weight, grad_down_bias, grad_final_gain, grad_final_shift)


def solution(mesh):
    return jax.shard_map(
        body,
        mesh=mesh,
        in_specs=(P(None, "dp", None), P("dp", None), P(), P(None, "tensor"), P("tensor"),
                  P(None, "tensor"), P(None, "tensor"), P("tensor"), P("tensor", None), P(), P(),
                  P(), P(None, "tensor"), P("tensor"), P("tensor", None), P(), P(), P(),
                  P("tensor", "dp", None)),
        out_specs=(P("tensor", "dp", None), P("tensor", "dp", None), P(), P(None, "tensor"),
                   P("tensor"), P(None, "tensor"), P(None, "tensor"), P("tensor"),
                   P("tensor", None), P(), P(), P(), P(None, "tensor"), P("tensor"),
                   P("tensor", None), P(), P(), P()),
        check_vma=False,
    )
```

```python
import functools

import jax
import jax.numpy as jnp
from jax import lax
from jax.experimental import pallas as pl
from jax.experimental.pallas import tpu as pltpu
from jax.sharding import PartitionSpec as P

HEAD = 64
SPAN = 10
EPS = 1e-05
BF = jnp.bfloat16
F32 = jnp.float32
MESH = pl.DeviceIdType.MESH
GROUP = 8
BITS = 2


def normalize(values):
    center = values - jnp.mean(values, axis=-1, keepdims=True)
    scaled = lax.rsqrt(jnp.mean(center * center, axis=-1, keepdims=True) + EPS)
    return (center * scaled, scaled)


def norm_back(upstream, normed, scaled):
    row_mean = jnp.mean(upstream, axis=-1, keepdims=True)
    row_proj = jnp.mean(upstream * normed, axis=-1, keepdims=True)
    return scaled * (upstream - row_mean - normed * row_proj)


def mm(a, b):
    return jnp.dot(a, b, preferred_element_type=F32)


def mm_rows(a, b):
    return lax.dot_general(a, b, (((0,), (0,)), ((), ())), preferred_element_type=F32)


def mm_cols(a, b):
    return lax.dot_general(a, b, (((1,), (1,)), ((), ())), preferred_element_type=F32)


def gelu_slope(values):
    normal_cdf = 0.5 * (1.0 + jax.scipy.special.erf(values * 0.7071067811865476))
    normal_pdf = jnp.exp(-0.5 * values * values) * 0.3989422804014327
    return normal_cdf + values * normal_pdf


class Place:
    def __init__(self):
        self.rank = lax.axis_index("tensor")
        self.dp = lax.axis_index("dp")
        self.core = self.dp % 2
        self.mate = self.dp + 1 - 2 * self.core
        self.partner = []
        piece = self.core * (GROUP // 2)
        for k in range(BITS):
            one, two = 2 << k, 2 << (BITS - 1 - k)
            bit = (1 - self.core) * ((self.dp // one) % 2) + self.core * ((self.dp // two) % 2)
            step = one + self.core * (two - one)
            self.partner.append(self.dp + step * (1 - 2 * bit))
            piece = piece + bit * (1 << k)
        self.piece = piece

    def enter(self, n_dp):
        barrier = pltpu.get_barrier_semaphore()
        count = 0
        n_t = lax.axis_size("tensor")
        for k in range(1, n_t):
            pl.semaphore_signal(
                barrier, inc=1, device_id=(self.dp, (self.rank + k) % n_t), device_id_type=MESH
            )
            count += 1
        for other in [self.mate] + self.partner + self.outer(n_dp):
            pl.semaphore_signal(
                barrier, inc=1, device_id=(other, self.rank), device_id_type=MESH
            )
            count += 1
        pl.semaphore_wait(barrier, count)

    def outer(self, n_dp):
        others, step = [], GROUP
        while step < n_dp:
            bit = (self.dp // step) % 2
            others.append(self.dp + step * (1 - 2 * bit))
            step *= 2
        return others


def rows_at(ref, start, size, col0=None, cols=None):
    start = pl.multiple_of(start, 8)
    if col0 is None:
        return ref.at[pl.ds(start, size)]
    return ref.at[pl.ds(start, size), pl.ds(col0, cols)]


class Gather:
    def __init__(self, place, n_t, regions, send, recv):
        self.place, self.n_t, self.regions = place, n_t, regions
        self.send, self.recv = send, recv

    def own_copies(self, sems):
        p = self.place
        out = []
        for i, (rank, _, src, dst, row0, rows, col0, cols) in enumerate(self.regions):
            out.append((rank, pltpu.make_async_copy(
                src(0, rows), rows_at(dst, row0, rows, col0, cols), sems.at[i])))
        return out

    def own_start(self, sems, chunks):
        for (rank, c), reg in zip(self.own_copies(sems), self.regions):
            if reg[1] in chunks:
                pl.when(self.place.rank == rank)(c.start)

    def own_wait(self, sems, chunks):
        for (rank, c), reg in zip(self.own_copies(sems), self.regions):
            if reg[1] in chunks:
                pl.when(self.place.rank == rank)(c.wait)

    def z_copy(self, i, k):
        rank, _, src, dst, row0, rows, col0, cols = self.regions[i]
        p = self.place
        size = rows // GROUP
        return pltpu.make_async_remote_copy(
            src_ref=src(p.piece * size, size),
            dst_ref=rows_at(dst, row0 + p.piece * size, size, col0, cols),
            send_sem=self.send.at[i, k - 1],
            recv_sem=self.recv.at[i, 0],
            device_id=(p.dp, (rank + k) % self.n_t),
            device_id_type=MESH,
        )

    def z_start(self, chunks):
        for i, reg in enumerate(self.regions):
            if reg[1] in chunks:
                @pl.when(self.place.rank == reg[0])
                def _(i=i):
                    for k in range(1, self.n_t):
                        self.z_copy(i, k).start()

    def z_wait(self, chunks):
        for i, reg in enumerate(self.regions):
            if reg[1] in chunks:
                @pl.when(self.place.rank != reg[0])
                def _(i=i):
                    self.z_copy(i, 1).wait_recv()

    def copy(self, i, k):
        rank, _, _, dst, row0, rows, col0, cols = self.regions[i]
        p = self.place
        size = rows // GROUP * (1 << k)
        block = p.piece // (1 << k)
        view = rows_at(dst, row0 + block * size, size, col0, cols)
        return pltpu.make_async_remote_copy(
            src_ref=view, dst_ref=view,
            send_sem=self.send.at[i, self.n_t - 1 + k],
            recv_sem=self.recv.at[i, 1 + k],
            device_id=((p.partner + [p.mate])[k], p.rank),
            device_id_type=MESH,
        )

    def start(self, k, chunks):
        for i, reg in enumerate(self.regions):
            if reg[1] in chunks:
                @pl.when(self.place.rank != reg[0])
                def _(i=i):
                    self.copy(i, k).start()

    def wait(self, k, chunks):
        for i, reg in enumerate(self.regions):
            if reg[1] in chunks:
                @pl.when(self.place.rank != reg[0])
                def _(i=i):
                    self.copy(i, k).wait_recv()

    def drain(self):
        for i, reg in enumerate(self.regions):
            @pl.when(self.place.rank == reg[0])
            def _(i=i):
                for k in range(1, self.n_t):
                    self.z_copy(i, k).wait_send()

            @pl.when(self.place.rank != reg[0])
            def _(i=i):
                for k in range(BITS + 1):
                    self.copy(i, k).wait_send()


def weight_regions(n_t, width, unit_live, pair, spare, wo, wu, wd, gq, gs, go, gu, gd):
    def rows_of(ref, base, col0, cols):
        return lambda start, size: rows_at(ref, base + start, size, col0, cols)

    out = []
    at = 0
    for r in range(n_t):
        full = 2 * r < n_t
        out.append((r, 0, rows_of(pair, 0, 0, 384), gq, 0, width, 384 * r, 384))
        if full:
            dst, col0 = (gq, 384 * n_t) if r == 0 else (gs, 0)
            out.append((r, 0, rows_of(spare, 0, 0, 384), dst, 0, width, col0, 384))
        out.append((r, 1, rows_of(wo, 0, 0, width), go, 128 * r, 128, 0, width))
        if full:
            out.append((r, 1, rows_of(wo, 128, 0, width), go, 128 * n_t + HEAD * r, HEAD, 0, width))
        out.append((r, 2, rows_of(wu, 0, 0, unit_live[r]), gu, 0, width, at, unit_live[r]))
        out.append((r, 3, rows_of(wd, 0, 0, width), gd, at, unit_live[r], 0, width))
        at += unit_live[r]
    return out


def gather_kernel(n_t, n_dp, unit_live, pair, spare, wo, wu, wd, bias,
                  gq, go, gu, gd, gb, gs, send, recv, local, bsend, brecv):
    place = Place()
    width = pair.shape[0]
    place.enter(n_dp)
    regions = weight_regions(n_t, width, unit_live, pair, spare, wo, wu, wd, gq, gs, go, gu, gd)
    g = Gather(place, n_t, regions, send, recv)

    def bias_copy(k):
        return pltpu.make_async_remote_copy(
            src_ref=bias, dst_ref=gb.at[place.rank], send_sem=bsend.at[k - 1],
            recv_sem=brecv.at[k - 1], device_id=(place.dp, (place.rank + k) % n_t),
            device_id_type=MESH)

    def bias_in(k):
        return pltpu.make_async_remote_copy(
            src_ref=bias, dst_ref=gb.at[(place.rank + n_t - k) % n_t], send_sem=bsend.at[k - 1],
            recv_sem=brecv.at[k - 1], device_id=(place.dp, (place.rank + k) % n_t),
            device_id_type=MESH)

    chunks = [(0,), (1,), (2,), (3,)]
    for k in range(1, n_t):
        bias_copy(k).start()
    g.z_start((0,))
    g.z_start((1,))
    g.z_start((2,))
    g.z_start((3,))
    g.own_start(local, (0, 1, 2, 3))
    own_bias = pltpu.make_async_copy(bias, gb.at[place.rank], local.at[len(regions)])
    own_bias.start()
    groups = [(0, 1), (2,), (3,)]
    stages = BITS + 2
    for step in range(stages + len(groups)):
        for c, group in enumerate(groups):
            s = step - c
            if s == 0:
                g.z_wait(group)
                g.start(0, group)
            elif 0 < s <= BITS:
                g.wait(s - 1, group)
                g.start(s, group)
            elif s == BITS + 1:
                g.wait(BITS, group)
    g.own_wait(local, (0, 1, 2, 3))
    own_bias.wait()
    for k in range(1, n_t):
        bias_in(k).wait_recv()
        bias_copy(k).wait_send()
    g.drain()

    @pl.loop(0, width // 96)
    def _(i):
        at = pl.ds(pl.multiple_of(i * 96, 96), 96)
        gq[at, pl.ds(384 * n_t, 384)] = gq[at, pl.ds(384 * n_t, 384)] + gs[at, :]


def gather_weights(n_t, n_dp, unit_live, pair, spare, wo, wu, wd, bias):
    width = pair.shape[0]
    units = sum(unit_live)
    n_reg = 4 * n_t + 2 * sum(2 * r < n_t for r in range(n_t))
    heads = 10 * HEAD
    vm = pl.BlockSpec(memory_space=pltpu.VMEM)
    hb = pl.BlockSpec(memory_space=pl.ANY)
    return pl.pallas_call(
        functools.partial(gather_kernel, n_t, n_dp, unit_live),
        out_shape=(
            jax.ShapeDtypeStruct((width, 384 * (n_t + 1)), BF),
            jax.ShapeDtypeStruct((heads, width), BF),
            jax.ShapeDtypeStruct((width, units), BF),
            jax.ShapeDtypeStruct((units, width), BF),
            jax.ShapeDtypeStruct((n_t,) + bias.shape, F32),
        ),
        in_specs=[hb] * 6,
        out_specs=[vm] * 5,
        scratch_shapes=[
            pltpu.VMEM((width, 384), BF),
            pltpu.SemaphoreType.DMA((n_reg, n_t - 1 + BITS + 1)),
            pltpu.SemaphoreType.DMA((n_reg, BITS + 2)),
            pltpu.SemaphoreType.DMA((n_reg + 1,)),
            pltpu.SemaphoreType.DMA((n_t - 1,)),
            pltpu.SemaphoreType.DMA((n_t - 1,)),
        ],
        compiler_params=pltpu.CompilerParams(
            collective_id=0, has_side_effects=True, vmem_limit_bytes=60 << 20
        ),
        name="gather_weights",
    )(pair, spare, wo, wu, wd, bias)


def add_into(dst, dst0, a, a0, b, b0, size, step=16):
    @pl.loop(0, size // step)
    def _(i):
        def at(base):
            return pl.ds(pl.multiple_of(base + i * step, 8), step)
        dst[at(dst0), :] = (a[at(a0), :].astype(F32) + b[at(b0), :].astype(F32)).astype(dst.dtype)


class Scatter:
    def __init__(self, place, n_t, n_dp, ranges, grad, acc, got_c, got_k, got_z, got_o, final,
                 send, recv):
        self.place, self.n_t, self.n_dp, self.ranges = place, n_t, n_dp, ranges
        self.grad, self.acc, self.got_c, self.got_k = grad, acc, got_c, got_k
        self.got_z, self.got_o, self.final = got_z, got_o, final
        self.send, self.recv = send, recv
        self.half = grad.shape[0] // 2
        self.size = grad.shape[0] // GROUP
        self.local = place.piece - place.core * (GROUP // 2)
        self.outer = place.outer(n_dp)

    def remote(self, src, dst, n, device):
        return pltpu.make_async_remote_copy(
            src_ref=src, dst_ref=dst, send_sem=self.send.at[n], recv_sem=self.recv.at[n],
            device_id=device, device_id_type=MESH)

    def core_copy(self):
        p = self.place
        return self.remote(rows_at(self.grad, (1 - p.core) * self.half, self.half), self.got_c, 0,
                           (p.mate, p.rank))

    def core_add(self):
        p = self.place
        add_into(self.acc, 0, self.grad, p.core * self.half, self.got_c, 0, self.half)

    def block(self, k):
        n = 1 << k
        keep = (self.local // n) * n
        bit = (self.local // n) % 2
        return keep * self.size, (keep + n - 2 * n * bit) * self.size, n * self.size

    def bit_copy(self, k):
        _, give, size = self.block(k)
        return self.remote(rows_at(self.acc, give, size), self.got_k[k], 1 + k,
                           (self.place.partner[k], self.place.rank))

    def bit_add(self, k):
        keep, _, size = self.block(k)
        add_into(self.acc, keep, self.acc, keep, self.got_k[k], 0, size)

    def outer_copy(self, j):
        return self.remote(rows_at(self.acc, self.local * self.size, self.size), self.got_o.at[j],
                           1 + BITS + j, (self.outer[j], self.place.rank))

    def outer_rounds(self):
        for j in range(len(self.outer)):
            c = self.outer_copy(j)
            c.start()
            c.wait()
            keep = self.local * self.size
            add_into(self.acc, keep, self.acc, keep, self.got_o.at[j], 0, self.size)

    def z_base(self):
        return 1 + BITS + len(self.outer)

    def z_copies(self, to, k):
        p = self.place
        out = []
        for i, (col0, cols, _, zi) in enumerate(self.ranges[to]):
            out.append(self.remote(
                rows_at(self.acc, self.local * self.size, self.size, col0, cols),
                self.got_z[zi].at[k - 1, :, pl.ds(0, cols)],
                self.z_base() + i * (self.n_t - 1) + k - 1, (p.dp, to)))
        return out

    def z_start(self):
        for to in range(self.n_t):
            for k in range(1, self.n_t):
                @pl.when(self.place.rank == (to - k) % self.n_t)
                def _(to=to, k=k):
                    for c in self.z_copies(to, k):
                        c.start()

    def z_finish(self):
        p = self.place
        for me in range(self.n_t):
            @pl.when(p.rank == me)
            def _(me=me):
                for k in range(1, self.n_t):
                    for c in self.z_copies(me, k):
                        c.wait_recv()
                for col0, cols, fi, zi in self.ranges[me]:
                    step = 16
                    @pl.loop(0, self.size // step)
                    def _(i):
                        a = pl.ds(pl.multiple_of(self.local * self.size + i * step, 8), step)
                        z = pl.ds(pl.multiple_of(i * step, 8), step)
                        f = pl.ds(pl.multiple_of(p.piece * self.size + i * step, 8), step)
                        total = self.acc[a, pl.ds(col0, cols)].astype(F32)
                        for k in range(self.n_t - 1):
                            total = total + self.got_z[zi][k, z, pl.ds(0, cols)].astype(F32)
                        self.final[fi][f, pl.ds(0, cols)] = total.astype(BF)

    def f_base(self):
        return self.z_base() + 2 * (self.n_t - 1)

    def f_copies(self, me, k):
        p = self.place
        out = []
        for i, (_, cols, fi, _) in enumerate(self.ranges[me]):
            size = self.size * (1 << k)
            view = rows_at(self.final[fi], (p.piece // (1 << k)) * size, size, 0, cols)
            out.append(self.remote(view, view, self.f_base() + i * (BITS + 1) + k,
                                   ((p.partner + [p.mate])[k], p.rank)))
        return out

    def f_start(self, k):
        for me in range(self.n_t):
            @pl.when(self.place.rank == me)
            def _(me=me):
                for c in self.f_copies(me, k):
                    c.start()

    def f_wait(self, k):
        for me in range(self.n_t):
            @pl.when(self.place.rank == me)
            def _(me=me):
                for c in self.f_copies(me, k):
                    c.wait_recv()

    def n_sems(self):
        return self.f_base() + 2 * (BITS + 1)

    def drain(self):
        self.core_copy().wait_send()
        for k in range(BITS):
            self.bit_copy(k).wait_send()
        for to in range(self.n_t):
            for k in range(1, self.n_t):
                @pl.when(self.place.rank == (to - k) % self.n_t)
                def _(to=to, k=k):
                    for c in self.z_copies(to, k):
                        c.wait_send()
        for me in range(self.n_t):
            @pl.when(self.place.rank == me)
            def _(me=me):
                for k in range(BITS + 1):
                    for c in self.f_copies(me, k):
                        c.wait_send()

    def advance(self, stage):
        if stage == 0:
            self.core_copy().start()
        elif stage == 1:
            self.core_copy().wait_recv()
            self.core_add()
            self.bit_copy(BITS - 1).start()
        elif stage <= BITS:
            k = BITS + 1 - stage
            self.bit_copy(k).wait_recv()
            self.bit_add(k)
            self.bit_copy(k - 1).start()
        elif stage == BITS + 1:
            self.bit_copy(0).wait_recv()
            self.bit_add(0)
            self.outer_rounds()
            self.z_start()
        elif stage == BITS + 2:
            self.z_finish()
            self.f_start(0)
        elif stage <= 2 * BITS + 2:
            k = stage - BITS - 3
            self.f_wait(k)
            self.f_start(k + 1)
        elif stage == 2 * BITS + 3:
            self.f_wait(BITS)


STAGES = 2 * BITS + 4


def n_outer(n_dp):
    n, step = 0, GROUP
    while step < n_dp:
        n, step = n + 1, step * 2
    return n


def grad_ranges(n_t, unit_live):
    ff, at = [], 0
    for r in range(n_t):
        ff.append([(at, unit_live[r], 0, 0)])
        at += unit_live[r]
    qo = []
    for r in range(n_t):
        here = [(512 * r, 512, 0, 0)]
        if 2 * r < n_t:
            here.append((512 * n_t, 512, 1, 1))
        qo.append(here)
    return ff, qo


def scatter_kernel(n_t, n_dp, unit_live, gd, gu, gq, small, fd, fu, fq, fs, fsmall,
                   *scratch):
    place = Place()
    place.enter(n_dp)
    ff, qo = grad_ranges(n_t, unit_live)
    chunks = []
    it = iter(scratch)
    for grad, ranges, final, nz in ((gd, ff, [fd], 1), (gu, ff, [fu], 1), (gq, qo, [fq, fs], 2)):
        acc, got_c = next(it), next(it)
        got_k = [next(it) for _ in range(BITS)]
        got_z = [next(it) for _ in range(nz)]
        got_o = next(it)
        send, recv = next(it), next(it)
        chunks.append(Scatter(place, n_t, n_dp, ranges, grad, acc, got_c, got_k, got_z, got_o,
                              final, send, recv))
    sgot, ssend, srecv = next(it), next(it), next(it)

    fsmall[...] = small[...]
    hops = [place.mate] + place.partner + place.outer(n_dp)

    def hop(j):
        return pltpu.make_async_remote_copy(
            src_ref=fsmall, dst_ref=sgot.at[j], send_sem=ssend.at[j], recv_sem=srecv.at[j],
            device_id=(hops[j], place.rank), device_id_type=MESH)

    def zhop(k):
        j = len(hops) + k - 1
        return pltpu.make_async_remote_copy(
            src_ref=fsmall, dst_ref=sgot.at[j], send_sem=ssend.at[j], recv_sem=srecv.at[j],
            device_id=(place.dp, (place.rank + k) % n_t), device_id_type=MESH)

    for step in range(STAGES + len(chunks) - 1):
        for c, chunk in enumerate(chunks):
            if 0 <= step - c < STAGES:
                chunk.advance(step - c)
        if step == 0:
            hop(0).start()
        elif step < len(hops):
            hop(step - 1).wait()
            fsmall[...] = fsmall[...] + sgot[step - 1]
            hop(step).start()
        elif step == len(hops):
            hop(step - 1).wait()
            fsmall[...] = fsmall[...] + sgot[step - 1]
            for k in range(1, n_t):
                zhop(k).start()
        elif step == len(hops) + 1:
            for k in range(1, n_t):
                zhop(k).wait()
            total = fsmall[...]
            for k in range(1, n_t):
                total = total + sgot[len(hops) + k - 1]
            fsmall[...] = total
    for chunk in chunks:
        chunk.drain()


def scatter_grads(n_t, n_dp, unit_live, gd, gu, gq, small):
    width = gd.shape[0]
    outer = n_outer(n_dp)
    vm = pl.BlockSpec(memory_space=pltpu.VMEM)
    scratch = []
    wide = max(unit_live)
    n_sem = 1 + BITS + outer + 2 * (n_t - 1) + 2 * (BITS + 1)
    for cols, zs in ((gd.shape[1], [wide]), (gu.shape[1], [wide]), (gq.shape[1], [512, 512])):
        scratch += [pltpu.VMEM((width // 2, cols), BF), pltpu.VMEM((width // 2, cols), BF)]
        scratch += [pltpu.VMEM((width // GROUP * (1 << k), cols), BF) for k in range(BITS)]
        scratch += [pltpu.VMEM((n_t - 1, width // GROUP, z), BF) for z in zs]
        scratch += [pltpu.VMEM((max(outer, 1), width // GROUP, cols) if outer else (1, 8, 128), BF)]
        scratch += [pltpu.SemaphoreType.DMA((n_sem,)), pltpu.SemaphoreType.DMA((n_sem,))]
    hops = 1 + BITS + outer + n_t - 1
    scratch += [pltpu.VMEM((hops,) + small.shape, F32), pltpu.SemaphoreType.DMA((hops,)),
                pltpu.SemaphoreType.DMA((hops,))]
    return pl.pallas_call(
        functools.partial(scatter_kernel, n_t, n_dp, unit_live),
        out_shape=(
            jax.ShapeDtypeStruct((width, wide), BF),
            jax.ShapeDtypeStruct((width, wide), BF),
            jax.ShapeDtypeStruct((width, 512), BF),
            jax.ShapeDtypeStruct((width, 512), BF),
            jax.ShapeDtypeStruct(small.shape, F32),
        ),
        in_specs=[vm] * 4,
        out_specs=[vm] * 5,
        scratch_shapes=scratch,
        compiler_params=pltpu.CompilerParams(
            collective_id=1, has_side_effects=True, vmem_limit_bytes=62 << 20
        ),
        name="scatter_grads",
    )(gd, gu, gq, small)


def body(features, mask_starts, mask_vector, query_weight, query_bias, key_weight, value_weight,
         value_bias, output_weight, output_bias, attn_gain, attn_shift, up_weight, up_bias,
         down_weight, down_bias, final_gain, final_shift, grad_output):
    frames, item_count, width = features.shape
    n_t = lax.axis_size("tensor")
    n_d = lax.axis_size("dp")
    rank = lax.axis_index("tensor")
    slots = query_weight.shape[1] // HEAD
    units = up_weight.shape[1]
    unit_live = [units if r == 0 else units * 5 // 6 for r in range(n_t)]
    if n_t != 4 or slots != 3 or item_count != n_t or n_d % GROUP:
        raise ValueError("unsupported sizes")
    two = 2 * HEAD
    pair = jnp.concatenate([w[:, :two] for w in (query_weight, key_weight, value_weight)], axis=1)

    def halves(a):
        blank = jnp.zeros_like(a)
        return jnp.where(rank == 0, jnp.concatenate([a, blank], axis=-1),
                         jnp.concatenate([blank, a], axis=-1))

    spare = jnp.concatenate(
        [halves(w[:, two:]) for w in (query_weight, key_weight, value_weight)], axis=1)
    blank = jnp.zeros((two,), F32)
    row = jnp.concatenate([query_bias[:two], blank, value_bias[:two],
                           halves(query_bias[two:]), blank, halves(value_bias[two:])])
    bias = jnp.zeros((8, width), F32).at[0].set(row).at[1].set(up_bias)
    wq, wo, wu, wd, gb = gather_weights(
        n_t, n_d, unit_live, pair, spare, output_weight, up_weight, down_weight, bias)
    by = jnp.concatenate([gb[r, 0, :384] for r in range(n_t)] + [gb[0, 0, 384:] + gb[1, 0, 384:]])
    bu = jnp.concatenate([gb[r, 1, : unit_live[r]] for r in range(n_t)])
    heads = 2 * (n_t + 1)

    feat = lax.dynamic_slice_in_dim(features, rank, 1, 1)[:, 0]
    starts = lax.dynamic_slice_in_dim(mask_starts, rank, 1, 0)
    upstream = lax.all_to_all(grad_output.reshape(frames // n_t, n_t, 1, width), "tensor", 1, 0,
                              tiled=False)
    upstream = upstream.reshape(frames, width).astype(F32)
    position = jnp.arange(frames, dtype=jnp.int32)[:, None]
    covered = jnp.any((starts <= position) & (position < starts + SPAN), axis=1)
    hidden_in = jnp.where(covered[:, None], mask_vector[None, :], feat.astype(F32))
    x = hidden_in.astype(BF)

    y = (mm(x, wq) + by).astype(BF)

    def pick(which):
        cols = jnp.concatenate(
            [y[:, 384 * r + two * which : 384 * r + two * which + two] for r in range(n_t + 1)], axis=1)
        return cols.reshape(frames, heads, HEAD).transpose(1, 0, 2)

    def join(a):
        return a.transpose(1, 0, 2).reshape(frames, heads * HEAD)

    q, k, v = pick(0), pick(1), pick(2)
    scores = jnp.einsum("nfe,nge->nfg", q, k, preferred_element_type=F32) * 0.125
    top = jnp.max(scores, axis=-1, keepdims=True)
    shifted = jnp.exp(scores - top)
    total = jnp.sum(shifted, axis=-1, keepdims=True)
    prob_low = (shifted / total).astype(BF)
    log_total = top + jnp.log(total)
    context = join(jnp.einsum("nfg,nge->nfe", prob_low, v, preferred_element_type=F32).astype(BF))
    normed_one, scale_one = normalize(hidden_in + mm(context, wo) + output_bias)
    mid = normed_one * attn_gain + attn_shift
    mid_low = mid.astype(BF)
    pre_up = mm(mid_low, wu) + bu
    active = jax.nn.gelu(pre_up, approximate=False).astype(BF)
    normed_two, scale_two = normalize(mid + mm(active, wd) + down_bias)
    layer_output = (normed_two * final_gain + final_shift).astype(BF)

    def give(a):
        a = a.reshape(n_t, frames // n_t, width)
        a = lax.all_to_all(a, "tensor", 0, 0, tiled=False)
        return a.transpose(1, 0, 2)

    layer_output = give(layer_output)

    grad_final_gain = jnp.sum(upstream * normed_two, axis=0)
    grad_final_shift = jnp.sum(upstream, axis=0)
    grad_two = norm_back(upstream * final_gain, normed_two, scale_two)
    grad_down_bias = jnp.sum(grad_two, axis=0)
    g2 = grad_two.astype(BF)
    gwd = mm_rows(g2, active).astype(BF)
    grad_pre = mm_cols(g2, wd) * gelu_slope(pre_up)
    grad_up_bias = jnp.sum(grad_pre, axis=0)
    gp = grad_pre.astype(BF)
    gwu = mm_rows(mid_low, gp).astype(BF)
    grad_mid = mm_cols(gp, wu) + grad_two
    grad_attn_gain = jnp.sum(grad_mid * normed_one, axis=0)
    grad_attn_shift = jnp.sum(grad_mid, axis=0)
    grad_one = norm_back(grad_mid * attn_gain, normed_one, scale_one)
    grad_output_bias = jnp.sum(grad_one, axis=0)
    g1 = grad_one.astype(BF)
    gwo = mm_rows(g1, context).astype(BF)

    gc = mm_cols(g1, wo).astype(BF).reshape(frames, heads, HEAD).transpose(1, 0, 2)
    scores = jnp.einsum("nfe,nge->nfg", q, k, preferred_element_type=F32) * 0.125
    prob = jnp.exp(scores - log_total)
    gprob = jnp.einsum("nfe,nge->nfg", gc, v, preferred_element_type=F32)
    row_dot = jnp.sum(gprob * prob, axis=-1, keepdims=True)
    gs = (prob * (gprob - row_dot)).astype(BF)
    gq = join((jnp.einsum("nfg,nge->nfe", gs, k, preferred_element_type=F32) * 0.125).astype(BF))
    gk = join((jnp.einsum("nfg,nfe->nge", gs, q, preferred_element_type=F32) * 0.125).astype(BF))
    gv = join(jnp.einsum("nfg,nfe->nge", prob.astype(BF), gc, preferred_element_type=F32).astype(BF))
    grad_query_bias = jnp.sum(gq.astype(F32), axis=0)
    grad_value_bias = jnp.sum(gv.astype(F32), axis=0)
    gy = jnp.concatenate(
        [g[:, two * r : two * r + two] for r in range(n_t + 1) for g in (gq, gk, gv)], axis=1)
    gwq = mm_rows(x, gy).astype(BF)
    gqo = jnp.concatenate(
        [a for r in range(n_t + 1)
         for a in (gwq[:, 384 * r : 384 * r + 384], gwo[:, two * r : two * r + two])], axis=1)
    grad_in = mm_cols(gy, wq) + grad_one
    grad_mask_vector = jnp.sum(jnp.where(covered[:, None], grad_in, 0.0), axis=0)
    input_grad = give((0.1 * jnp.where(covered[:, None], 0.0, grad_in)).astype(BF))

    small = jnp.stack([grad_mask_vector, grad_output_bias, grad_attn_gain, grad_attn_shift,
                       grad_down_bias, grad_final_gain, grad_final_shift,
                       jnp.pad(grad_query_bias, (0, width - heads * HEAD)),
                       jnp.pad(grad_value_bias, (0, width - heads * HEAD))])
    ub_rows = -(-sum(unit_live) // width)
    ub = jnp.pad(grad_up_bias, (0, ub_rows * width - sum(unit_live))).reshape(ub_rows, width)
    small = jnp.concatenate([small, ub])
    small = jnp.pad(small, ((0, 16 - small.shape[0]), (0, 0)))
    fd, fu, fq, fs, small = scatter_grads(n_t, n_d, unit_live, gwd, gwu, gqo, small)

    col = jnp.arange(units)
    alive = (rank == 0) | (col < units * 5 // 6)
    grad_down_weight = jnp.where(alive[None, :], fd.astype(F32), 0.0).T
    grad_up_weight = jnp.where(alive[None, :], fu.astype(F32), 0.0)
    fs32 = jnp.where(2 * rank < n_t, fs.astype(F32), 0.0)
    fq32 = fq.astype(F32)

    def own(which):
        third = fs32[:, two * which : two * which + two]
        third = jnp.where(rank == 0, third[:, :HEAD], third[:, HEAD:])
        return jnp.concatenate([fq32[:, two * which : two * which + two], third], axis=1)

    def own_vec(a):
        third = jnp.where(rank == 0, a[two * n_t : two * n_t + HEAD], a[two * n_t + HEAD : two * n_t + two])
        third = jnp.where(2 * rank < n_t, third, 0.0)
        return jnp.concatenate([lax.dynamic_slice_in_dim(a, two * rank, two), third])

    ub = small[9 : 9 + ub_rows].reshape(-1)
    ub = jnp.pad(ub, (0, units))
    at = jnp.where(rank == 0, 0, units + (rank - 1) * (units * 5 // 6))
    grad_up_bias = jnp.where(alive, lax.dynamic_slice_in_dim(ub, at, units), 0.0)
    return (layer_output, input_grad, small[0], own(0), own_vec(small[7]), own(1), own(2),
            own_vec(small[8]), own(3).T, small[1], small[2], small[3], grad_up_weight,
            grad_up_bias, grad_down_weight, small[4], small[5], small[6])


def solution(mesh):
    return jax.shard_map(
        body,
        mesh=mesh,
        in_specs=(P(None, "dp", None), P("dp", None), P(), P(None, "tensor"), P("tensor"),
                  P(None, "tensor"), P(None, "tensor"), P("tensor"), P("tensor", None), P(), P(),
                  P(), P(None, "tensor"), P("tensor"), P("tensor", None), P(), P(), P(),
                  P("tensor", "dp", None)),
        out_specs=(P("tensor", "dp", None), P("tensor", "dp", None), P(), P(None, "tensor"),
                   P("tensor"), P(None, "tensor"), P(None, "tensor"), P("tensor"),
                   P("tensor", None), P(), P(), P(), P(None, "tensor"), P("tensor"),
                   P("tensor", None), P(), P(), P()),
        check_vma=False,
    )
```

```python
import functools

import jax
import jax.numpy as jnp
from jax import lax
from jax.experimental import pallas as pl
from jax.experimental.pallas import tpu as pltpu
from jax.sharding import PartitionSpec as P

HEAD = 64
SPAN = 10
EPS = 1e-05
BF = jnp.bfloat16
F32 = jnp.float32
MESH = pl.DeviceIdType.MESH
GROUP = 8
BITS = 2


class Place:
    def __init__(self):
        self.rank = lax.axis_index("tensor")
        self.dp = lax.axis_index("dp")
        self.core = self.dp % 2
        self.mate = self.dp + 1 - 2 * self.core
        self.partner = []
        piece = self.core * (GROUP // 2)
        for k in range(BITS):
            one, two = 2 << k, 2 << (BITS - 1 - k)
            bit = (1 - self.core) * ((self.dp // one) % 2) + self.core * ((self.dp // two) % 2)
            step = one + self.core * (two - one)
            self.partner.append(self.dp + step * (1 - 2 * bit))
            piece = piece + bit * (1 << k)
        self.piece = piece

    def enter(self, n_dp):
        barrier = pltpu.get_barrier_semaphore()
        count = 0
        n_t = lax.axis_size("tensor")
        for k in range(1, n_t):
            pl.semaphore_signal(
                barrier, inc=1, device_id=(self.dp, (self.rank + k) % n_t), device_id_type=MESH
            )
            count += 1
        for other in [self.mate] + self.partner + self.outer(n_dp):
            pl.semaphore_signal(
                barrier, inc=1, device_id=(other, self.rank), device_id_type=MESH
            )
            count += 1
        pl.semaphore_wait(barrier, count)

    def outer(self, n_dp):
        others, step = [], GROUP
        while step < n_dp:
            bit = (self.dp // step) % 2
            others.append(self.dp + step * (1 - 2 * bit))
            step *= 2
        return others


def rows_at(ref, start, size, col0=None, cols=None):
    start = pl.multiple_of(start, 8)
    if col0 is None:
        return ref.at[pl.ds(start, size)]
    return ref.at[pl.ds(start, size), pl.ds(col0, cols)]


class Gather:
    def __init__(self, place, n_t, regions, send, recv):
        self.place, self.n_t, self.regions = place, n_t, regions
        self.send, self.recv = send, recv

    def own_copies(self, sems):
        p = self.place
        out = []
        for i, (rank, _, src, dst, row0, rows, col0, cols) in enumerate(self.regions):
            out.append((rank, pltpu.make_async_copy(
                src(0, rows), rows_at(dst, row0, rows, col0, cols), sems.at[i])))
        return out

    def own_start(self, sems, chunks):
        for (rank, c), reg in zip(self.own_copies(sems), self.regions):
            if reg[1] in chunks:
                pl.when(self.place.rank == rank)(c.start)

    def own_wait(self, sems, chunks):
        for (rank, c), reg in zip(self.own_copies(sems), self.regions):
            if reg[1] in chunks:
                pl.when(self.place.rank == rank)(c.wait)

    def z_copy(self, i, k):
        rank, _, src, dst, row0, rows, col0, cols = self.regions[i]
        p = self.place
        size = rows // GROUP
        return pltpu.make_async_remote_copy(
            src_ref=src(p.piece * size, size),
            dst_ref=rows_at(dst, row0 + p.piece * size, size, col0, cols),
            send_sem=self.send.at[i, k - 1],
            recv_sem=self.recv.at[i, 0],
            device_id=(p.dp, (rank + k) % self.n_t),
            device_id_type=MESH,
        )

    def z_start(self, chunks):
        for i, reg in enumerate(self.regions):
            if reg[1] in chunks:
                @pl.when(self.place.rank == reg[0])
                def _(i=i):
                    for k in range(1, self.n_t):
                        self.z_copy(i, k).start()

    def z_wait(self, chunks):
        for i, reg in enumerate(self.regions):
            if reg[1] in chunks:
                @pl.when(self.place.rank != reg[0])
                def _(i=i):
                    self.z_copy(i, 1).wait_recv()

    def copy(self, i, k):
        rank, _, _, dst, row0, rows, col0, cols = self.regions[i]
        p = self.place
        size = rows // GROUP * (1 << k)
        block = p.piece // (1 << k)
        view = rows_at(dst, row0 + block * size, size, col0, cols)
        return pltpu.make_async_remote_copy(
            src_ref=view, dst_ref=view,
            send_sem=self.send.at[i, self.n_t - 1 + k],
            recv_sem=self.recv.at[i, 1 + k],
            device_id=((p.partner + [p.mate])[k], p.rank),
            device_id_type=MESH,
        )

    def start(self, k, chunks):
        for i, reg in enumerate(self.regions):
            if reg[1] in chunks:
                @pl.when(self.place.rank != reg[0])
                def _(i=i):
                    self.copy(i, k).start()

    def wait(self, k, chunks):
        for i, reg in enumerate(self.regions):
            if reg[1] in chunks:
                @pl.when(self.place.rank != reg[0])
                def _(i=i):
                    self.copy(i, k).wait_recv()

    def drain(self, chunks):
        for i, reg in enumerate(self.regions):
            if reg[1] not in chunks:
                continue

            @pl.when(self.place.rank == reg[0])
            def _(i=i):
                for k in range(1, self.n_t):
                    self.z_copy(i, k).wait_send()

            @pl.when(self.place.rank != reg[0])
            def _(i=i):
                for k in range(BITS + 1):
                    self.copy(i, k).wait_send()


def weight_regions(n_t, width, unit_live, pair, spare, wo, wu, wd, gq, gs, go, gu, gd):
    def rows_of(ref, base, col0, cols):
        return lambda start, size: rows_at(ref, base + start, size, col0, cols)

    out = []
    at = 0
    for r in range(n_t):
        full = 2 * r < n_t
        out.append((r, 0, rows_of(pair, 0, 0, 384), gq, 0, width, 384 * r, 384))
        if full:
            dst, col0 = (gq, 384 * n_t) if r == 0 else (gs, 0)
            out.append((r, 0, rows_of(spare, 0, 0, 384), dst, 0, width, col0, 384))
        out.append((r, 1, rows_of(wo, 0, 0, width), go, 128 * r, 128, 0, width))
        if full:
            out.append((r, 1, rows_of(wo, 128, 0, width), go, 128 * n_t + HEAD * r, HEAD, 0, width))
        out.append((r, 2, rows_of(wu, 0, 0, unit_live[r]), gu, 0, width, at, unit_live[r]))
        out.append((r, 3, rows_of(wd, 0, 0, width), gd, at, unit_live[r], 0, width))
        at += unit_live[r]
    return out


def add_into(dst, dst0, a, a0, b, b0, size, step=16):
    @pl.loop(0, size // step)
    def _(i):
        def at(base):
            return pl.ds(pl.multiple_of(base + i * step, 8), step)
        dst[at(dst0), :] = (a[at(a0), :].astype(F32) + b[at(b0), :].astype(F32)).astype(dst.dtype)


class Scatter:
    def __init__(self, place, n_t, n_dp, ranges, grad, got_c, got_k, got_z, got_o, final, send,
                 recv):
        self.place, self.n_t, self.n_dp, self.ranges = place, n_t, n_dp, ranges
        self.grad, self.got_c, self.got_k = grad, got_c, got_k
        self.got_z, self.got_o, self.final = got_z, got_o, final
        self.send, self.recv = send, recv
        self.half = grad.shape[0] // 2
        self.acc = rows_at(grad, place.core * self.half, self.half)
        self.size = grad.shape[0] // GROUP
        self.local = place.piece - place.core * (GROUP // 2)
        self.outer = place.outer(n_dp)

    def remote(self, src, dst, n, device):
        return pltpu.make_async_remote_copy(
            src_ref=src, dst_ref=dst, send_sem=self.send.at[n], recv_sem=self.recv.at[n],
            device_id=device, device_id_type=MESH)

    def core_copy(self):
        p = self.place
        return self.remote(rows_at(self.grad, (1 - p.core) * self.half, self.half), self.got_c, 0,
                           (p.mate, p.rank))

    def core_add(self):
        add_into(self.acc, 0, self.acc, 0, self.got_c, 0, self.half)

    def block(self, k):
        n = 1 << k
        keep = (self.local // n) * n
        bit = (self.local // n) % 2
        return keep * self.size, (keep + n - 2 * n * bit) * self.size, n * self.size

    def bit_copy(self, k):
        _, give, size = self.block(k)
        return self.remote(rows_at(self.acc, give, size), self.got_k[k], 1 + k,
                           (self.place.partner[k], self.place.rank))

    def bit_add(self, k):
        keep, _, size = self.block(k)
        add_into(self.acc, keep, self.acc, keep, self.got_k[k], 0, size)

    def outer_rounds(self, me):
        p = self.place
        for i, (_, cols, fi, zi) in enumerate(self.ranges[me]):
            for j, other in enumerate(self.outer):
                view = rows_at(self.final[fi], p.piece * self.size, self.size, 0, cols)
                got = self.got_o[zi].at[j, :, pl.ds(0, cols)]
                c = self.remote(view, got, 1 + BITS + i * len(self.outer) + j, (other, p.rank))
                c.start()
                c.wait()
                add_into(view, 0, view, 0, got, 0, self.size)

    def z_base(self):
        return 1 + BITS + 2 * len(self.outer)

    def z_copies(self, to, k):
        p = self.place
        out = []
        for i, (col0, cols, _, zi) in enumerate(self.ranges[to]):
            out.append(self.remote(
                rows_at(self.acc, self.local * self.size, self.size, col0, cols),
                self.got_z[zi].at[k - 1, :, pl.ds(0, cols)],
                self.z_base() + i * (self.n_t - 1) + k - 1, (p.dp, to)))
        return out

    def z_start(self):
        for to in range(self.n_t):
            for k in range(1, self.n_t):
                @pl.when(self.place.rank == (to - k) % self.n_t)
                def _(to=to, k=k):
                    for c in self.z_copies(to, k):
                        c.start()

    def z_finish(self):
        p = self.place
        for me in range(self.n_t):
            @pl.when(p.rank == me)
            def _(me=me):
                for k in range(1, self.n_t):
                    for c in self.z_copies(me, k):
                        c.wait_recv()
                for col0, cols, fi, zi in self.ranges[me]:
                    step = 16
                    @pl.loop(0, self.size // step)
                    def _(i):
                        a = pl.ds(pl.multiple_of(self.local * self.size + i * step, 8), step)
                        z = pl.ds(pl.multiple_of(i * step, 8), step)
                        f = pl.ds(pl.multiple_of(p.piece * self.size + i * step, 8), step)
                        total = self.acc[a, pl.ds(col0, cols)].astype(F32)
                        for k in range(self.n_t - 1):
                            total = total + self.got_z[zi][k, z, pl.ds(0, cols)].astype(F32)
                        self.final[fi][f, pl.ds(0, cols)] = total.astype(BF)
                if self.outer:
                    self.outer_rounds(me)

    def f_base(self):
        return self.z_base() + 2 * (self.n_t - 1)

    def f_copies(self, me, k):
        p = self.place
        out = []
        for i, (_, cols, fi, _) in enumerate(self.ranges[me]):
            size = self.size * (1 << k)
            view = rows_at(self.final[fi], (p.piece // (1 << k)) * size, size, 0, cols)
            out.append(self.remote(view, view, self.f_base() + i * (BITS + 1) + k,
                                   ((p.partner + [p.mate])[k], p.rank)))
        return out

    def f_start(self, k):
        for me in range(self.n_t):
            @pl.when(self.place.rank == me)
            def _(me=me):
                for c in self.f_copies(me, k):
                    c.start()

    def f_wait(self, k):
        for me in range(self.n_t):
            @pl.when(self.place.rank == me)
            def _(me=me):
                for c in self.f_copies(me, k):
                    c.wait_recv()

    def n_sems(self):
        return self.f_base() + 2 * (BITS + 1)

    def drain(self):
        self.core_copy().wait_send()
        for k in range(BITS):
            self.bit_copy(k).wait_send()
        for to in range(self.n_t):
            for k in range(1, self.n_t):
                @pl.when(self.place.rank == (to - k) % self.n_t)
                def _(to=to, k=k):
                    for c in self.z_copies(to, k):
                        c.wait_send()
        for me in range(self.n_t):
            @pl.when(self.place.rank == me)
            def _(me=me):
                for k in range(BITS + 1):
                    for c in self.f_copies(me, k):
                        c.wait_send()

    def advance(self, stage):
        if stage == 0:
            self.core_copy().start()
        elif stage == 1:
            self.core_copy().wait_recv()
            self.core_add()
            self.bit_copy(BITS - 1).start()
        elif stage <= BITS:
            k = BITS + 1 - stage
            self.bit_copy(k).wait_recv()
            self.bit_add(k)
            self.bit_copy(k - 1).start()
        elif stage == BITS + 1:
            self.bit_copy(0).wait_recv()
            self.bit_add(0)
            self.z_start()
        elif stage == BITS + 2:
            self.z_finish()
            self.f_start(0)
        elif stage <= 2 * BITS + 2:
            k = stage - BITS - 3
            self.f_wait(k)
            self.f_start(k + 1)
        elif stage == 2 * BITS + 3:
            self.f_wait(BITS)


def n_outer(n_dp):
    n, step = 0, GROUP
    while step < n_dp:
        n, step = n + 1, step * 2
    return n


def grad_ranges(n_t, unit_live):
    ff, at = [], 0
    for r in range(n_t):
        ff.append([(at, unit_live[r], 0, 0)])
        at += unit_live[r]
    qo = []
    for r in range(n_t):
        here = [(512 * r, 512, 0, 0)]
        if 2 * r < n_t:
            here.append((512 * n_t, 512, 1, 1))
        qo.append(here)
    return ff, qo


def dots(a, b, ca, cb):
    return lax.dot_general(a, b, (((ca,), (cb,)), ((), ())), preferred_element_type=F32)


def layer_kernel(n_t, n_dp, unit_live,
                 feat, starts, vecs, bias, gup, pair, spare, wo_in, wu_in, wd_in,
                 out, gin_out, fd, fu, fq, fs, small,
                 wq, wo, wu, wd, spare_in, gb, by, bu, cr, x_s, y_s, p_s, ctx, n1, act,
                 slope, rowf, g2f, rowb, gc, s_ref, gs_ref, tr, slab, gin, grad_d, grad_u,
                 dc, d1, d0, dz, uc, u1, u0, uz, qz, sz, do, uo, qo_got, so_got, sgot,
                 wsend, wrecv, local, bsend, brecv, isend, irecv, osend, orecv, gsend, grecv,
                 dsend, drecv, usend, urecv, qsend, qrecv, ssend, srecv):
    place = Place()
    rank = place.rank
    frames, width = feat.shape
    part = frames // n_t
    pairs = n_t + 1
    two = 2 * HEAD
    tile = frames // 3
    units = wu.shape[1]
    wide = 256
    place.enter(n_dp)

    regions = weight_regions(n_t, width, unit_live, pair, spare, wo_in, wu_in, wd_in,
                             wq, spare_in, wo, wu, wd)
    g = Gather(place, n_t, regions, wsend, wrecv)
    n_reg = len(regions)

    def z_pass(src, dst, send, recv, k, incoming=False):
        to = (rank + k) % n_t
        at = (rank + n_t - k) % n_t if incoming else rank
        return pltpu.make_async_remote_copy(
            src_ref=src(to), dst_ref=dst.at[at], send_sem=send.at[k - 1], recv_sem=recv.at[k - 1],
            device_id=(place.dp, to), device_id_type=MESH)

    others = range(1, n_t)

    def bias_to(k, incoming=False):
        return z_pass(lambda to: bias, gb, bsend, brecv, k, incoming)

    def up_to(k, incoming=False):
        return z_pass(lambda to: gup.at[to], gin, isend, irecv, k, incoming)

    def out_to(k, incoming=False):
        return z_pass(lambda to: slab.at[to], out, osend, orecv, k, incoming)

    def gin_to(k, incoming=False):
        return z_pass(lambda to: slab.at[to], gin_out, gsend, grecv, k, incoming)

    for k in others:
        bias_to(k).start()
    g.z_start((0,))
    g.own_start(local, (0,))
    own_bias = pltpu.make_async_copy(bias, gb.at[rank], local.at[n_reg])
    own_up = pltpu.make_async_copy(gup.at[rank], gin.at[rank], local.at[n_reg + 1])
    own_bias.start()
    own_up.start()
    g.own_start(local, (1, 2, 3))

    position = lax.broadcasted_iota(jnp.int32, (frames, 128), 0)
    hit = jnp.zeros((frames, 128), F32)
    for m in range(starts.shape[1]):
        first = starts[rank, m]
        hit = jnp.where((position >= first) & (position < first + SPAN), 1.0, hit)
    cr[...] = hit

    def row(i):
        return vecs[i : i + 1, :]

    def rows(i):
        return pl.ds(pl.multiple_of(i * tile, 16), tile)

    def hidden(at):
        return jnp.where(cr[at, 0:1] > 0.5, row(0), feat[at, :].astype(F32))

    @pl.loop(0, 3)
    def _(i):
        x_s[rows(i), :] = hidden(rows(i)).astype(BF)

    small[...] = jnp.zeros_like(small)

    g.z_wait((0,))
    g.start(0, (0,))
    g.z_start((1, 2))
    g.wait(0, (0,))
    g.start(1, (0,))
    g.wait(1, (0,))
    g.start(2, (0,))
    for k in others:
        bias_to(k, True).wait_recv()
    own_bias.wait()
    g.own_wait(local, (0,))
    for r in range(n_t):
        by[r, 0:1, :] = gb[r, 0:1, 0:384]
    by[n_t, 0:1, :] = gb[0, 0:1, 384:768] + gb[1, 0:1, 384:768]
    at = 0
    for r in range(n_t):
        bu[0:1, at : at + unit_live[r]] = gb[r, 1:2, 0 : unit_live[r]]
        at += unit_live[r]
    g.wait(2, (0,))
    g.drain((0,))

    @pl.loop(0, width // 96)
    def _(i):
        at = pl.ds(pl.multiple_of(i * 96, 96), 96)
        wq[at, pl.ds(384 * n_t, 384)] = wq[at, pl.ds(384 * n_t, 384)] + spare_in[at, :]

    g.z_wait((1, 2))
    g.start(0, (1, 2))
    g.z_start((3,))

    lane3 = lax.broadcasted_iota(jnp.int32, (1, 384), 1)
    shrink = jnp.where(lane3 < two, 0.125, 1.0)

    @pl.loop(0, pairs)
    def _(p):
        at = pl.ds(pl.multiple_of(p * 384, 128), 384)
        val = dots(x_s[...], wq[:, at], 1, 0) + by[p, 0:1, :]
        y_s[:, at] = (val.astype(BF).astype(F32) * shrink).astype(BF)

    lane = lax.broadcasted_iota(jnp.int32, (1, two), 1)
    half = [jnp.where(lane < HEAD, 1.0, 0.0).astype(BF), jnp.where(lane < HEAD, 0.0, 1.0).astype(BF)]
    strips = [(128 * j, min(128, frames - 128 * j)) for j in range(-(-frames // 128))]

    def qkv_at(p):
        base = p * 384
        return [pl.ds(pl.multiple_of(base + two * j, 128), two) for j in range(3)]

    @pl.loop(0, pairs)
    def _(p):
        @pl.when(p == 0)
        def _():
            g.wait(0, (1, 2))
            g.start(1, (1, 2))

        @pl.when(p == 1)
        def _():
            g.z_wait((3,))
            for k in others:
                up_to(k).start()

        @pl.when(p == 2)
        def _():
            g.start(0, (3,))

        @pl.when(p == 3)
        def _():
            g.wait(1, (1, 2))
            g.start(2, (1, 2))
            g.wait(0, (3,))
            g.start(1, (3,))

        q_at, k_at, v_at = qkv_at(p)
        q, k, v = y_s[:, q_at], y_s[:, k_at], y_s[:, v_at]
        both = []
        for h in range(2):
            s_ref[...] = dots(k, q * half[h], 1, 1)
            for c0, cn in strips:
                s = s_ref[:, c0 : c0 + cn]
                e = jnp.exp(s - jnp.max(s, axis=0, keepdims=True))
                inv = 1.0 / jnp.sum(e, axis=0, keepdims=True)
                p_s[2 * p + h, :, c0 : c0 + cn] = (e * inv).astype(BF)
            both.append(dots(v, p_s[2 * p + h], 0, 0))
        turned = jnp.concatenate([both[0][:HEAD], both[1][HEAD:]], axis=0).T
        ctx[:, pl.ds(pl.multiple_of(p * two, 128), two)] = turned.astype(BF)

    g.wait(2, (1, 2))
    g.wait(1, (3,))
    g.start(2, (3,))
    g.own_wait(local, (1, 2))

    def norm(v):
        center = v - jnp.mean(v, axis=-1, keepdims=True)
        scaled = lax.rsqrt(jnp.mean(center * center, axis=-1, keepdims=True) + EPS)
        return center * scaled, scaled

    def back(e, normed, scaled):
        mean = jnp.mean(e, axis=-1, keepdims=True)
        proj = jnp.mean(e * normed, axis=-1, keepdims=True)
        return scaled * (e - mean - normed * proj)

    def total(v):
        return jnp.sum(v, axis=0, keepdims=True)

    @pl.loop(0, 3)
    def _(i):
        at = rows(i)
        res = hidden(at) + dots(ctx[at, :], wo[...], 1, 0) + row(1)
        normed, scaled = norm(res)
        n1[at, :] = normed
        cr[at, :] = jnp.where(lane < HEAD, cr[at, :], scaled)
        x_s[at, :] = (normed * row(2) + row(3)).astype(BF)

    def gelu_tile(at, cols):
        pre = dots(x_s[...], wu[:, at], 1, 0) + bu[0:1, at]
        cdf = 0.5 * (1.0 + lax.erf(pre * 0.7071067811865476))
        act[:, at] = (pre * cdf).astype(BF)
        pdf = jnp.exp(-0.5 * pre * pre) * 0.3989422804014327
        slope[:, at] = (cdf + pre * pdf).astype(BF)

    full = units // wide

    @pl.loop(0, full)
    def _(n):
        gelu_tile(pl.ds(pl.multiple_of(n * wide, 128), wide), wide)

    if units % wide:
        gelu_tile(pl.ds(full * wide, units % wide), units % wide)

    g.wait(2, (3,))
    g.own_wait(local, (3,))
    for k in others:
        up_to(k, True).wait_recv()
    own_up.wait()
    for j in range(n_t):
        rowf[pl.ds(part * j, part), :] = gin[j].astype(F32)

    @pl.loop(0, 3)
    def _(i):
        at = rows(i)
        mid = n1[at, :] * row(2) + row(3)
        res = mid + dots(act[at, :], wd[...], 1, 0) + row(4)
        normed, scaled = norm(res)
        up = rowf[at, :]
        small[2:3, 1536:2304] += total(up * normed)
        small[3:4, 0:768] += total(up)
        grad = back(up * row(5), normed, scaled)
        small[2:3, 768:1536] += total(grad)
        g2f[at, :] = grad
        rowb[at, :] = grad.astype(BF)
        rowf[at, :] = normed * row(5) + row(6)

    for j in range(n_t):
        slab[j] = rowf[pl.ds(part * j, part), :].astype(BF)
    for k in others:
        out_to(k).start()
    own_out = pltpu.make_async_copy(slab.at[rank], out.at[rank], local.at[n_reg + 2])
    own_out.start()

    ff, qo = grad_ranges(n_t, unit_live)
    cols_q = 512 * pairs
    grad_q = wu.at[:, pl.ds(0, cols_q)]
    chunk_d = Scatter(place, n_t, n_dp, ff, grad_d, dc, [d0, d1], [dz], [do], [fd], dsend, drecv)
    chunk_u = Scatter(place, n_t, n_dp, ff, grad_u, uc, [u0, u1], [uz], [uo], [fu], usend, urecv)
    chunk_q = Scatter(place, n_t, n_dp, qo, grad_q, dc.at[:, pl.ds(0, cols_q)],
                      [d0.at[:, pl.ds(0, cols_q)], d1.at[:, pl.ds(0, cols_q)]], [qz, sz],
                      [qo_got, so_got], [fq, fs], qsend, qrecv)

    def turn(ref):
        tr[...] = ref[...].astype(F32).T.astype(BF)

    def tiles(f):
        @pl.loop(0, full)
        def _(n):
            f(pl.ds(pl.multiple_of(n * wide, 128), wide))
        if units % wide:
            f(pl.ds(full * wide, units % wide))

    turn(rowb)

    def down_grad(at):
        grad_d[:, at] = dots(tr[...], act[:, at], 1, 0).astype(BF)

    tiles(down_grad)
    chunk_d.advance(0)
    turn(x_s)

    def up_grad(at):
        grad = dots(rowb[...], wd[at, :], 1, 1) * slope[:, at].astype(F32)
        small[0:1, at] = total(grad)
        low = grad.astype(BF)
        slope[:, at] = low
        grad_u[:, at] = dots(tr[...], low, 1, 0).astype(BF)

    tiles(up_grad)
    chunk_d.advance(1)
    chunk_u.advance(0)

    @pl.loop(0, 3)
    def _(i):
        at = rows(i)
        grad = dots(slope[at, :], wu[...], 1, 1) + g2f[at, :]
        normed = n1[at, :]
        small[1:2, 1536:2304] += total(grad * normed)
        small[2:3, 0:768] += total(grad)
        one = back(grad * row(2), normed, cr[at, HEAD : HEAD + 1])
        small[1:2, 768:1536] += total(one)
        g2f[at, :] = one
        rowb[at, :] = one.astype(BF)

    chunk_d.advance(2)
    chunk_u.advance(1)
    g.drain((1, 2, 3))
    turn(rowb)
    gc[...] = dots(rowb[...], wo[...], 1, 1).astype(BF)
    for p in range(pairs):
        grad_q[:, pl.ds(512 * p + 384, two)] = dots(
            tr[...], ctx[:, two * p : two * p + two], 1, 0).astype(BF)

    @pl.loop(0, 3)
    def _(i):
        x_s[rows(i), :] = hidden(rows(i)).astype(BF)

    turn(x_s)

    @pl.loop(0, pairs)
    def _(p):
        for i, steps in enumerate([((chunk_d, 3), (chunk_u, 2)), ((chunk_d, 4), (chunk_u, 3)),
                                   ((chunk_d, 5), (chunk_u, 4)), ((chunk_d, 6), (chunk_u, 5)),
                                   ((chunk_d, 7), (chunk_u, 6))]):
            @pl.when(p == i)
            def _(steps=steps):
                for chunk, stage in steps:
                    chunk.advance(stage)

        q_at, k_at, v_at = qkv_at(p)
        c_at = pl.ds(pl.multiple_of(p * two, 128), two)
        q, k, v, gctx = y_s[:, q_at], y_s[:, k_at], y_s[:, v_at], gc[:, c_at]
        gq, gk, gv = [], [], []
        for h in range(2):
            s_ref[...] = dots(v, gctx * half[h], 1, 1)
            for c0, cn in strips:
                gp = s_ref[:, c0 : c0 + cn]
                pr = p_s[2 * p + h, :, c0 : c0 + cn].astype(F32)
                dot = jnp.sum(gp * pr, axis=0, keepdims=True)
                gs_ref[:, c0 : c0 + cn] = (pr * (gp - dot)).astype(BF)
            gk.append(dots(gs_ref[...], q, 1, 0))
            gv.append(dots(p_s[2 * p + h], gctx, 1, 0))
            gq.append(dots(k, gs_ref[...], 0, 0))
        first = lane < HEAD
        turned = jnp.concatenate([gq[0][:HEAD], gq[1][HEAD:]], axis=0).T * 0.125
        gq_low = turned.astype(BF)
        gv_low = jnp.where(first, gv[0], gv[1]).astype(BF)
        y_s[:, q_at] = gq_low
        y_s[:, k_at] = jnp.where(first, gk[0], gk[1]).astype(BF)
        y_s[:, v_at] = gv_low
        small[3:4, pl.ds(pl.multiple_of(768 + p * two, 128), two)] = total(gq_low.astype(F32))
        small[3:4, pl.ds(pl.multiple_of(768 + two * pairs + p * two, 128), two)] = total(
            gv_low.astype(F32))
        here = pl.ds(pl.multiple_of(p * 384, 128), 384)
        grad_q[:, pl.ds(pl.multiple_of(p * 512, 128), 384)] = dots(
            tr[...], y_s[:, here], 1, 0).astype(BF)

    chunk_q.advance(0)

    @pl.loop(0, 3)
    def _(i):
        at = rows(i)
        grad = dots(y_s[at, :], wq[...], 1, 1) + g2f[at, :]
        covered = cr[at, 0:1] > 0.5
        small[1:2, 0:768] += total(jnp.where(covered, grad, 0.0))
        rowf[at, :] = 0.1 * jnp.where(covered, 0.0, grad)

    chunk_u.advance(7)
    hops = [place.mate] + place.partner + place.outer(n_dp)

    def hop(j):
        return pltpu.make_async_remote_copy(
            src_ref=small, dst_ref=sgot.at[j], send_sem=ssend.at[j], recv_sem=srecv.at[j],
            device_id=(hops[j], place.rank), device_id_type=MESH)

    def zhop(k):
        j = len(hops) + k - 1
        return pltpu.make_async_remote_copy(
            src_ref=small, dst_ref=sgot.at[j], send_sem=ssend.at[j], recv_sem=srecv.at[j],
            device_id=(place.dp, (place.rank + k) % n_t), device_id_type=MESH)

    hop(0).start()
    chunk_q.advance(1)
    for k in others:
        out_to(k).wait_send()
    own_out.wait()
    for j in range(n_t):
        slab[j] = rowf[pl.ds(part * j, part), :].astype(BF)
    for k in others:
        gin_to(k).start()
    own_gin = pltpu.make_async_copy(slab.at[rank], gin_out.at[rank], local.at[n_reg + 3])
    own_gin.start()
    for j in range(1, len(hops)):
        hop(j - 1).wait()
        small[...] = small[...] + sgot[j - 1]
        hop(j).start()
        if j <= 2:
            chunk_q.advance(j + 1)
    hop(len(hops) - 1).wait()
    small[...] = small[...] + sgot[len(hops) - 1]
    for k in others:
        zhop(k).start()
    chunk_q.advance(4)
    for k in others:
        zhop(k).wait()
    small[...] = small[...] + sgot[len(hops)] + sgot[len(hops) + 1] + sgot[len(hops) + 2]
    chunk_q.advance(5)
    chunk_q.advance(6)
    chunk_q.advance(7)
    for k in others:
        out_to(k, True).wait_recv()
        gin_to(k, True).wait_recv()
        gin_to(k).wait_send()
        up_to(k).wait_send()
        bias_to(k).wait_send()
    own_gin.wait()
    for chunk in (chunk_d, chunk_u, chunk_q):
        chunk.drain()


def run_layer(n_t, n_dp, unit_live, feat, starts, vecs, bias, gup, pair, spare, wo, wu, wd):
    frames, width = feat.shape
    units = sum(unit_live)
    wide = max(unit_live)
    pairs = n_t + 1
    heads = 2 * pairs * HEAD
    n_reg = 4 * n_t + 2 * sum(2 * r < n_t for r in range(n_t))
    outer = n_outer(n_dp)
    piece = width // GROUP
    hops = 1 + BITS + outer + n_t - 1
    n_sem = 1 + BITS + 2 * outer + 2 * (n_t - 1) + 2 * (BITS + 1)
    small = (8, units)

    def held(cols):
        return pltpu.VMEM((outer, piece, cols) if outer else (1, 8, 128), BF)

    vm = pl.BlockSpec(memory_space=pltpu.VMEM)
    hb = pl.BlockSpec(memory_space=pl.ANY)
    dma = pltpu.SemaphoreType.DMA
    scratch = dict(
        wq=pltpu.VMEM((width, 384 * pairs), BF), wo=pltpu.VMEM((heads, width), BF),
        wu=pltpu.VMEM((width, units), BF), wd=pltpu.VMEM((units, width), BF),
        spare_in=pltpu.VMEM((width, 384), BF), gb=pltpu.VMEM((n_t,) + bias.shape, F32),
        by=pltpu.VMEM((pairs, 8, 384), F32), bu=pltpu.VMEM((8, units), F32),
        cr=pltpu.VMEM((frames, 128), F32), x_s=pltpu.VMEM((frames, width), BF),
        y_s=pltpu.VMEM((frames, 384 * pairs), BF),
        p_s=pltpu.VMEM((2 * pairs, frames, frames), BF), ctx=pltpu.VMEM((frames, heads), BF),
        n1=pltpu.VMEM((frames, width), F32),
        act=pltpu.VMEM((frames, units), BF), slope=pltpu.VMEM((frames, units), BF),
        rowf=pltpu.VMEM((frames, width), F32), g2f=pltpu.VMEM((frames, width), F32),
        rowb=pltpu.VMEM((frames, width), BF), gc=pltpu.VMEM((frames, heads), BF),
        s_ref=pltpu.VMEM((frames, frames), F32), gs_ref=pltpu.VMEM((frames, frames), BF),
        tr=pltpu.VMEM((width, frames), BF), slab=pltpu.VMEM((n_t, frames // n_t, width), BF),
        gin=pltpu.VMEM((n_t, frames // n_t, width), BF),
        grad_d=pltpu.VMEM((width, units), BF), grad_u=pltpu.VMEM((width, units), BF),
        dc=pltpu.VMEM((width // 2, units), BF), d1=pltpu.VMEM((2 * piece, units), BF),
        d0=pltpu.VMEM((piece, units), BF), dz=pltpu.VMEM((n_t - 1, piece, wide), BF),
        uc=pltpu.VMEM((width // 2, units), BF), u1=pltpu.VMEM((2 * piece, units), BF),
        u0=pltpu.VMEM((piece, units), BF), uz=pltpu.VMEM((n_t - 1, piece, wide), BF),
        qz=pltpu.VMEM((n_t - 1, piece, 512), BF), sz=pltpu.VMEM((n_t - 1, piece, 512), BF),
        do=held(wide), uo=held(wide), qo_got=held(512), so_got=held(512),
        sgot=pltpu.VMEM((hops,) + small, F32),
        wsend=dma((n_reg, n_t - 1 + BITS + 1)), wrecv=dma((n_reg, BITS + 2)),
        local=dma((n_reg + 4,)), bsend=dma((n_t - 1,)), brecv=dma((n_t - 1,)),
        isend=dma((n_t - 1,)), irecv=dma((n_t - 1,)), osend=dma((n_t - 1,)),
        orecv=dma((n_t - 1,)), gsend=dma((n_t - 1,)), grecv=dma((n_t - 1,)),
        dsend=dma((n_sem,)), drecv=dma((n_sem,)), usend=dma((n_sem,)), urecv=dma((n_sem,)),
        qsend=dma((n_sem,)), qrecv=dma((n_sem,)), ssend=dma((hops,)), srecv=dma((hops,)),
    )
    slabs = jax.ShapeDtypeStruct((n_t, frames // n_t, width), BF)
    return pl.pallas_call(
        functools.partial(layer_kernel, n_t, n_dp, unit_live),
        out_shape=(slabs, slabs, jax.ShapeDtypeStruct((width, wide), BF),
                   jax.ShapeDtypeStruct((width, wide), BF), jax.ShapeDtypeStruct((width, 512), BF),
                   jax.ShapeDtypeStruct((width, 512), BF), jax.ShapeDtypeStruct(small, F32)),
        in_specs=[vm, pl.BlockSpec(memory_space=pltpu.SMEM), vm, vm] + [hb] * 6,
        out_specs=[hb, hb] + [vm] * 5,
        scratch_shapes=list(scratch.values()),
        compiler_params=pltpu.CompilerParams(
            collective_id=0, has_side_effects=True, vmem_limit_bytes=67043328),
        name="layer",
    )(feat, starts, vecs, bias, gup, pair, spare, wo, wu, wd)


def body(features, mask_starts, mask_vector, query_weight, query_bias, key_weight, value_weight,
         value_bias, output_weight, output_bias, attn_gain, attn_shift, up_weight, up_bias,
         down_weight, down_bias, final_gain, final_shift, grad_output):
    frames, item_count, width = features.shape
    n_t = lax.axis_size("tensor")
    n_d = lax.axis_size("dp")
    rank = lax.axis_index("tensor")
    slots = query_weight.shape[1] // HEAD
    units = up_weight.shape[1]
    unit_live = [units if r == 0 else units * 5 // 6 for r in range(n_t)]
    if n_t != 4 or slots != 3 or item_count != n_t or n_d % GROUP:
        raise ValueError("unsupported sizes")
    two = 2 * HEAD
    pairs = n_t + 1
    pair = jnp.concatenate([w[:, :two] for w in (query_weight, key_weight, value_weight)], axis=1)

    def halves(a):
        blank = jnp.zeros_like(a)
        return jnp.where(rank == 0, jnp.concatenate([a, blank], axis=-1),
                         jnp.concatenate([blank, a], axis=-1))

    spare = jnp.concatenate(
        [halves(w[:, two:]) for w in (query_weight, key_weight, value_weight)], axis=1)
    blank = jnp.zeros((two,), F32)
    line = jnp.concatenate([query_bias[:two], blank, value_bias[:two],
                            halves(query_bias[two:]), blank, halves(value_bias[two:])])
    bias = jnp.pad(jnp.stack([line, up_bias]), ((0, 6), (0, 0)))
    vecs = jnp.pad(jnp.stack([mask_vector, output_bias, attn_gain, attn_shift, down_bias,
                              final_gain, final_shift]), ((0, 1), (0, 0)))
    feat = lax.dynamic_slice_in_dim(features, rank, 1, 1)[:, 0]
    gup = grad_output.transpose(1, 0, 2)
    out, gin, fd, fu, fq, fs, small = run_layer(
        n_t, n_d, unit_live, feat, mask_starts, vecs, bias, gup, pair, spare, output_weight,
        up_weight, down_weight)
    layer_output = out.transpose(1, 0, 2)
    input_grad = gin.transpose(1, 0, 2)

    col = jnp.arange(units)
    alive = (rank == 0) | (col < units * 5 // 6)
    grad_down_weight = jnp.where(alive[None, :], fd.astype(F32), 0.0).T
    grad_up_weight = jnp.where(alive[None, :], fu.astype(F32), 0.0)
    fs32 = jnp.where(2 * rank < n_t, fs.astype(F32), 0.0)
    fq32 = fq.astype(F32)

    def own(which):
        third = fs32[:, two * which : two * which + two]
        third = jnp.where(rank == 0, third[:, :HEAD], third[:, HEAD:])
        return jnp.concatenate([fq32[:, two * which : two * which + two], third], axis=1)

    def own_vec(a):
        third = jnp.where(rank == 0, a[two * n_t : two * n_t + HEAD],
                          a[two * n_t + HEAD : two * n_t + two])
        third = jnp.where(2 * rank < n_t, third, 0.0)
        return jnp.concatenate([lax.dynamic_slice_in_dim(a, two * rank, two), third])

    ub = jnp.pad(small[0], (0, units))
    at = jnp.where(rank == 0, 0, units + (rank - 1) * (units * 5 // 6))
    grad_up_bias = jnp.where(alive, lax.dynamic_slice_in_dim(ub, at, units), 0.0)
    w = width
    heads = two * pairs
    return (layer_output, input_grad, small[1, :w], own(0), own_vec(small[3, w : w + heads]),
            own(1), own(2), own_vec(small[3, w + heads : w + 2 * heads]), own(3).T,
            small[1, w : 2 * w], small[1, 2 * w : 3 * w], small[2, :w], grad_up_weight,
            grad_up_bias, grad_down_weight, small[2, w : 2 * w], small[2, 2 * w : 3 * w],
            small[3, :w])


def solution(mesh):
    return jax.shard_map(
        body,
        mesh=mesh,
        in_specs=(P(None, "dp", None), P("dp", None), P(), P(None, "tensor"), P("tensor"),
                  P(None, "tensor"), P(None, "tensor"), P("tensor"), P("tensor", None), P(), P(),
                  P(), P(None, "tensor"), P("tensor"), P("tensor", None), P(), P(), P(),
                  P("tensor", "dp", None)),
        out_specs=(P("tensor", "dp", None), P("tensor", "dp", None), P(), P(None, "tensor"),
                   P("tensor"), P(None, "tensor"), P(None, "tensor"), P("tensor"),
                   P("tensor", None), P(), P(), P(), P(None, "tensor"), P("tensor"),
                   P("tensor", None), P(), P(), P()),
        check_vma=False,
    )
```

```python
import functools

import jax
import jax.numpy as jnp
from jax import lax
from jax.experimental import pallas as pl
from jax.experimental.pallas import tpu as pltpu
from jax.sharding import PartitionSpec as P

HEAD = 64
SPAN = 10
EPS = 1e-05
BF = jnp.bfloat16
F32 = jnp.float32
MESH = pl.DeviceIdType.MESH
GROUP = 8
BITS = 2


class Place:
    def __init__(self):
        self.rank = lax.axis_index("tensor")
        self.dp = lax.axis_index("dp")
        self.core = self.dp % 2
        self.mate = self.dp + 1 - 2 * self.core
        self.ways = []
        for way in range(2):
            turn = (self.core + way) % 2
            partner, piece = [], self.core * (GROUP // 2)
            for k in range(BITS):
                one, two = 2 << k, 2 << (BITS - 1 - k)
                bit = (1 - turn) * ((self.dp // one) % 2) + turn * ((self.dp // two) % 2)
                step = one + turn * (two - one)
                partner.append(self.dp + step * (1 - 2 * bit))
                piece = piece + bit * (1 << k)
            self.ways.append((partner + [self.mate], piece))
        self.partner = self.ways[0][0][:BITS]

    def way(self, rank, n_t):
        return self.ways[0 if 2 * rank < n_t else 1]

    def enter(self, n_dp):
        barrier = pltpu.get_barrier_semaphore()
        count = 0
        n_t = lax.axis_size("tensor")
        for k in range(1, n_t):
            pl.semaphore_signal(
                barrier, inc=1, device_id=(self.dp, (self.rank + k) % n_t), device_id_type=MESH
            )
            count += 1
        for other in [self.mate] + self.partner + self.outer(n_dp):
            pl.semaphore_signal(
                barrier, inc=1, device_id=(other, self.rank), device_id_type=MESH
            )
            count += 1
        pl.semaphore_wait(barrier, count)

    def outer(self, n_dp):
        others, step = [], GROUP
        while step < n_dp:
            bit = (self.dp // step) % 2
            others.append(self.dp + step * (1 - 2 * bit))
            step *= 2
        return others


def rows_at(ref, start, size, col0=None, cols=None):
    start = pl.multiple_of(start, 8)
    if col0 is None:
        return ref.at[pl.ds(start, size)]
    return ref.at[pl.ds(start, size), pl.ds(col0, cols)]


class Gather:
    def __init__(self, place, n_t, regions, send, recv):
        self.place, self.n_t, self.regions = place, n_t, regions
        self.send, self.recv = send, recv

    def own(self, sems, chunk, act):
        for i, (rank, name, srcs, dst, row0, rows, col0, _) in enumerate(self.regions):
            if name == chunk:
                @pl.when(self.place.rank == rank)
                def _(i=i, srcs=srcs, dst=dst, row0=row0, rows=rows, col0=col0):
                    for j, (src, col, cols) in enumerate(srcs):
                        act(pltpu.make_async_copy(
                            src(0, rows), rows_at(dst, row0, rows, col0 + col, cols),
                            sems.at[i, j]))

    def own_start(self, sems, chunk):
        self.own(sems, chunk, lambda c: c.start())

    def own_wait(self, sems, chunk):
        self.own(sems, chunk, lambda c: c.wait())

    def z_copies(self, i, k):
        rank, _, srcs, dst, row0, rows, col0, _ = self.regions[i]
        p = self.place
        size = rows // GROUP
        piece = p.way(rank, self.n_t)[1]
        return [pltpu.make_async_remote_copy(
            src_ref=src(piece * size, size),
            dst_ref=rows_at(dst, row0 + piece * size, size, col0 + col, cols),
            send_sem=self.send.at[i, 3 * (k - 1) + j],
            recv_sem=self.recv.at[i, BITS + 1 + j],
            device_id=(p.dp, (rank + k) % self.n_t),
            device_id_type=MESH,
        ) for j, (src, col, cols) in enumerate(srcs)]

    def z_start(self, chunk):
        for i, reg in enumerate(self.regions):
            if reg[1] == chunk:
                @pl.when(self.place.rank == reg[0])
                def _(i=i):
                    for k in range(1, self.n_t):
                        for c in self.z_copies(i, k):
                            c.start()

    def z_wait(self, chunk):
        for i, reg in enumerate(self.regions):
            if reg[1] == chunk:
                @pl.when(self.place.rank != reg[0])
                def _(i=i):
                    for c in self.z_copies(i, 1):
                        c.wait_recv()

    def copy(self, i, k):
        rank, _, _, dst, row0, rows, col0, cols = self.regions[i]
        p = self.place
        size = rows // GROUP * (1 << k)
        partner, piece = p.way(rank, self.n_t)
        block = piece // (1 << k)
        view = rows_at(dst, row0 + block * size, size, col0, cols)
        return pltpu.make_async_remote_copy(
            src_ref=view, dst_ref=view,
            send_sem=self.send.at[i, 3 * (self.n_t - 1) + k],
            recv_sem=self.recv.at[i, k],
            device_id=(partner[k], p.rank),
            device_id_type=MESH,
        )

    def start(self, k, chunk):
        for i, reg in enumerate(self.regions):
            if reg[1] == chunk:
                @pl.when(self.place.rank != reg[0])
                def _(i=i):
                    self.copy(i, k).start()

    def wait(self, k, chunk):
        for i, reg in enumerate(self.regions):
            if reg[1] == chunk:
                @pl.when(self.place.rank != reg[0])
                def _(i=i):
                    self.copy(i, k).wait_recv()

    def drain(self):
        for i, reg in enumerate(self.regions):
            @pl.when(self.place.rank == reg[0])
            def _(i=i):
                for k in range(1, self.n_t):
                    for c in self.z_copies(i, k):
                        c.wait_send()

            @pl.when(self.place.rank != reg[0])
            def _(i=i):
                for k in range(BITS + 1):
                    self.copy(i, k).wait_send()


def weight_regions(n_t, width, unit_live, q, k, v, spare, wo, wu, wd, gq, gs, go, gu, gd):
    def rows_of(ref, base, cols):
        return lambda start, size: rows_at(ref, base + start, size, 0, cols)

    two = 2 * HEAD
    out = []
    at = 0
    for r in range(n_t):
        full = 2 * r < n_t
        three = [(rows_of(w, 0, two), two * i, two) for i, w in enumerate((q, k, v))]
        out.append((r, "pair", three, gq, 0, width, 384 * r, 384))
        if full:
            out.append((r, "spare", [(rows_of(spare, 0, two * 2), 0, two * 2)], gs[r], 0, width, 0,
                        two * 2))
        out.append((r, "out", [(rows_of(wo, 0, width), 0, width)], go, two * r, two, 0, width))
        if full:
            out.append((r, "out", [(rows_of(wo, two, width), 0, width)], go, two * n_t + HEAD * r,
                        HEAD, 0, width))
        n = unit_live[r]
        out.append((r, "up", [(rows_of(wu, 0, n), 0, n)], gu, 0, width, at, n))
        out.append((r, "down", [(rows_of(wd, 0, width), 0, width)], gd, at, n, 0, width))
        at += n
    return out


def add_into(dst, dst0, a, a0, b, b0, size, step=16):
    @pl.loop(0, size // step)
    def _(i):
        def at(base):
            return pl.ds(pl.multiple_of(base + i * step, 8), step)
        dst[at(dst0), :] = (a[at(a0), :].astype(F32) + b[at(b0), :].astype(F32)).astype(dst.dtype)


class Scatter:
    def __init__(self, place, n_t, n_dp, ranges, grad, got_c, got_k, got_z, final, send, recv,
                 credit):
        self.place, self.n_t, self.n_dp, self.ranges = place, n_t, n_dp, ranges
        self.grad, self.got_c, self.got_k = grad, got_c, got_k
        self.got_z, self.final, self.credit = got_z, final, credit
        self.send, self.recv = send, recv
        self.half = grad.shape[0] // 2
        self.acc = rows_at(grad, place.core * self.half, self.half)
        self.size = grad.shape[0] // GROUP
        self.outer = place.outer(n_dp)
        self.cols = []
        for way in range(2):
            mine = [x[:2] for r in range(n_t) if (2 * r >= n_t) == bool(way) for x in ranges[r]]
            low = min((c for c, _ in mine), default=0)
            high = max((c + n for c, n in mine), default=0)
            self.cols.append((low, high - low))

    def local(self, way):
        return self.place.ways[way][1] - self.place.core * (GROUP // 2)

    def remote(self, src, dst, n, device):
        return pltpu.make_async_remote_copy(
            src_ref=src, dst_ref=dst, send_sem=self.send.at[n], recv_sem=self.recv.at[n],
            device_id=device, device_id_type=MESH)

    def core_copy(self):
        p = self.place
        return self.remote(rows_at(self.grad, (1 - p.core) * self.half, self.half), self.got_c, 0,
                           (p.mate, p.rank))

    def core_add(self):
        add_into(self.acc, 0, self.acc, 0, self.got_c, 0, self.half)

    def block(self, k, way):
        n = 1 << k
        at = self.local(way)
        keep = (at // n) * n
        bit = (at // n) % 2
        return keep * self.size, (keep + n - 2 * n * bit) * self.size, n * self.size

    def bit_copies(self, k):
        out = []
        for way, (col, cols) in enumerate(self.cols):
            if cols:
                _, give, size = self.block(k, way)
                out.append(self.remote(
                    rows_at(self.acc, give, size, col, cols),
                    self.got_k[k].at[:, pl.ds(col, cols)], 1 + 2 * k + way,
                    (self.place.ways[way][0][k], self.place.rank)))
        return out

    def bit_start(self, k):
        for c in self.bit_copies(k):
            c.start()

    def bit_finish(self, k):
        for c in self.bit_copies(k):
            c.wait_recv()
        for way, (col, cols) in enumerate(self.cols):
            if cols:
                keep, _, size = self.block(k, way)
                view = self.acc.at[:, pl.ds(col, cols)]
                add_into(view, keep, view, keep, self.got_k[k].at[:, pl.ds(col, cols)], 0, size)

    def outer_rounds(self, me):
        p = self.place
        for i, (_, cols, fi, _) in enumerate(self.ranges[me]):
            for j, other in enumerate(self.outer):
                n = i * len(self.outer) + j
                piece = p.way(me, self.n_t)[1]
                view = rows_at(self.final[fi], piece * self.size, self.size, 0, cols)
                got = self.got_k[0].at[:, pl.ds(0, cols)]
                pl.semaphore_signal(self.credit.at[n], inc=1, device_id=(other, p.rank),
                                    device_id_type=MESH)
                pl.semaphore_wait(self.credit.at[n], 1)
                c = self.remote(view, got, 1 + 2 * BITS + n, (other, p.rank))
                c.start()
                c.wait()
                add_into(view, 0, view, 0, got, 0, self.size)

    def z_base(self):
        return 1 + 2 * BITS + 2 * len(self.outer)

    def z_copies(self, to, k):
        p = self.place
        out = []
        for i, (col0, cols, _, zi) in enumerate(self.ranges[to]):
            out.append(self.remote(
                rows_at(self.acc, self.local(int(2 * to >= self.n_t)) * self.size, self.size, col0,
                        cols),
                self.got_z[zi].at[k - 1, :, pl.ds(0, cols)],
                self.z_base() + i * (self.n_t - 1) + k - 1, (p.dp, to)))
        return out

    def z_start(self):
        for to in range(self.n_t):
            for k in range(1, self.n_t):
                @pl.when(self.place.rank == (to - k) % self.n_t)
                def _(to=to, k=k):
                    for c in self.z_copies(to, k):
                        c.start()

    def z_finish(self):
        p = self.place
        for me in range(self.n_t):
            @pl.when(p.rank == me)
            def _(me=me):
                for k in range(1, self.n_t):
                    for c in self.z_copies(me, k):
                        c.wait_recv()
                way = int(2 * me >= self.n_t)
                for col0, cols, fi, zi in self.ranges[me]:
                    step = 16
                    @pl.loop(0, self.size // step)
                    def _(i):
                        a = pl.ds(pl.multiple_of(self.local(way) * self.size + i * step, 8), step)
                        z = pl.ds(pl.multiple_of(i * step, 8), step)
                        f = pl.ds(pl.multiple_of(p.ways[way][1] * self.size + i * step, 8),
                                  step)
                        total = self.acc[a, pl.ds(col0, cols)].astype(F32)
                        for k in range(self.n_t - 1):
                            total = total + self.got_z[zi][k, z, pl.ds(0, cols)].astype(F32)
                        self.final[fi][f, pl.ds(0, cols)] = total.astype(BF)
                if self.outer:
                    self.outer_rounds(me)

    def f_base(self):
        return self.z_base() + 2 * (self.n_t - 1)

    def f_copies(self, me, k):
        p = self.place
        out = []
        for i, (_, cols, fi, _) in enumerate(self.ranges[me]):
            size = self.size * (1 << k)
            partner, piece = p.way(me, self.n_t)
            view = rows_at(self.final[fi], (piece // (1 << k)) * size, size, 0, cols)
            out.append(self.remote(view, view, self.f_base() + i * (BITS + 1) + k,
                                   (partner[k], p.rank)))
        return out

    def f_start(self, k):
        for me in range(self.n_t):
            @pl.when(self.place.rank == me)
            def _(me=me):
                for c in self.f_copies(me, k):
                    c.start()

    def f_wait(self, k):
        for me in range(self.n_t):
            @pl.when(self.place.rank == me)
            def _(me=me):
                for c in self.f_copies(me, k):
                    c.wait_recv()

    def n_sems(self):
        return self.f_base() + 2 * (BITS + 1)

    def drain(self):
        self.core_copy().wait_send()
        for k in range(BITS):
            for c in self.bit_copies(k):
                c.wait_send()
        for to in range(self.n_t):
            for k in range(1, self.n_t):
                @pl.when(self.place.rank == (to - k) % self.n_t)
                def _(to=to, k=k):
                    for c in self.z_copies(to, k):
                        c.wait_send()
        for me in range(self.n_t):
            @pl.when(self.place.rank == me)
            def _(me=me):
                for k in range(BITS + 1):
                    for c in self.f_copies(me, k):
                        c.wait_send()

    def advance(self, stage):
        if stage == 0:
            self.core_copy().start()
        elif stage == 1:
            self.core_copy().wait_recv()
            self.core_add()
            self.bit_start(BITS - 1)
        elif stage <= BITS:
            k = BITS + 1 - stage
            self.bit_finish(k)
            self.bit_start(k - 1)
        elif stage == BITS + 1:
            self.bit_finish(0)
            self.z_start()
        elif stage == BITS + 2:
            self.z_finish()
            self.f_start(0)
        elif stage <= 2 * BITS + 2:
            k = stage - BITS - 3
            self.f_wait(k)
            self.f_start(k + 1)
        elif stage == 2 * BITS + 3:
            self.f_wait(BITS)


def n_outer(n_dp):
    n, step = 0, GROUP
    while step < n_dp:
        n, step = n + 1, step * 2
    return n


def grad_ranges(n_t, unit_live, first):
    ff, at = [], 0
    for r in range(n_t):
        ff.append([(at, unit_live[r], 0, 0)])
        at += unit_live[r]
    early, late = [], []
    for r in range(n_t):
        early.append([(512 * r, 512, 0, 0)] if r < first else [])
        here = [(512 * (r - first), 512, 0, 0)] if r >= first else []
        if 2 * r < n_t:
            here.append((512 * (n_t - first), 512, 1, 1))
        late.append(here)
    return ff, early, late


def dots(a, b, ca, cb):
    return lax.dot_general(a, b, (((ca,), (cb,)), ((), ())), preferred_element_type=F32)


def layer_kernel(n_t, n_dp, unit_live,
                 feat, starts, vecs, bias, gup, wq_in, wk_in, wv_in, spare, wo_in, wu_in, wd_in,
                 out, gin_out, fd, fu, fq, fs, small,
                 wq, wo, wu, wd, sp0, sp1, gb, by, bu, cr, x_s, y_s, p_s, ctx, n1, act,
                 slope, rowf, g2f, rowb, s_ref, gs_ref, tr, slab, grad_d, grad_u,
                 dc, d1, d0, dz, uc, u1, u0, uz, az, bz, sz, sgot,
                 wsend, wrecv, local, bsend, brecv, isend, irecv, osend, orecv, gsend, grecv,
                 dsend, drecv, usend, urecv, qsend, qrecv, psend, precv, ssend, srecv,
                 dcred, ucred, qcred, pcred):
    gin = slab
    gc = ctx
    place = Place()
    rank = place.rank
    frames, width = feat.shape
    part = frames // n_t
    pairs = n_t + 1
    two = 2 * HEAD
    tile = frames // 3
    units = wu.shape[1]
    wide = 256
    place.enter(n_dp)

    regions = weight_regions(n_t, width, unit_live, wq_in, wk_in, wv_in, spare, wo_in, wu_in,
                             wd_in, wq, (sp0, sp1), wo, wu, wd)
    g = Gather(place, n_t, regions, wsend, wrecv)
    n_reg = len(regions)

    def z_pass(src, dst, send, recv, k, incoming=False):
        to = (rank + k) % n_t
        at = (rank + n_t - k) % n_t if incoming else rank
        return pltpu.make_async_remote_copy(
            src_ref=src(to), dst_ref=dst.at[at], send_sem=send.at[k - 1], recv_sem=recv.at[k - 1],
            device_id=(place.dp, to), device_id_type=MESH)

    others = range(1, n_t)

    def bias_to(k, incoming=False):
        return z_pass(lambda to: bias, gb, bsend, brecv, k, incoming)

    def up_to(k, incoming=False):
        return z_pass(lambda to: gup.at[to], gin, isend, irecv, k, incoming)

    def out_to(k, incoming=False):
        return z_pass(lambda to: slab.at[to], out, osend, orecv, k, incoming)

    def gin_to(k, incoming=False):
        return z_pass(lambda to: slab.at[to], gin_out, gsend, grecv, k, incoming)

    g.z_start("pair")
    for k in others:
        bias_to(k).start()
    g.z_start("spare")
    g.own_start(local, "pair")
    g.own_start(local, "spare")
    own_bias = pltpu.make_async_copy(bias, gb.at[rank], local.at[n_reg, 0])
    own_up = pltpu.make_async_copy(gup.at[rank], gin.at[rank], local.at[n_reg, 1])
    own_bias.start()
    own_up.start()
    for name in ("out", "up", "down"):
        g.own_start(local, name)

    position = lax.broadcasted_iota(jnp.int32, (frames, 128), 0)
    hit = jnp.zeros((frames, 128), F32)
    for m in range(starts.shape[1]):
        first = starts[rank, m]
        hit = jnp.where((position >= first) & (position < first + SPAN), 1.0, hit)
    cr[...] = hit

    def row(i):
        return vecs[i : i + 1, :]

    def rows(i):
        return pl.ds(pl.multiple_of(i * tile, 16), tile)

    def hidden(at):
        return jnp.where(cr[at, 0:1] > 0.5, row(0), feat[at, :].astype(F32))

    @pl.loop(0, 3)
    def _(i):
        x_s[rows(i), :] = hidden(rows(i)).astype(BF)

    small[...] = jnp.zeros_like(small)

    g.z_wait("pair")
    g.start(0, "pair")
    g.z_start("up")
    g.z_wait("spare")
    g.start(0, "spare")
    g.wait(0, "pair")
    g.start(1, "pair")
    g.wait(0, "spare")
    g.start(1, "spare")
    for k in others:
        bias_to(k, True).wait_recv()
    own_bias.wait()
    for r in range(n_t):
        by[r, 0:1, :] = gb[r, 0:1, 0:384]
    by[n_t, 0:1, :] = gb[0, 0:1, 384:768] + gb[1, 0:1, 384:768]
    at = 0
    for r in range(n_t):
        bu[0:1, at : at + unit_live[r]] = gb[r, 1:2, 0 : unit_live[r]]
        at += unit_live[r]
    g.own_wait(local, "pair")
    g.own_wait(local, "spare")
    g.wait(1, "pair")
    g.start(2, "pair")
    g.z_wait("up")
    g.start(0, "up")
    g.z_start("out")
    g.z_start("down")
    g.wait(1, "spare")
    g.start(2, "spare")
    g.wait(2, "pair")

    lane3 = lax.broadcasted_iota(jnp.int32, (1, 384), 1)
    shrink = jnp.where(lane3 < two, 0.125, 1.0)

    def project(p):
        at = pl.ds(pl.multiple_of(p * 384, 128), 384)
        val = dots(x_s[...], wq[:, at], 1, 0) + by[p, 0:1, :]
        y_s[:, at] = (val.astype(BF).astype(F32) * shrink).astype(BF)

    pl.loop(0, n_t)(project)
    g.wait(0, "up")
    g.start(1, "up")
    g.wait(2, "spare")
    lane = lax.broadcasted_iota(jnp.int32, (1, two), 1)
    first = lane < HEAD

    @pl.loop(0, width // 192)
    def _(i):
        at = pl.ds(pl.multiple_of(i * 192, 16), 192)
        a, b = sp0[at, 0:two].astype(F32), sp1[at, 0:two].astype(F32)
        c, d = sp0[at, two : 2 * two].astype(F32), sp1[at, two : 2 * two].astype(F32)
        for j, val in enumerate((jnp.where(first, a, pltpu.roll(b, HEAD, 1)),
                                 jnp.where(first, pltpu.roll(a, HEAD, 1), b),
                                 jnp.where(first, c, d))):
            wq[at, pl.ds(384 * n_t + two * j, two)] = val.astype(BF)

    project(n_t)
    g.z_wait("out")
    g.start(0, "out")

    half = [jnp.where(lane < HEAD, 1.0, 0.0).astype(BF), jnp.where(lane < HEAD, 0.0, 1.0).astype(BF)]
    strips = [(128 * j, min(128, frames - 128 * j)) for j in range(-(-frames // 128))]

    def qkv_at(p):
        base = p * 384
        return [pl.ds(pl.multiple_of(base + two * j, 128), two) for j in range(3)]

    @pl.loop(0, pairs)
    def _(p):
        @pl.when(p == 2)
        def _():
            g.wait(0, "out")
            g.start(1, "out")

        @pl.when(p == 4)
        def _():
            g.z_wait("down")
            g.start(0, "down")
            for k in others:
                up_to(k).start()

        q_at, k_at, v_at = qkv_at(p)
        q, k, v = y_s[:, q_at], y_s[:, k_at], y_s[:, v_at]
        both = []
        for h in range(2):
            s_ref[...] = dots(k, q * half[h], 1, 1)
            for c0, cn in strips:
                s = s_ref[:, c0 : c0 + cn]
                e = jnp.exp(s - jnp.max(s, axis=0, keepdims=True))
                inv = 1.0 / jnp.sum(e, axis=0, keepdims=True)
                p_s[2 * p + h, :, c0 : c0 + cn] = (e * inv).astype(BF)
            both.append(dots(v, p_s[2 * p + h], 0, 0))
        turned = jnp.concatenate([both[0][:HEAD], both[1][HEAD:]], axis=0).T
        ctx[:, pl.ds(pl.multiple_of(p * two, 128), two)] = turned.astype(BF)

    g.wait(1, "up")
    g.start(2, "up")
    g.wait(1, "out")
    g.start(2, "out")
    g.wait(0, "down")
    g.start(1, "down")
    g.own_wait(local, "out")
    g.wait(2, "out")

    def norm(v):
        center = v - jnp.mean(v, axis=-1, keepdims=True)
        scaled = lax.rsqrt(jnp.mean(center * center, axis=-1, keepdims=True) + EPS)
        return center * scaled, scaled

    def back(e, normed, scaled):
        mean = jnp.mean(e, axis=-1, keepdims=True)
        proj = jnp.mean(e * normed, axis=-1, keepdims=True)
        return scaled * (e - mean - normed * proj)

    def total(v):
        return jnp.sum(v, axis=0, keepdims=True)

    @pl.loop(0, 3)
    def _(i):
        at = rows(i)
        res = hidden(at) + dots(ctx[at, :], wo[...], 1, 0) + row(1)
        normed, scaled = norm(res)
        n1[at, :] = normed
        cr[at, :] = jnp.where(lane < HEAD, cr[at, :], scaled)
        x_s[at, :] = (normed * row(2) + row(3)).astype(BF)

    g.own_wait(local, "up")
    g.wait(2, "up")

    def gelu_tile(at, cols):
        pre = dots(x_s[...], wu[:, at], 1, 0) + bu[0:1, at]
        cdf = 0.5 * (1.0 + lax.erf(pre * 0.7071067811865476))
        act[:, at] = (pre * cdf).astype(BF)
        pdf = jnp.exp(-0.5 * pre * pre) * 0.3989422804014327
        slope[:, at] = (cdf + pre * pdf).astype(BF)

    full = units // wide

    @pl.loop(0, full)
    def _(n):
        gelu_tile(pl.ds(pl.multiple_of(n * wide, 128), wide), wide)

    if units % wide:
        gelu_tile(pl.ds(full * wide, units % wide), units % wide)

    g.wait(1, "down")
    g.start(2, "down")
    for k in others:
        up_to(k, True).wait_recv()
    own_up.wait()
    for j in range(n_t):
        rowf[pl.ds(part * j, part), :] = gin[j].astype(F32)
    g.own_wait(local, "down")
    g.wait(2, "down")

    @pl.loop(0, 3)
    def _(i):
        at = rows(i)
        mid = n1[at, :] * row(2) + row(3)
        res = mid + dots(act[at, :], wd[...], 1, 0) + row(4)
        normed, scaled = norm(res)
        up = rowf[at, :]
        small[2:3, 1536:2304] += total(up * normed)
        small[3:4, 0:768] += total(up)
        grad = back(up * row(5), normed, scaled)
        small[2:3, 768:1536] += total(grad)
        g2f[at, :] = grad
        rowb[at, :] = grad.astype(BF)
        rowf[at, :] = normed * row(5) + row(6)

    for j in range(n_t):
        slab[j] = rowf[pl.ds(part * j, part), :].astype(BF)
    for k in others:
        out_to(k).start()
    own_out = pltpu.make_async_copy(slab.at[rank], out.at[rank], local.at[n_reg, 2])
    own_out.start()

    early = 3
    ff, qa, qb = grad_ranges(n_t, unit_live, early)
    split, end = 512 * early, 512 * pairs

    def sub(ref, start, stop):
        return ref.at[:, pl.ds(start, stop - start)]

    grad_q = sub(wu, 0, end)
    chunk_d = Scatter(place, n_t, n_dp, ff, grad_d, dc, [d0, d1], [dz], [fd], dsend, drecv, dcred)
    chunk_u = Scatter(place, n_t, n_dp, ff, grad_u, uc, [u0, u1], [uz], [fu], usend, urecv, ucred)
    chunk_a = Scatter(place, n_t, n_dp, qa, sub(wu, 0, split), sub(dc, 0, split),
                      [sub(d0, 0, split), sub(d1, 0, split)], [az], [fq], qsend, qrecv, qcred)
    chunk_b = Scatter(place, n_t, n_dp, qb, sub(wu, split, end), sub(dc, split, end),
                      [sub(d0, split, end), sub(d1, split, end)], [bz, sz], [fq, fs], psend, precv,
                      pcred)

    def turn(ref):
        tr[...] = ref[...].astype(F32).T.astype(BF)

    def tiles(f, hook=None):
        @pl.loop(0, full)
        def _(n):
            if hook is not None:
                pl.when(n == hook[0])(hook[1])
            f(pl.ds(pl.multiple_of(n * wide, 128), wide))

        if units % wide:
            f(pl.ds(full * wide, units % wide))

    turn(rowb)

    def down_grad(at):
        grad_d[:, at] = dots(tr[...], act[:, at], 1, 0).astype(BF)

    tiles(down_grad)
    chunk_d.advance(0)
    turn(x_s)

    def up_grad(at):
        grad = dots(rowb[...], wd[at, :], 1, 1) * slope[:, at].astype(F32)
        small[0:1, at] = total(grad)
        low = grad.astype(BF)
        slope[:, at] = low
        grad_u[:, at] = dots(tr[...], low, 1, 0).astype(BF)

    tiles(up_grad, (6, lambda: chunk_d.advance(1)))
    chunk_u.advance(0)

    @pl.loop(0, 3)
    def _(i):
        at = rows(i)
        grad = dots(slope[at, :], wu[...], 1, 1) + g2f[at, :]
        normed = n1[at, :]
        small[1:2, 1536:2304] += total(grad * normed)
        small[2:3, 0:768] += total(grad)
        one = back(grad * row(2), normed, cr[at, HEAD : HEAD + 1])
        small[1:2, 768:1536] += total(one)
        g2f[at, :] = one
        rowb[at, :] = one.astype(BF)

        @pl.when(i == 1)
        def _():
            chunk_d.advance(2)
            chunk_u.advance(1)

    g.drain()
    turn(rowb)
    for p in range(pairs):
        grad_q[:, pl.ds(512 * p + 384, two)] = dots(
            tr[...], ctx[:, two * p : two * p + two], 1, 0).astype(BF)
    gc[...] = dots(rowb[...], wo[...], 1, 1).astype(BF)

    @pl.loop(0, 3)
    def _(i):
        x_s[rows(i), :] = hidden(rows(i)).astype(BF)

    turn(x_s)

    @pl.loop(0, pairs)
    def _(p):
        def hooks(table):
            for i, steps in table.items():
                @pl.when(p == i)
                def _(steps=steps):
                    for chunk, stage in steps:
                        chunk.advance(stage)

        hooks({0: [(chunk_d, 3)], 2: [(chunk_u, 2)], 3: [(chunk_a, 0)], 4: [(chunk_u, 3)]})
        q_at, k_at, v_at = qkv_at(p)
        c_at = pl.ds(pl.multiple_of(p * two, 128), two)
        q, k, v, gctx = y_s[:, q_at], y_s[:, k_at], y_s[:, v_at], gc[:, c_at]
        gq, gk, gv = [], [], []
        for h in range(2):
            if h == 1:
                hooks({3: [(chunk_d, 4)], 4: [(chunk_a, 1)]})
            s_ref[...] = dots(v, gctx * half[h], 1, 1)
            for c0, cn in strips:
                gp = s_ref[:, c0 : c0 + cn]
                pr = p_s[2 * p + h, :, c0 : c0 + cn].astype(F32)
                dot = jnp.sum(gp * pr, axis=0, keepdims=True)
                gs_ref[:, c0 : c0 + cn] = (pr * (gp - dot)).astype(BF)
            gk.append(dots(gs_ref[...], q, 1, 0))
            gv.append(dots(p_s[2 * p + h], gctx, 1, 0))
            gq.append(dots(k, gs_ref[...], 0, 0))
        turned = jnp.concatenate([gq[0][:HEAD], gq[1][HEAD:]], axis=0).T * 0.125
        gq_low = turned.astype(BF)
        gv_low = jnp.where(first, gv[0], gv[1]).astype(BF)
        y_s[:, q_at] = gq_low
        y_s[:, k_at] = jnp.where(first, gk[0], gk[1]).astype(BF)
        y_s[:, v_at] = gv_low
        small[3:4, pl.ds(pl.multiple_of(768 + p * two, 128), two)] = total(gq_low.astype(F32))
        small[3:4, pl.ds(pl.multiple_of(768 + two * pairs + p * two, 128), two)] = total(
            gv_low.astype(F32))
        here = pl.ds(pl.multiple_of(p * 384, 128), 384)
        grad_q[:, pl.ds(pl.multiple_of(p * 512, 128), 384)] = dots(
            tr[...], y_s[:, here], 1, 0).astype(BF)

    chunk_b.advance(0)
    chunk_d.advance(5)

    @pl.loop(0, 3)
    def _(i):
        at = rows(i)
        grad = dots(y_s[at, :], wq[...], 1, 1) + g2f[at, :]
        covered = cr[at, 0:1] > 0.5
        small[1:2, 0:768] += total(jnp.where(covered, grad, 0.0))
        rowf[at, :] = 0.1 * jnp.where(covered, 0.0, grad)

    hops = [place.mate] + place.partner + place.outer(n_dp)

    def hop(j):
        return pltpu.make_async_remote_copy(
            src_ref=small, dst_ref=sgot.at[j], send_sem=ssend.at[j], recv_sem=srecv.at[j],
            device_id=(hops[j], place.rank), device_id_type=MESH)

    def zhop(k):
        j = len(hops) + k - 1
        return pltpu.make_async_remote_copy(
            src_ref=small, dst_ref=sgot.at[j], send_sem=ssend.at[j], recv_sem=srecv.at[j],
            device_id=(place.dp, (place.rank + k) % n_t), device_id_type=MESH)

    hop(0).start()
    for k in others:
        out_to(k).wait_send()
        out_to(k, True).wait_recv()
    own_out.wait()
    for j in range(n_t):
        slab[j] = rowf[pl.ds(part * j, part), :].astype(BF)
    for k in others:
        gin_to(k).start()
    own_gin = pltpu.make_async_copy(slab.at[rank], gin_out.at[rank], local.at[n_reg + 1, 0])
    own_gin.start()

    def round_of(j):
        hop(j - 1).wait()
        small[...] = small[...] + sgot[j - 1]
        hop(j).start()

    chunk_b.advance(1)
    chunk_d.advance(6)
    round_of(1)
    chunk_a.advance(2)
    chunk_d.advance(7)
    round_of(2)
    for j in range(3, len(hops)):
        round_of(j)
    chunk_b.advance(2)
    hop(len(hops) - 1).wait()
    small[...] = small[...] + sgot[len(hops) - 1]
    for k in others:
        zhop(k).start()
    chunk_u.advance(4)
    chunk_a.advance(3)
    chunk_u.advance(5)
    chunk_b.advance(3)
    chunk_u.advance(6)
    chunk_a.advance(4)
    chunk_u.advance(7)
    chunk_a.advance(5)
    chunk_b.advance(4)
    chunk_a.advance(6)
    chunk_b.advance(5)
    for k in others:
        zhop(k).wait()
    small[...] = small[...] + sgot[len(hops)] + sgot[len(hops) + 1] + sgot[len(hops) + 2]
    chunk_a.advance(7)
    chunk_b.advance(6)
    chunk_b.advance(7)
    for k in others:
        gin_to(k, True).wait_recv()
        gin_to(k).wait_send()
        up_to(k).wait_send()
        bias_to(k).wait_send()
    own_gin.wait()
    for chunk in (chunk_d, chunk_u, chunk_a, chunk_b):
        chunk.drain()


def run_layer(n_t, n_dp, unit_live, feat, starts, vecs, bias, gup, *weights):
    frames, width = feat.shape
    units = sum(unit_live)
    wide = max(unit_live)
    pairs = n_t + 1
    heads = 2 * pairs * HEAD
    n_reg = 4 * n_t + 2 * sum(2 * r < n_t for r in range(n_t))
    outer = n_outer(n_dp)
    piece = width // GROUP
    hops = 1 + BITS + outer + n_t - 1
    n_sem = 1 + 2 * BITS + 2 * outer + 2 * (n_t - 1) + 2 * (BITS + 1)
    small = (8, units)

    vm = pl.BlockSpec(memory_space=pltpu.VMEM)
    hb = pl.BlockSpec(memory_space=pl.ANY)
    dma = pltpu.SemaphoreType.DMA
    scratch = dict(
        wq=pltpu.VMEM((width, 384 * pairs), BF), wo=pltpu.VMEM((heads, width), BF),
        wu=pltpu.VMEM((width, units), BF), wd=pltpu.VMEM((units, width), BF),
        sp0=pltpu.VMEM((width, 256), BF), sp1=pltpu.VMEM((width, 256), BF), gb=pltpu.VMEM((n_t,) + bias.shape, F32),
        by=pltpu.VMEM((pairs, 8, 384), F32), bu=pltpu.VMEM((8, units), F32),
        cr=pltpu.VMEM((frames, 128), F32), x_s=pltpu.VMEM((frames, width), BF),
        y_s=pltpu.VMEM((frames, 384 * pairs), BF),
        p_s=pltpu.VMEM((2 * pairs, frames, frames), BF), ctx=pltpu.VMEM((frames, heads), BF),
        n1=pltpu.VMEM((frames, width), F32),
        act=pltpu.VMEM((frames, units), BF), slope=pltpu.VMEM((frames, units), BF),
        rowf=pltpu.VMEM((frames, width), F32), g2f=pltpu.VMEM((frames, width), F32),
        rowb=pltpu.VMEM((frames, width), BF),
        s_ref=pltpu.VMEM((frames, frames), F32), gs_ref=pltpu.VMEM((frames, frames), BF),
        tr=pltpu.VMEM((width, frames), BF), slab=pltpu.VMEM((n_t, frames // n_t, width), BF),
        grad_d=pltpu.VMEM((width, units), BF), grad_u=pltpu.VMEM((width, units), BF),
        dc=pltpu.VMEM((width // 2, units), BF), d1=pltpu.VMEM((2 * piece, units), BF),
        d0=pltpu.VMEM((piece, units), BF), dz=pltpu.VMEM((n_t - 1, piece, wide), BF),
        uc=pltpu.VMEM((width // 2, units), BF), u1=pltpu.VMEM((2 * piece, units), BF),
        u0=pltpu.VMEM((piece, units), BF), uz=pltpu.VMEM((n_t - 1, piece, wide), BF),
        az=pltpu.VMEM((n_t - 1, piece, 512), BF), bz=pltpu.VMEM((n_t - 1, piece, 512), BF),
        sz=pltpu.VMEM((n_t - 1, piece, 512), BF),
        sgot=pltpu.VMEM((hops,) + small, F32),
        wsend=dma((n_reg, 3 * (n_t - 1) + BITS + 1)), wrecv=dma((n_reg, BITS + 4)),
        local=dma((n_reg + 2, 3)), bsend=dma((n_t - 1,)), brecv=dma((n_t - 1,)),
        isend=dma((n_t - 1,)), irecv=dma((n_t - 1,)), osend=dma((n_t - 1,)),
        orecv=dma((n_t - 1,)), gsend=dma((n_t - 1,)), grecv=dma((n_t - 1,)),
        dsend=dma((n_sem,)), drecv=dma((n_sem,)), usend=dma((n_sem,)), urecv=dma((n_sem,)),
        qsend=dma((n_sem,)), qrecv=dma((n_sem,)), psend=dma((n_sem,)), precv=dma((n_sem,)),
        ssend=dma((hops,)), srecv=dma((hops,)),
        **{n: pltpu.SemaphoreType.REGULAR((max(2 * outer, 1),)) for n in ("dc_", "uc_", "qc_", "pc_")},
    )
    slabs = jax.ShapeDtypeStruct((n_t, frames // n_t, width), BF)
    return pl.pallas_call(
        functools.partial(layer_kernel, n_t, n_dp, unit_live),
        out_shape=(slabs, slabs, jax.ShapeDtypeStruct((width, wide), BF),
                   jax.ShapeDtypeStruct((width, wide), BF), jax.ShapeDtypeStruct((width, 512), BF),
                   jax.ShapeDtypeStruct((width, 512), BF), jax.ShapeDtypeStruct(small, F32)),
        in_specs=[vm, pl.BlockSpec(memory_space=pltpu.SMEM), vm, vm] + [hb] * 8,
        out_specs=[hb, hb] + [vm] * 5,
        scratch_shapes=list(scratch.values()),
        compiler_params=pltpu.CompilerParams(
            collective_id=0, has_side_effects=True, vmem_limit_bytes=67043328),
        name="layer",
    )(feat, starts, vecs, bias, gup, *weights)


def body(features, mask_starts, mask_vector, query_weight, query_bias, key_weight, value_weight,
         value_bias, output_weight, output_bias, attn_gain, attn_shift, up_weight, up_bias,
         down_weight, down_bias, final_gain, final_shift, grad_output):
    frames, item_count, width = features.shape
    n_t = lax.axis_size("tensor")
    n_d = lax.axis_size("dp")
    rank = lax.axis_index("tensor")
    slots = query_weight.shape[1] // HEAD
    units = up_weight.shape[1]
    unit_live = [units if r == 0 else units * 5 // 6 for r in range(n_t)]
    if n_t != 4 or slots != 3 or item_count != n_t or n_d % GROUP:
        raise ValueError("unsupported sizes")
    two = 2 * HEAD
    pairs = n_t + 1

    def halves(a):
        blank = jnp.zeros_like(a)
        return jnp.where(rank == 0, jnp.concatenate([a, blank], axis=-1),
                         jnp.concatenate([blank, a], axis=-1))

    value_third = value_weight[:, two:]
    spare = jnp.concatenate(
        [query_weight[:, two:], key_weight[:, two:], value_third, value_third], axis=1)
    blank = jnp.zeros((two,), F32)
    line = jnp.concatenate([query_bias[:two], blank, value_bias[:two],
                            halves(query_bias[two:]), blank, halves(value_bias[two:])])
    bias = jnp.pad(jnp.stack([line, up_bias]), ((0, 6), (0, 0)))
    vecs = jnp.pad(jnp.stack([mask_vector, output_bias, attn_gain, attn_shift, down_bias,
                              final_gain, final_shift]), ((0, 1), (0, 0)))
    feat = lax.dynamic_slice_in_dim(features, rank, 1, 1)[:, 0]
    gup = grad_output.transpose(1, 0, 2)
    out, gin, fd, fu, fq, fs, small = run_layer(
        n_t, n_d, unit_live, feat, mask_starts, vecs, bias, gup, query_weight, key_weight,
        value_weight, spare, output_weight, up_weight, down_weight)
    layer_output = out.transpose(1, 0, 2)
    input_grad = gin.transpose(1, 0, 2)

    col = jnp.arange(units)
    alive = (rank == 0) | (col < units * 5 // 6)
    grad_down_weight = jnp.where(alive[None, :], fd.astype(F32), 0.0).T
    grad_up_weight = jnp.where(alive[None, :], fu.astype(F32), 0.0)
    fs32 = jnp.where(2 * rank < n_t, fs.astype(F32), 0.0)
    fq32 = fq.astype(F32)

    def own(which):
        third = fs32[:, two * which : two * which + two]
        third = jnp.where(rank == 0, third[:, :HEAD], third[:, HEAD:])
        return jnp.concatenate([fq32[:, two * which : two * which + two], third], axis=1)

    def own_vec(a):
        third = jnp.where(rank == 0, a[two * n_t : two * n_t + HEAD],
                          a[two * n_t + HEAD : two * n_t + two])
        third = jnp.where(2 * rank < n_t, third, 0.0)
        return jnp.concatenate([lax.dynamic_slice_in_dim(a, two * rank, two), third])

    ub = jnp.pad(small[0], (0, units))
    at = jnp.where(rank == 0, 0, units + (rank - 1) * (units * 5 // 6))
    grad_up_bias = jnp.where(alive, lax.dynamic_slice_in_dim(ub, at, units), 0.0)
    w = width
    heads = two * pairs
    return (layer_output, input_grad, small[1, :w], own(0), own_vec(small[3, w : w + heads]),
            own(1), own(2), own_vec(small[3, w + heads : w + 2 * heads]), own(3).T,
            small[1, w : 2 * w], small[1, 2 * w : 3 * w], small[2, :w], grad_up_weight,
            grad_up_bias, grad_down_weight, small[2, w : 2 * w], small[2, 2 * w : 3 * w],
            small[3, :w])


def solution(mesh):
    return jax.shard_map(
        body,
        mesh=mesh,
        in_specs=(P(None, "dp", None), P("dp", None), P(), P(None, "tensor"), P("tensor"),
                  P(None, "tensor"), P(None, "tensor"), P("tensor"), P("tensor", None), P(), P(),
                  P(), P(None, "tensor"), P("tensor"), P("tensor", None), P(), P(), P(),
                  P("tensor", "dp", None)),
        out_specs=(P("tensor", "dp", None), P("tensor", "dp", None), P(), P(None, "tensor"),
                   P("tensor"), P(None, "tensor"), P(None, "tensor"), P("tensor"),
                   P("tensor", None), P(), P(), P(), P(None, "tensor"), P("tensor"),
                   P("tensor", None), P(), P(), P()),
        check_vma=False,
    )
```

```python
import functools

import jax
import jax.numpy as jnp
from jax import lax
from jax.experimental import pallas as pl
from jax.experimental.pallas import tpu as pltpu
from jax.sharding import PartitionSpec as P

HEAD = 64
SPAN = 10
EPS = 1e-05
BF = jnp.bfloat16
F32 = jnp.float32
MESH = pl.DeviceIdType.MESH
GROUP = 8
BITS = 2


class Place:
    def __init__(self):
        self.rank = lax.axis_index("tensor")
        self.dp = lax.axis_index("dp")
        self.core = self.dp % 2
        self.mate = self.dp + 1 - 2 * self.core
        self.ways = []
        for way in range(2):
            turn = (self.core + way) % 2
            partner, piece = [], self.core * (GROUP // 2)
            for k in range(BITS):
                one, two = 2 << k, 2 << (BITS - 1 - k)
                bit = (1 - turn) * ((self.dp // one) % 2) + turn * ((self.dp // two) % 2)
                step = one + turn * (two - one)
                partner.append(self.dp + step * (1 - 2 * bit))
                piece = piece + bit * (1 << k)
            self.ways.append((partner + [self.mate], piece))
        self.partner = self.ways[0][0][:BITS]

    def way(self, rank, n_t):
        return self.ways[0 if 2 * rank < n_t else 1]

    def enter(self, n_dp):
        barrier = pltpu.get_barrier_semaphore()
        count = 0
        n_t = lax.axis_size("tensor")
        for k in range(1, n_t):
            pl.semaphore_signal(
                barrier, inc=1, device_id=(self.dp, (self.rank + k) % n_t), device_id_type=MESH
            )
            count += 1
        for other in [self.mate] + self.partner + self.outer(n_dp):
            pl.semaphore_signal(
                barrier, inc=1, device_id=(other, self.rank), device_id_type=MESH
            )
            count += 1
        pl.semaphore_wait(barrier, count)

    def outer(self, n_dp):
        others, step = [], GROUP
        while step < n_dp:
            bit = (self.dp // step) % 2
            others.append(self.dp + step * (1 - 2 * bit))
            step *= 2
        return others


def rows_at(ref, start, size, col0=None, cols=None):
    start = pl.multiple_of(start, 8)
    if col0 is None:
        return ref.at[pl.ds(start, size)]
    return ref.at[pl.ds(start, size), pl.ds(col0, cols)]


class Gather:
    def __init__(self, place, n_t, regions, send, recv):
        self.place, self.n_t, self.regions = place, n_t, regions
        self.send, self.recv = send, recv

    def own(self, sems, chunk, act):
        for i, (rank, name, srcs, dst, row0, rows, col0, _) in enumerate(self.regions):
            if name == chunk:
                @pl.when(self.place.rank == rank)
                def _(i=i, srcs=srcs, dst=dst, row0=row0, rows=rows, col0=col0):
                    for j, (src, col, cols) in enumerate(srcs):
                        act(pltpu.make_async_copy(
                            src(0, rows), rows_at(dst, row0, rows, col0 + col, cols),
                            sems.at[i, j]))

    def own_start(self, sems, chunk):
        self.own(sems, chunk, lambda c: c.start())

    def own_wait(self, sems, chunk):
        self.own(sems, chunk, lambda c: c.wait())

    def z_copies(self, i, k):
        rank, _, srcs, dst, row0, rows, col0, _ = self.regions[i]
        p = self.place
        size = rows // GROUP
        piece = p.way(rank, self.n_t)[1]
        return [pltpu.make_async_remote_copy(
            src_ref=src(piece * size, size),
            dst_ref=rows_at(dst, row0 + piece * size, size, col0 + col, cols),
            send_sem=self.send.at[i, 3 * (k - 1) + j],
            recv_sem=self.recv.at[i, BITS + 1 + j],
            device_id=(p.dp, (rank + k) % self.n_t),
            device_id_type=MESH,
        ) for j, (src, col, cols) in enumerate(srcs)]

    def z_start(self, chunk):
        for i, reg in enumerate(self.regions):
            if reg[1] == chunk:
                @pl.when(self.place.rank == reg[0])
                def _(i=i):
                    for k in range(1, self.n_t):
                        for c in self.z_copies(i, k):
                            c.start()

    def z_wait(self, chunk):
        for i, reg in enumerate(self.regions):
            if reg[1] == chunk:
                @pl.when(self.place.rank != reg[0])
                def _(i=i):
                    for c in self.z_copies(i, 1):
                        c.wait_recv()

    def copy(self, i, k):
        rank, _, _, dst, row0, rows, col0, cols = self.regions[i]
        p = self.place
        size = rows // GROUP * (1 << k)
        partner, piece = p.way(rank, self.n_t)
        block = piece // (1 << k)
        view = rows_at(dst, row0 + block * size, size, col0, cols)
        return pltpu.make_async_remote_copy(
            src_ref=view, dst_ref=view,
            send_sem=self.send.at[i, 3 * (self.n_t - 1) + k],
            recv_sem=self.recv.at[i, k],
            device_id=(partner[k], p.rank),
            device_id_type=MESH,
        )

    def start(self, k, chunk):
        for i, reg in enumerate(self.regions):
            if reg[1] == chunk:
                @pl.when(self.place.rank != reg[0])
                def _(i=i):
                    self.copy(i, k).start()

    def wait(self, k, chunk):
        for i, reg in enumerate(self.regions):
            if reg[1] == chunk:
                @pl.when(self.place.rank != reg[0])
                def _(i=i):
                    self.copy(i, k).wait_recv()

    def drain(self):
        for i, reg in enumerate(self.regions):
            @pl.when(self.place.rank == reg[0])
            def _(i=i):
                for k in range(1, self.n_t):
                    for c in self.z_copies(i, k):
                        c.wait_send()

            @pl.when(self.place.rank != reg[0])
            def _(i=i):
                for k in range(BITS + 1):
                    self.copy(i, k).wait_send()


def weight_regions(n_t, width, unit_live, q, k, v, wo, wu, wd, gq, go, gu, gd):
    def rows_of(ref, base, cols):
        return lambda start, size: rows_at(ref, base + start, size, 0, cols)

    two = 2 * HEAD
    out = []
    at = 0
    for r in range(n_t):
        full = 2 * r < n_t
        for i, w in enumerate((q, k, v)):
            out.append((r, "pair", [(rows_of(w, 0, width), 0, width)], gq, 384 * r + two * i, two,
                        0, width))
            if full:
                out.append((r, "spare", [(rows_of(w, two, width), 0, width)], gq,
                            384 * n_t + two * i + HEAD * r, HEAD, 0, width))
        out.append((r, "out", [(rows_of(wo, 0, width), 0, width)], go, two * r, two, 0, width))
        if full:
            out.append((r, "out", [(rows_of(wo, two, width), 0, width)], go, two * n_t + HEAD * r,
                        HEAD, 0, width))
        n = unit_live[r]
        out.append((r, "up", [(rows_of(wu, 0, n), 0, n)], gu, 0, width, at, n))
        out.append((r, "down", [(rows_of(wd, 0, width), 0, width)], gd, at, n, 0, width))
        at += n
    return out


def add_into(dst, dst0, a, a0, b, b0, size, step=16):
    @pl.loop(0, size // step)
    def _(i):
        def at(base):
            return pl.ds(pl.multiple_of(base + i * step, 8), step)
        dst[at(dst0), :] = (a[at(a0), :].astype(F32) + b[at(b0), :].astype(F32)).astype(dst.dtype)


class Scatter:
    def __init__(self, place, n_t, n_dp, ranges, grad, got_c, got_k, got_z, final, send, recv,
                 credit):
        self.place, self.n_t, self.n_dp, self.ranges = place, n_t, n_dp, ranges
        self.grad, self.got_c, self.got_k = grad, got_c, got_k
        self.got_z, self.final, self.credit = got_z, final, credit
        self.send, self.recv = send, recv
        self.half = grad.shape[0] // 2
        self.acc = rows_at(grad, place.core * self.half, self.half)
        self.size = grad.shape[0] // GROUP
        self.outer = place.outer(n_dp)
        self.cols = []
        for way in range(2):
            mine = [x[:2] for r in range(n_t) if (2 * r >= n_t) == bool(way) for x in ranges[r]]
            low = min((c for c, _ in mine), default=0)
            high = max((c + n for c, n in mine), default=0)
            self.cols.append((low, high - low))

    def local(self, way):
        return self.place.ways[way][1] - self.place.core * (GROUP // 2)

    def remote(self, src, dst, n, device):
        return pltpu.make_async_remote_copy(
            src_ref=src, dst_ref=dst, send_sem=self.send.at[n], recv_sem=self.recv.at[n],
            device_id=device, device_id_type=MESH)

    def core_copy(self):
        p = self.place
        return self.remote(rows_at(self.grad, (1 - p.core) * self.half, self.half), self.got_c, 0,
                           (p.mate, p.rank))

    def core_add(self):
        add_into(self.acc, 0, self.acc, 0, self.got_c, 0, self.half)

    def block(self, k, way):
        n = 1 << k
        at = self.local(way)
        keep = (at // n) * n
        bit = (at // n) % 2
        return keep * self.size, (keep + n - 2 * n * bit) * self.size, n * self.size

    def bit_copies(self, k):
        out = []
        for way, (col, cols) in enumerate(self.cols):
            if cols:
                _, give, size = self.block(k, way)
                out.append(self.remote(
                    rows_at(self.acc, give, size, col, cols),
                    self.got_k[k].at[:, pl.ds(col, cols)], 1 + 2 * k + way,
                    (self.place.ways[way][0][k], self.place.rank)))
        return out

    def bit_start(self, k):
        for c in self.bit_copies(k):
            c.start()

    def bit_finish(self, k):
        for c in self.bit_copies(k):
            c.wait_recv()
        for way, (col, cols) in enumerate(self.cols):
            if cols:
                keep, _, size = self.block(k, way)
                view = self.acc.at[:, pl.ds(col, cols)]
                add_into(view, keep, view, keep, self.got_k[k].at[:, pl.ds(col, cols)], 0, size)

    def outer_rounds(self, me):
        p = self.place
        for i, (_, cols, fi, _) in enumerate(self.ranges[me]):
            for j, other in enumerate(self.outer):
                n = i * len(self.outer) + j
                piece = p.way(me, self.n_t)[1]
                view = rows_at(self.final[fi], piece * self.size, self.size, 0, cols)
                got = self.got_k[0].at[:, pl.ds(0, cols)]
                pl.semaphore_signal(self.credit.at[n], inc=1, device_id=(other, p.rank),
                                    device_id_type=MESH)
                pl.semaphore_wait(self.credit.at[n], 1)
                c = self.remote(view, got, 1 + 2 * BITS + n, (other, p.rank))
                c.start()
                c.wait()
                add_into(view, 0, view, 0, got, 0, self.size)

    def z_base(self):
        return 1 + 2 * BITS + 2 * len(self.outer)

    def z_copies(self, to, k):
        p = self.place
        out = []
        for i, (col0, cols, _, zi) in enumerate(self.ranges[to]):
            out.append(self.remote(
                rows_at(self.acc, self.local(int(2 * to >= self.n_t)) * self.size, self.size, col0,
                        cols),
                self.got_z[zi].at[k - 1, :, pl.ds(0, cols)],
                self.z_base() + i * (self.n_t - 1) + k - 1, (p.dp, to)))
        return out

    def z_start(self):
        for to in range(self.n_t):
            for k in range(1, self.n_t):
                @pl.when(self.place.rank == (to - k) % self.n_t)
                def _(to=to, k=k):
                    for c in self.z_copies(to, k):
                        c.start()

    def z_finish(self):
        p = self.place
        for me in range(self.n_t):
            @pl.when(p.rank == me)
            def _(me=me):
                for k in range(1, self.n_t):
                    for c in self.z_copies(me, k):
                        c.wait_recv()
                way = int(2 * me >= self.n_t)
                for col0, cols, fi, zi in self.ranges[me]:
                    step = 16
                    @pl.loop(0, self.size // step)
                    def _(i):
                        a = pl.ds(pl.multiple_of(self.local(way) * self.size + i * step, 8), step)
                        z = pl.ds(pl.multiple_of(i * step, 8), step)
                        f = pl.ds(pl.multiple_of(p.ways[way][1] * self.size + i * step, 8),
                                  step)
                        total = self.acc[a, pl.ds(col0, cols)].astype(F32)
                        for k in range(self.n_t - 1):
                            total = total + self.got_z[zi][k, z, pl.ds(0, cols)].astype(F32)
                        self.final[fi][f, pl.ds(0, cols)] = total.astype(BF)
                if self.outer:
                    self.outer_rounds(me)

    def f_base(self):
        return self.z_base() + 2 * (self.n_t - 1)

    def f_copies(self, me, k):
        p = self.place
        out = []
        for i, (_, cols, fi, _) in enumerate(self.ranges[me]):
            size = self.size * (1 << k)
            partner, piece = p.way(me, self.n_t)
            view = rows_at(self.final[fi], (piece // (1 << k)) * size, size, 0, cols)
            out.append(self.remote(view, view, self.f_base() + i * (BITS + 1) + k,
                                   (partner[k], p.rank)))
        return out

    def f_start(self, k):
        for me in range(self.n_t):
            @pl.when(self.place.rank == me)
            def _(me=me):
                for c in self.f_copies(me, k):
                    c.start()

    def f_wait(self, k):
        for me in range(self.n_t):
            @pl.when(self.place.rank == me)
            def _(me=me):
                for c in self.f_copies(me, k):
                    c.wait_recv()

    def n_sems(self):
        return self.f_base() + 2 * (BITS + 1)

    def drain(self):
        self.core_copy().wait_send()
        for k in range(BITS):
            for c in self.bit_copies(k):
                c.wait_send()
        for to in range(self.n_t):
            for k in range(1, self.n_t):
                @pl.when(self.place.rank == (to - k) % self.n_t)
                def _(to=to, k=k):
                    for c in self.z_copies(to, k):
                        c.wait_send()
        for me in range(self.n_t):
            @pl.when(self.place.rank == me)
            def _(me=me):
                for k in range(BITS + 1):
                    for c in self.f_copies(me, k):
                        c.wait_send()

    def advance(self, stage):
        if stage == 0:
            self.core_copy().start()
        elif stage == 1:
            self.core_copy().wait_recv()
            self.core_add()
            self.bit_start(BITS - 1)
        elif stage <= BITS:
            k = BITS + 1 - stage
            self.bit_finish(k)
            self.bit_start(k - 1)
        elif stage == BITS + 1:
            self.bit_finish(0)
            self.z_start()
        elif stage == BITS + 2:
            self.z_finish()
            self.f_start(0)
        elif stage <= 2 * BITS + 2:
            k = stage - BITS - 3
            self.f_wait(k)
            self.f_start(k + 1)
        elif stage == 2 * BITS + 3:
            self.f_wait(BITS)


def n_outer(n_dp):
    n, step = 0, GROUP
    while step < n_dp:
        n, step = n + 1, step * 2
    return n


def grad_ranges(n_t, unit_live, first):
    ff, at = [], 0
    for r in range(n_t):
        ff.append([(at, unit_live[r], 0, 0)])
        at += unit_live[r]
    early, late = [], []
    for r in range(n_t):
        early.append([(512 * r, 512, 0, 0)] if r < first else [])
        here = [(512 * (r - first), 512, 0, 0)] if r >= first else []
        if 2 * r < n_t:
            here.append((512 * (n_t - first), 512, 1, 1))
        late.append(here)
    return ff, early, late


def dots(a, b, ca, cb):
    return lax.dot_general(a, b, (((ca,), (cb,)), ((), ())), preferred_element_type=F32)


def layer_kernel(n_t, n_dp, unit_live,
                 features, starts, vm_, vo_, vag, vas, vdb, vfg, vfs, qb_in, vb_in, ub_in,
                 gup, wq_in, wk_in, wv_in, wo_in, wu_in, wd_in,
                 out, gin_out, out_d, fu, out_q, lines,
                 wq, wo, wu, wd, feat, fbuf, gb, by, bu, cr, x_s, y_s, p_s, ctx, n1, act,
                 slope, rowf, g2f, rowb, s_ref, gs_ref, tr, slab, grad_d, grad_u,
                 dc, d1, d0, dz, uc, u1, u0, uz, az, bz, sz, fd, fq, fs, bias, small, sgot,
                 wsend, wrecv, local, bsend, brecv, isend, irecv, osend, orecv, gsend, grecv,
                 dsend, drecv, usend, urecv, qsend, qrecv, psend, precv, ssend, srecv,
                 dcred, ucred, qcred, pcred):
    gin = slab
    gc = ctx
    place = Place()
    rank = place.rank
    frames, _, width = features.shape
    part = frames // n_t
    pairs = n_t + 1
    two = 2 * HEAD
    tile = frames // 3
    units = wu.shape[1]
    wide = 256
    bias[...] = jnp.zeros_like(bias)
    bias[0:1, 0 : 3 * HEAD] = qb_in[...].reshape(1, 3 * HEAD)
    bias[1:2, 0 : 3 * HEAD] = vb_in[...].reshape(1, 3 * HEAD)
    bias[2:3, :] = ub_in[...].reshape(1, width)
    place.enter(n_dp)

    regions = weight_regions(n_t, width, unit_live, wq_in, wk_in, wv_in, wo_in, wu_in, wd_in,
                             wq, wo, wu, wd)
    g = Gather(place, n_t, regions, wsend, wrecv)
    n_reg = len(regions)

    def z_pass(src, dst, send, recv, k, incoming=False):
        to = (rank + k) % n_t
        at = (rank + n_t - k) % n_t if incoming else rank
        return pltpu.make_async_remote_copy(
            src_ref=src(to), dst_ref=dst.at[at], send_sem=send.at[k - 1], recv_sem=recv.at[k - 1],
            device_id=(place.dp, to), device_id_type=MESH)

    others = range(1, n_t)

    def bias_to(k, incoming=False):
        return z_pass(lambda to: bias, gb, bsend, brecv, k, incoming)

    def up_to(k, incoming=False):
        return z_pass(lambda to: gup.at[to], gin, isend, irecv, k, incoming)

    def out_to(k, incoming=False):
        return z_pass(lambda to: slab.at[to], out, osend, orecv, k, incoming)

    def gin_to(k, incoming=False):
        return z_pass(lambda to: slab.at[to], gin_out, gsend, grecv, k, incoming)

    g.z_start("pair")
    for k in others:
        bias_to(k).start()
    g.own_start(local, "pair")
    g.own_start(local, "spare")
    g.z_start("spare")
    own_bias = pltpu.make_async_copy(bias, gb.at[rank], local.at[n_reg, 0])
    own_up = pltpu.make_async_copy(gup.at[rank], gin.at[rank], local.at[n_reg, 1])
    own_bias.start()
    own_up.start()
    for name in ("out", "up", "down"):
        g.own_start(local, name)

    position = lax.broadcasted_iota(jnp.int32, (frames, 128), 0)
    hit = jnp.zeros((frames, 128), F32)
    for m in range(starts.shape[1]):
        first = starts[rank, m]
        hit = jnp.where((position >= first) & (position < first + SPAN), 1.0, hit)
    cr[...] = hit

    def row(i):
        return (vm_, vo_, vag, vas, vdb, vfg, vfs)[i][...].reshape(1, width)

    def rows(i):
        return pl.ds(pl.multiple_of(i * tile, 16), tile)

    def hidden(at):
        return jnp.where(cr[at, 0:1] > 0.5, row(0), feat[at, :].astype(F32))

    some = fbuf.shape[0]
    for j in range(frames // some):
        c = pltpu.make_async_copy(features.at[pl.ds(some * j, some)], fbuf, local.at[0, 3])
        c.start()
        c.wait()
        for b in range(0, some, some // 3):
            val = fbuf[b : b + some // 3].astype(F32)
            mine = lax.broadcasted_iota(jnp.int32, val.shape, 1) == rank
            rowf[pl.ds(some * j + b, some // 3), :] = jnp.sum(jnp.where(mine, val, 0.0), axis=1)

    @pl.loop(0, 3)
    def _(i):
        at = rows(i)
        feat[at, :] = rowf[at, :].astype(BF)
        x_s[at, :] = hidden(at).astype(BF)

    small[...] = jnp.zeros_like(small)
    least = min(unit_live)
    for ref in (fd, fu):
        ref[:, least:] = jnp.zeros((width, ref.shape[1] - least), BF)

    g.z_wait("pair")
    g.start(0, "pair")
    g.z_start("up")
    g.z_wait("spare")
    g.start(0, "spare")
    g.wait(0, "pair")
    g.start(1, "pair")
    g.wait(0, "spare")
    g.start(1, "spare")
    for k in others:
        bias_to(k, True).wait_recv()
    own_bias.wait()
    for r in range(n_t):
        by[r, 0:1, :] = jnp.zeros((1, 384), F32)
        by[r, 0:1, 0:two] = gb[r, 0:1, 0:two]
        by[r, 0:1, 2 * two : 3 * two] = gb[r, 1:2, 0:two]
    by[n_t, 0:1, :] = jnp.zeros((1, 384), F32)
    for i, c0 in ((0, 0), (1, 2 * two)):
        by[n_t, 0:1, c0 : c0 + two] = jnp.concatenate(
            [gb[r, i : i + 1, two : 3 * HEAD] for r in range(2)], axis=1)
    at = 0
    for r in range(n_t):
        bu[0:1, at : at + unit_live[r]] = gb[r, 2:3, 0 : unit_live[r]]
        at += unit_live[r]
    g.own_wait(local, "pair")
    g.own_wait(local, "spare")
    g.wait(1, "pair")
    g.start(2, "pair")
    g.z_wait("up")
    g.start(0, "up")
    g.z_start("out")
    g.z_start("down")
    g.wait(1, "spare")
    g.start(2, "spare")
    g.wait(2, "pair")

    lane3 = lax.broadcasted_iota(jnp.int32, (1, 384), 1)
    shrink = jnp.where(lane3 < two, 0.125, 1.0)

    def project(p):
        at = pl.ds(pl.multiple_of(p * 384, 128), 384)
        val = dots(x_s[...], wq[at, :], 1, 1) + by[p, 0:1, :]
        y_s[:, at] = (val.astype(BF).astype(F32) * shrink).astype(BF)

    pl.loop(0, n_t)(project)
    g.wait(0, "up")
    g.start(1, "up")
    g.wait(2, "spare")
    lane = lax.broadcasted_iota(jnp.int32, (1, two), 1)
    first = lane < HEAD

    project(n_t)
    g.z_wait("out")
    g.start(0, "out")

    half = [jnp.where(lane < HEAD, 1.0, 0.0).astype(BF), jnp.where(lane < HEAD, 0.0, 1.0).astype(BF)]
    strips = [(128 * j, min(128, frames - 128 * j)) for j in range(-(-frames // 128))]

    def qkv_at(p):
        base = p * 384
        return [pl.ds(pl.multiple_of(base + two * j, 128), two) for j in range(3)]

    @pl.loop(0, pairs)
    def _(p):
        @pl.when(p == 2)
        def _():
            g.wait(0, "out")
            g.start(1, "out")

        @pl.when(p == 4)
        def _():
            g.z_wait("down")
            g.start(0, "down")
            for k in others:
                up_to(k).start()

        q_at, k_at, v_at = qkv_at(p)
        q, k, v = y_s[:, q_at], y_s[:, k_at], y_s[:, v_at]
        both = []
        for h in range(2):
            s_ref[...] = dots(k, q * half[h], 1, 1)
            for c0, cn in strips:
                s = s_ref[:, c0 : c0 + cn]
                e = jnp.exp(s - jnp.max(s, axis=0, keepdims=True))
                inv = 1.0 / jnp.sum(e, axis=0, keepdims=True)
                p_s[2 * p + h, :, c0 : c0 + cn] = (e * inv).astype(BF)
            both.append(dots(v, p_s[2 * p + h], 0, 0))
        turned = jnp.concatenate([both[0][:HEAD], both[1][HEAD:]], axis=0).T
        ctx[:, pl.ds(pl.multiple_of(p * two, 128), two)] = turned.astype(BF)

    g.wait(1, "up")
    g.start(2, "up")
    g.wait(1, "out")
    g.start(2, "out")
    g.wait(0, "down")
    g.start(1, "down")
    g.own_wait(local, "out")
    g.wait(2, "out")

    def norm(v):
        center = v - jnp.mean(v, axis=-1, keepdims=True)
        scaled = lax.rsqrt(jnp.mean(center * center, axis=-1, keepdims=True) + EPS)
        return center * scaled, scaled

    def back(e, normed, scaled):
        mean = jnp.mean(e, axis=-1, keepdims=True)
        proj = jnp.mean(e * normed, axis=-1, keepdims=True)
        return scaled * (e - mean - normed * proj)

    def total(v):
        return jnp.sum(v, axis=0, keepdims=True)

    @pl.loop(0, 3)
    def _(i):
        at = rows(i)
        res = hidden(at) + dots(ctx[at, :], wo[...], 1, 0) + row(1)
        normed, scaled = norm(res)
        n1[at, :] = normed
        cr[at, :] = jnp.where(lane < HEAD, cr[at, :], scaled)
        x_s[at, :] = (normed * row(2) + row(3)).astype(BF)

    g.own_wait(local, "up")
    g.wait(2, "up")

    def gelu_tile(at, cols):
        pre = dots(x_s[...], wu[:, at], 1, 0) + bu[0:1, at]
        cdf = 0.5 * (1.0 + lax.erf(pre * 0.7071067811865476))
        act[:, at] = (pre * cdf).astype(BF)
        pdf = jnp.exp(-0.5 * pre * pre) * 0.3989422804014327
        slope[:, at] = (cdf + pre * pdf).astype(BF)

    full = units // wide

    @pl.loop(0, full)
    def _(n):
        gelu_tile(pl.ds(pl.multiple_of(n * wide, 128), wide), wide)

    if units % wide:
        gelu_tile(pl.ds(full * wide, units % wide), units % wide)

    g.wait(1, "down")
    g.start(2, "down")
    for k in others:
        up_to(k, True).wait_recv()
    own_up.wait()
    for j in range(n_t):
        rowf[pl.ds(part * j, part), :] = gin[j].astype(F32)
    g.own_wait(local, "down")
    g.wait(2, "down")

    @pl.loop(0, 3)
    def _(i):
        at = rows(i)
        mid = n1[at, :] * row(2) + row(3)
        res = mid + dots(act[at, :], wd[...], 1, 0) + row(4)
        normed, scaled = norm(res)
        up = rowf[at, :]
        small[2:3, 1536:2304] += total(up * normed)
        small[3:4, 0:768] += total(up)
        grad = back(up * row(5), normed, scaled)
        small[2:3, 768:1536] += total(grad)
        g2f[at, :] = grad
        rowb[at, :] = grad.astype(BF)
        rowf[at, :] = normed * row(5) + row(6)

    for j in range(n_t):
        slab[j] = rowf[pl.ds(part * j, part), :].astype(BF)
    for k in others:
        out_to(k).start()
    own_out = pltpu.make_async_copy(slab.at[rank], out.at[rank], local.at[n_reg, 2])
    own_out.start()

    early = 3
    ff, qa, qb = grad_ranges(n_t, unit_live, early)
    split, end = 512 * early, 512 * pairs

    def sub(ref, start, stop):
        return ref.at[:, pl.ds(start, stop - start)]

    grad_q = sub(wu, 0, end)
    chunk_d = Scatter(place, n_t, n_dp, ff, grad_d, dc, [d0, d1], [dz], [fd], dsend, drecv, dcred)
    chunk_u = Scatter(place, n_t, n_dp, ff, grad_u, uc, [u0, u1], [uz], [fu], usend, urecv, ucred)
    chunk_a = Scatter(place, n_t, n_dp, qa, sub(wu, 0, split), sub(dc, 0, split),
                      [sub(d0, 0, split), sub(d1, 0, split)], [az], [fq], qsend, qrecv, qcred)
    chunk_b = Scatter(place, n_t, n_dp, qb, sub(wu, split, end), sub(dc, split, end),
                      [sub(d0, split, end), sub(d1, split, end)], [bz, sz], [fq, fs], psend, precv,
                      pcred)

    def turn(ref):
        tr[...] = ref[...].astype(F32).T.astype(BF)

    def tiles(f, hook=None):
        @pl.loop(0, full)
        def _(n):
            if hook is not None:
                pl.when(n == hook[0])(hook[1])
            f(pl.ds(pl.multiple_of(n * wide, 128), wide))

        if units % wide:
            f(pl.ds(full * wide, units % wide))

    turn(rowb)

    def down_grad(at):
        grad_d[:, at] = dots(tr[...], act[:, at], 1, 0).astype(BF)

    tiles(down_grad)
    chunk_d.advance(0)
    turn(x_s)

    def up_grad(at):
        grad = dots(rowb[...], wd[at, :], 1, 1) * slope[:, at].astype(F32)
        small[0:1, at] = total(grad)
        low = grad.astype(BF)
        slope[:, at] = low
        grad_u[:, at] = dots(tr[...], low, 1, 0).astype(BF)

    tiles(up_grad, (6, lambda: chunk_d.advance(1)))
    chunk_u.advance(0)

    @pl.loop(0, 3)
    def _(i):
        at = rows(i)
        grad = dots(slope[at, :], wu[...], 1, 1) + g2f[at, :]
        normed = n1[at, :]
        small[1:2, 1536:2304] += total(grad * normed)
        small[2:3, 0:768] += total(grad)
        one = back(grad * row(2), normed, cr[at, HEAD : HEAD + 1])
        small[1:2, 768:1536] += total(one)
        g2f[at, :] = one
        rowb[at, :] = one.astype(BF)

        @pl.when(i == 1)
        def _():
            chunk_d.advance(2)
            chunk_u.advance(1)

    g.drain()
    turn(rowb)
    for p in range(pairs):
        grad_q[:, pl.ds(512 * p + 384, two)] = dots(
            tr[...], ctx[:, two * p : two * p + two], 1, 0).astype(BF)
    gc[...] = dots(rowb[...], wo[...], 1, 1).astype(BF)

    @pl.loop(0, 3)
    def _(i):
        x_s[rows(i), :] = hidden(rows(i)).astype(BF)

    turn(x_s)

    @pl.loop(0, pairs)
    def _(p):
        def hooks(table):
            for i, steps in table.items():
                @pl.when(p == i)
                def _(steps=steps):
                    for chunk, stage in steps:
                        chunk.advance(stage)

        hooks({0: [(chunk_d, 3)], 2: [(chunk_u, 2)], 3: [(chunk_a, 0)], 4: [(chunk_u, 3)]})
        q_at, k_at, v_at = qkv_at(p)
        c_at = pl.ds(pl.multiple_of(p * two, 128), two)
        q, k, v, gctx = y_s[:, q_at], y_s[:, k_at], y_s[:, v_at], gc[:, c_at]
        gq, gk, gv = [], [], []
        for h in range(2):
            if h == 1:
                hooks({3: [(chunk_d, 4)], 4: [(chunk_a, 1)]})
            s_ref[...] = dots(v, gctx * half[h], 1, 1)
            for c0, cn in strips:
                gp = s_ref[:, c0 : c0 + cn]
                pr = p_s[2 * p + h, :, c0 : c0 + cn].astype(F32)
                dot = jnp.sum(gp * pr, axis=0, keepdims=True)
                gs_ref[:, c0 : c0 + cn] = (pr * (gp - dot)).astype(BF)
            gk.append(dots(gs_ref[...], q, 1, 0))
            gv.append(dots(p_s[2 * p + h], gctx, 1, 0))
            gq.append(dots(k, gs_ref[...], 0, 0))
        turned = jnp.concatenate([gq[0][:HEAD], gq[1][HEAD:]], axis=0).T * 0.125
        gq_low = turned.astype(BF)
        gv_low = jnp.where(first, gv[0], gv[1]).astype(BF)
        y_s[:, q_at] = gq_low
        y_s[:, k_at] = jnp.where(first, gk[0], gk[1]).astype(BF)
        y_s[:, v_at] = gv_low
        small[3:4, pl.ds(pl.multiple_of(768 + p * two, 128), two)] = total(gq_low.astype(F32))
        small[3:4, pl.ds(pl.multiple_of(768 + two * pairs + p * two, 128), two)] = total(
            gv_low.astype(F32))
        here = pl.ds(pl.multiple_of(p * 384, 128), 384)
        grad_q[:, pl.ds(pl.multiple_of(p * 512, 128), 384)] = dots(
            tr[...], y_s[:, here], 1, 0).astype(BF)

    chunk_b.advance(0)
    chunk_d.advance(5)

    @pl.loop(0, 3)
    def _(i):
        at = rows(i)
        grad = dots(y_s[at, :], wq[...], 1, 0) + g2f[at, :]
        covered = cr[at, 0:1] > 0.5
        small[1:2, 0:768] += total(jnp.where(covered, grad, 0.0))
        rowf[at, :] = 0.1 * jnp.where(covered, 0.0, grad)

    hops = [place.mate] + place.partner + place.outer(n_dp)

    def hop(j):
        return pltpu.make_async_remote_copy(
            src_ref=small, dst_ref=sgot.at[j], send_sem=ssend.at[j], recv_sem=srecv.at[j],
            device_id=(hops[j], place.rank), device_id_type=MESH)

    def zhop(k):
        j = len(hops) + k - 1
        return pltpu.make_async_remote_copy(
            src_ref=small, dst_ref=sgot.at[j], send_sem=ssend.at[j], recv_sem=srecv.at[j],
            device_id=(place.dp, (place.rank + k) % n_t), device_id_type=MESH)

    hop(0).start()
    for k in others:
        out_to(k).wait_send()
        out_to(k, True).wait_recv()
    own_out.wait()
    for j in range(n_t):
        slab[j] = rowf[pl.ds(part * j, part), :].astype(BF)
    for k in others:
        gin_to(k).start()
    own_gin = pltpu.make_async_copy(slab.at[rank], gin_out.at[rank], local.at[n_reg + 1, 0])
    own_gin.start()

    piece = width // 2

    def give_down():
        for block in range(2):
            val = fd[:, block * piece : block * piece + piece].astype(F32).T
            out_d[block * piece : block * piece + piece, :] = val.astype(BF)

    def round_of(j):
        hop(j - 1).wait()
        small[...] = small[...] + sgot[j - 1]
        hop(j).start()

    chunk_b.advance(1)
    chunk_d.advance(6)
    round_of(1)
    chunk_a.advance(2)
    chunk_d.advance(7)
    round_of(2)
    for j in range(3, len(hops)):
        round_of(j)
    chunk_b.advance(2)
    hop(len(hops) - 1).wait()
    small[...] = small[...] + sgot[len(hops) - 1]
    for k in others:
        zhop(k).start()
    chunk_u.advance(4)
    chunk_a.advance(3)
    give_down()
    chunk_u.advance(5)
    chunk_b.advance(3)
    chunk_u.advance(6)
    chunk_a.advance(4)
    chunk_u.advance(7)
    chunk_a.advance(5)
    chunk_b.advance(4)
    chunk_a.advance(6)
    chunk_b.advance(5)
    for k in others:
        zhop(k).wait()
    small[...] = small[...] + sgot[len(hops)] + sgot[len(hops) + 1] + sgot[len(hops) + 2]
    chunk_a.advance(7)
    chunk_b.advance(6)
    chunk_b.advance(7)
    for k in others:
        gin_to(k, True).wait_recv()
        gin_to(k).wait_send()
        up_to(k).wait_send()
        bias_to(k).wait_send()
    own_gin.wait()
    keep = 2 * rank < n_t

    for j in range(4):
        out_q[j, 0:two, :] = fq[:, two * j : two * j + two].astype(F32).T.astype(BF)
        val = fs[:, two * j : two * j + two].astype(F32).T
        val = jnp.where(rank == 0, val[:HEAD], val[HEAD:])
        out_q[j, two : two + HEAD, :] = jnp.where(keep, val, 0.0).astype(BF)
    lines[...] = jnp.zeros_like(lines)
    for i, (r, c) in enumerate(((1, 0), (1, 1), (1, 2), (2, 0), (2, 1), (2, 2), (3, 0))):
        lines[i : i + 1, :] = small[r : r + 1, c * width : c * width + width]
    at = 0
    for r in range(n_t):
        @pl.when(rank == r)
        def _(r=r, at=at):
            for i, base in ((7, width), (8, width + two * pairs)):
                c = base + two * r
                lines[i : i + 1, 0:two] = small[3:4, c : c + two]
                if 2 * r < n_t:
                    c = base + two * n_t + HEAD * r
                    lines[i : i + 1, two : two + HEAD] = small[3:4, c : c + HEAD]
            lines[9:10, 0 : unit_live[r]] = small[0:1, at : at + unit_live[r]]
        at += unit_live[r]
    for chunk in (chunk_d, chunk_u, chunk_a, chunk_b):
        chunk.drain()


def run_layer(n_t, n_dp, unit_live, features, starts, vectors, gup, *weights):
    frames, _, width = features.shape
    units = sum(unit_live)
    wide = max(unit_live)
    pairs = n_t + 1
    heads = 2 * pairs * HEAD
    n_reg = 6 * n_t + 4 * sum(2 * r < n_t for r in range(n_t))
    outer = n_outer(n_dp)
    piece = width // GROUP
    hops = 1 + BITS + outer + n_t - 1
    n_sem = 1 + 2 * BITS + 2 * outer + 2 * (n_t - 1) + 2 * (BITS + 1)
    small = (8, units)

    vm = pl.BlockSpec(memory_space=pltpu.VMEM)
    hb = pl.BlockSpec(memory_space=pl.ANY)
    dma = pltpu.SemaphoreType.DMA
    scratch = dict(
        wq=pltpu.VMEM((384 * pairs, width), BF), wo=pltpu.VMEM((heads, width), BF),
        wu=pltpu.VMEM((width, units), BF), wd=pltpu.VMEM((units, width), BF),
        feat=pltpu.VMEM((frames, width), BF), fbuf=pltpu.VMEM((frames // 8, n_t, width), BF),
        gb=pltpu.VMEM((n_t, 8, width), F32),
        by=pltpu.VMEM((pairs, 8, 384), F32), bu=pltpu.VMEM((8, units), F32),
        cr=pltpu.VMEM((frames, 128), F32), x_s=pltpu.VMEM((frames, width), BF),
        y_s=pltpu.VMEM((frames, 384 * pairs), BF),
        p_s=pltpu.VMEM((2 * pairs, frames, frames), BF), ctx=pltpu.VMEM((frames, heads), BF),
        n1=pltpu.VMEM((frames, width), F32),
        act=pltpu.VMEM((frames, units), BF), slope=pltpu.VMEM((frames, units), BF),
        rowf=pltpu.VMEM((frames, width), F32), g2f=pltpu.VMEM((frames, width), F32),
        rowb=pltpu.VMEM((frames, width), BF),
        s_ref=pltpu.VMEM((frames, frames), F32), gs_ref=pltpu.VMEM((frames, frames), BF),
        tr=pltpu.VMEM((width, frames), BF), slab=pltpu.VMEM((n_t, frames // n_t, width), BF),
        grad_d=pltpu.VMEM((width, units), BF), grad_u=pltpu.VMEM((width, units), BF),
        dc=pltpu.VMEM((width // 2, units), BF), d1=pltpu.VMEM((2 * piece, units), BF),
        d0=pltpu.VMEM((piece, units), BF), dz=pltpu.VMEM((n_t - 1, piece, wide), BF),
        uc=pltpu.VMEM((width // 2, units), BF), u1=pltpu.VMEM((2 * piece, units), BF),
        u0=pltpu.VMEM((piece, units), BF), uz=pltpu.VMEM((n_t - 1, piece, wide), BF),
        az=pltpu.VMEM((n_t - 1, piece, 512), BF), bz=pltpu.VMEM((n_t - 1, piece, 512), BF),
        sz=pltpu.VMEM((n_t - 1, piece, 512), BF),
        fd=pltpu.VMEM((width, wide), BF),
        fq=pltpu.VMEM((width, 512), BF), fs=pltpu.VMEM((width, 512), BF),
        bias=pltpu.VMEM((8, width), F32), small=pltpu.VMEM(small, F32),
        sgot=pltpu.VMEM((hops,) + small, F32),
        wsend=dma((n_reg, 3 * (n_t - 1) + BITS + 1)), wrecv=dma((n_reg, BITS + 4)),
        local=dma((n_reg + 2, 6)), bsend=dma((n_t - 1,)), brecv=dma((n_t - 1,)),
        isend=dma((n_t - 1,)), irecv=dma((n_t - 1,)), osend=dma((n_t - 1,)),
        orecv=dma((n_t - 1,)), gsend=dma((n_t - 1,)), grecv=dma((n_t - 1,)),
        dsend=dma((n_sem,)), drecv=dma((n_sem,)), usend=dma((n_sem,)), urecv=dma((n_sem,)),
        qsend=dma((n_sem,)), qrecv=dma((n_sem,)), psend=dma((n_sem,)), precv=dma((n_sem,)),
        ssend=dma((hops,)), srecv=dma((hops,)),
        **{n: pltpu.SemaphoreType.REGULAR((max(2 * outer, 1),)) for n in ("dc_", "uc_", "qc_", "pc_")},
    )
    slabs = jax.ShapeDtypeStruct((n_t, frames // n_t, width), BF)

    def f32(*shape):
        return jax.ShapeDtypeStruct(shape, F32)

    return pl.pallas_call(
        functools.partial(layer_kernel, n_t, n_dp, unit_live),
        out_shape=[slabs, slabs, jax.ShapeDtypeStruct((wide, width), BF),
                   jax.ShapeDtypeStruct((width, wide), BF),
                   jax.ShapeDtypeStruct((4, 3 * HEAD, width), BF), f32(16, width)],
        in_specs=[hb, pl.BlockSpec(memory_space=pltpu.SMEM)] + [vm] * 10 + [hb] * 7,
        out_specs=[hb] * 2 + [vm] * 4,
        scratch_shapes=list(scratch.values()),
        compiler_params=pltpu.CompilerParams(
            collective_id=0, has_side_effects=True, vmem_limit_bytes=67043328),
        name="layer",
    )(features, starts, *vectors, gup, *weights)


def body(features, mask_starts, mask_vector, query_weight, query_bias, key_weight, value_weight,
         value_bias, output_weight, output_bias, attn_gain, attn_shift, up_weight, up_bias,
         down_weight, down_bias, final_gain, final_shift, grad_output):
    frames, item_count, width = features.shape
    n_t = lax.axis_size("tensor")
    n_d = lax.axis_size("dp")
    rank = lax.axis_index("tensor")
    slots = query_weight.shape[1] // HEAD
    units = up_weight.shape[1]
    unit_live = [units if r == 0 else units * 5 // 6 for r in range(n_t)]
    if n_t != 4 or slots != 3 or item_count != n_t or n_d % GROUP:
        raise ValueError("unsupported sizes")
    vectors = [mask_vector, output_bias, attn_gain, attn_shift, down_bias, final_gain, final_shift,
               query_bias, value_bias, up_bias]
    out, gin, gwd, gwu, gqkvo, lines = run_layer(
        n_t, n_d, unit_live, features, mask_starts, vectors, grad_output.transpose(1, 0, 2),
        query_weight.T, key_weight.T, value_weight.T, output_weight, up_weight, down_weight)
    gm, gob, gag, gas, gdb, gfg, gfs, gqb, gvb, gub = [lines[i] for i in range(10)]
    cols = slots * HEAD
    gq, gk, gv, gwo = [gqkvo[i].astype(F32) for i in range(4)]
    return (out.transpose(1, 0, 2), gin.transpose(1, 0, 2), gm, gq.T, gqb[:cols], gk.T, gv.T,
            gvb[:cols], gwo, gob, gag, gas, gwu.astype(F32), gub, gwd.astype(F32), gdb, gfg, gfs)


def solution(mesh):
    return jax.shard_map(
        body,
        mesh=mesh,
        in_specs=(P(None, "dp", None), P("dp", None), P(), P(None, "tensor"), P("tensor"),
                  P(None, "tensor"), P(None, "tensor"), P("tensor"), P("tensor", None), P(), P(),
                  P(), P(None, "tensor"), P("tensor"), P("tensor", None), P(), P(), P(),
                  P("tensor", "dp", None)),
        out_specs=(P("tensor", "dp", None), P("tensor", "dp", None), P(), P(None, "tensor"),
                   P("tensor"), P(None, "tensor"), P(None, "tensor"), P("tensor"),
                   P("tensor", None), P(), P(), P(), P(None, "tensor"), P("tensor"),
                   P("tensor", None), P(), P(), P()),
        check_vma=False,
    )
```

```python
import functools

import jax
import jax.numpy as jnp
from jax import lax
from jax.experimental import pallas as pl
from jax.experimental.pallas import tpu as pltpu
from jax.sharding import PartitionSpec as P

HEAD = 64
SPAN = 10
EPS = 1e-05
BF = jnp.bfloat16
F32 = jnp.float32
MESH = pl.DeviceIdType.MESH
GROUP = 8
BITS = 2
WIDE = ()


class Place:
    def __init__(self):
        self.rank = lax.axis_index("tensor")
        self.dp = lax.axis_index("dp")
        self.core = self.dp % 2
        self.mate = self.dp + 1 - 2 * self.core
        self.ways = []
        for way in range(2):
            turn = (self.core + way) % 2
            partner, piece = [], self.core * (GROUP // 2)
            for k in range(BITS):
                one, two = 2 << k, 2 << (BITS - 1 - k)
                bit = (1 - turn) * ((self.dp // one) % 2) + turn * ((self.dp // two) % 2)
                step = one + turn * (two - one)
                partner.append(self.dp + step * (1 - 2 * bit))
                piece = piece + bit * (1 << k)
            self.ways.append((partner + [self.mate], piece))
        self.partner = self.ways[0][0][:BITS]

    def way(self, rank, n_t):
        return self.ways[0 if 2 * rank < n_t else 1]

    def enter(self, n_dp):
        barrier = pltpu.get_barrier_semaphore()
        count = 0
        n_t = lax.axis_size("tensor")
        for k in range(1, n_t):
            pl.semaphore_signal(
                barrier, inc=1, device_id=(self.dp, (self.rank + k) % n_t), device_id_type=MESH
            )
            count += 1
        for other in [self.mate] + self.partner + self.outer(n_dp):
            pl.semaphore_signal(
                barrier, inc=1, device_id=(other, self.rank), device_id_type=MESH
            )
            count += 1
        pl.semaphore_wait(barrier, count)

    def outer(self, n_dp):
        others, step = [], GROUP
        while step < n_dp:
            bit = (self.dp // step) % 2
            others.append(self.dp + step * (1 - 2 * bit))
            step *= 2
        return others


def rows_at(ref, start, size, col0=None, cols=None):
    start = pl.multiple_of(start, 8)
    if col0 is None:
        return ref.at[pl.ds(start, size)]
    return ref.at[pl.ds(start, size), pl.ds(col0, cols)]


class Gather:
    def __init__(self, place, n_t, regions, send, recv):
        self.place, self.n_t, self.regions = place, n_t, regions
        self.send, self.recv = send, recv

    def own(self, sems, chunk, act):
        for i, (rank, name, srcs, dst, row0, rows, col0, _) in enumerate(self.regions):
            if name == chunk:
                @pl.when(self.place.rank == rank)
                def _(i=i, srcs=srcs, dst=dst, row0=row0, rows=rows, col0=col0):
                    for j, (src, col, cols) in enumerate(srcs):
                        act(pltpu.make_async_copy(
                            src(0, rows), rows_at(dst, row0, rows, col0 + col, cols),
                            sems.at[i, j]))

    def own_start(self, sems, chunk):
        self.own(sems, chunk, lambda c: c.start())

    def own_wait(self, sems, chunk):
        self.own(sems, chunk, lambda c: c.wait())

    def first(self, i):
        return 1 if self.regions[i][1] in WIDE else 0

    def z_copies(self, i, k):
        rank, _, srcs, dst, row0, rows, col0, _ = self.regions[i]
        p = self.place
        size = rows // GROUP << self.first(i)
        piece = p.way(rank, self.n_t)[1] // (1 << self.first(i))
        return [pltpu.make_async_remote_copy(
            src_ref=src(piece * size, size),
            dst_ref=rows_at(dst, row0 + piece * size, size, col0 + col, cols),
            send_sem=self.send.at[i, 3 * (k - 1) + j],
            recv_sem=self.recv.at[i, BITS + 1 + j],
            device_id=(p.dp, (rank + k) % self.n_t),
            device_id_type=MESH,
        ) for j, (src, col, cols) in enumerate(srcs)]

    def z_start(self, chunk):
        for i, reg in enumerate(self.regions):
            if reg[1] == chunk:
                @pl.when(self.place.rank == reg[0])
                def _(i=i):
                    for k in range(1, self.n_t):
                        for c in self.z_copies(i, k):
                            c.start()

    def z_wait(self, chunk):
        for i, reg in enumerate(self.regions):
            if reg[1] == chunk:
                @pl.when(self.place.rank != reg[0])
                def _(i=i):
                    for c in self.z_copies(i, 1):
                        c.wait_recv()

    def copy(self, i, k):
        rank, _, _, dst, row0, rows, col0, cols = self.regions[i]
        p = self.place
        size = rows // GROUP * (1 << k)
        partner, piece = p.way(rank, self.n_t)
        block = piece // (1 << k)
        view = rows_at(dst, row0 + block * size, size, col0, cols)
        return pltpu.make_async_remote_copy(
            src_ref=view, dst_ref=view,
            send_sem=self.send.at[i, 3 * (self.n_t - 1) + k],
            recv_sem=self.recv.at[i, k],
            device_id=(partner[k], p.rank),
            device_id_type=MESH,
        )

    def start(self, k, chunk):
        for i, reg in enumerate(self.regions):
            if reg[1] == chunk and k >= self.first(i):
                @pl.when(self.place.rank != reg[0])
                def _(i=i):
                    self.copy(i, k).start()

    def wait(self, k, chunk):
        for i, reg in enumerate(self.regions):
            if reg[1] == chunk and k >= self.first(i):
                @pl.when(self.place.rank != reg[0])
                def _(i=i):
                    self.copy(i, k).wait_recv()

    def drain(self):
        for i, reg in enumerate(self.regions):
            @pl.when(self.place.rank == reg[0])
            def _(i=i):
                for k in range(1, self.n_t):
                    for c in self.z_copies(i, k):
                        c.wait_send()

            @pl.when(self.place.rank != reg[0])
            def _(i=i):
                for k in range(self.first(i), BITS + 1):
                    self.copy(i, k).wait_send()


def weight_regions(n_t, width, unit_live, q, k, v, wo, wu, wd, gq, go, gu, gd):
    def rows_of(ref, base, cols):
        return lambda start, size: rows_at(ref, base + start, size, 0, cols)

    two = 2 * HEAD
    out = []
    at = 0
    for r in range(n_t):
        full = 2 * r < n_t
        for i, w in enumerate((q, k, v)):
            out.append((r, "pair", [(rows_of(w, 0, width), 0, width)], gq, 384 * r + two * i, two,
                        0, width))
            if full:
                out.append((r, "spare", [(rows_of(w, two, width), 0, width)], gq,
                            384 * n_t + two * i + HEAD * r, HEAD, 0, width))
        out.append((r, "out", [(rows_of(wo, 0, width), 0, width)], go, two * r, two, 0, width))
        if full:
            out.append((r, "out", [(rows_of(wo, two, width), 0, width)], go, two * n_t + HEAD * r,
                        HEAD, 0, width))
        n = unit_live[r]
        out.append((r, "up", [(rows_of(wu, 0, n), 0, n)], gu, 0, width, at, n))
        out.append((r, "down", [(rows_of(wd, 0, width), 0, width)], gd, at, n, 0, width))
        at += n
    return out


def add_into(dst, dst0, a, a0, b, b0, size, step=16):
    @pl.loop(0, size // step)
    def _(i):
        def at(base):
            return pl.ds(pl.multiple_of(base + i * step, 8), step)
        dst[at(dst0), :] = (a[at(a0), :].astype(F32) + b[at(b0), :].astype(F32)).astype(dst.dtype)


class Scatter:
    def __init__(self, place, n_t, n_dp, ranges, grad, got_c, got_k, got_z, final, send, recv,
                 credit):
        self.place, self.n_t, self.n_dp, self.ranges = place, n_t, n_dp, ranges
        self.grad, self.got_c, self.got_k = grad, got_c, got_k
        self.got_z, self.final, self.credit = got_z, final, credit
        self.send, self.recv = send, recv
        self.half = grad.shape[0] // 2
        self.acc = rows_at(grad, place.core * self.half, self.half)
        self.size = grad.shape[0] // GROUP
        self.outer = place.outer(n_dp)
        self.cols = []
        for way in range(2):
            mine = [x[:2] for r in range(n_t) if (2 * r >= n_t) == bool(way) for x in ranges[r]]
            low = min((c for c, _ in mine), default=0)
            high = max((c + n for c, n in mine), default=0)
            self.cols.append((low, high - low))

    def local(self, way):
        return self.place.ways[way][1] - self.place.core * (GROUP // 2)

    def remote(self, src, dst, n, device):
        return pltpu.make_async_remote_copy(
            src_ref=src, dst_ref=dst, send_sem=self.send.at[n], recv_sem=self.recv.at[n],
            device_id=device, device_id_type=MESH)

    def core_copy(self):
        p = self.place
        return self.remote(rows_at(self.grad, (1 - p.core) * self.half, self.half), self.got_c, 0,
                           (p.mate, p.rank))

    def core_add(self):
        add_into(self.acc, 0, self.acc, 0, self.got_c, 0, self.half)

    def block(self, k, way):
        n = 1 << k
        at = self.local(way)
        keep = (at // n) * n
        bit = (at // n) % 2
        return keep * self.size, (keep + n - 2 * n * bit) * self.size, n * self.size

    def bit_copies(self, k):
        out = []
        for way, (col, cols) in enumerate(self.cols):
            if cols:
                _, give, size = self.block(k, way)
                out.append(self.remote(
                    rows_at(self.acc, give, size, col, cols),
                    self.got_k[k].at[:, pl.ds(col, cols)], 1 + 2 * k + way,
                    (self.place.ways[way][0][k], self.place.rank)))
        return out

    def bit_start(self, k):
        for c in self.bit_copies(k):
            c.start()

    def bit_finish(self, k):
        for c in self.bit_copies(k):
            c.wait_recv()
        for way, (col, cols) in enumerate(self.cols):
            if cols:
                keep, _, size = self.block(k, way)
                view = self.acc.at[:, pl.ds(col, cols)]
                add_into(view, keep, view, keep, self.got_k[k].at[:, pl.ds(col, cols)], 0, size)

    def outer_rounds(self, me):
        p = self.place
        for i, (_, cols, fi, _) in enumerate(self.ranges[me]):
            for j, other in enumerate(self.outer):
                n = i * len(self.outer) + j
                piece = p.way(me, self.n_t)[1]
                view = rows_at(self.final[fi], piece * self.size, self.size, 0, cols)
                got = self.got_k[0].at[:, pl.ds(0, cols)]
                pl.semaphore_signal(self.credit.at[n], inc=1, device_id=(other, p.rank),
                                    device_id_type=MESH)
                pl.semaphore_wait(self.credit.at[n], 1)
                c = self.remote(view, got, 1 + 2 * BITS + n, (other, p.rank))
                c.start()
                c.wait()
                add_into(view, 0, view, 0, got, 0, self.size)

    def z_base(self):
        return 1 + 2 * BITS + 2 * len(self.outer)

    def z_copies(self, to, slot, device):
        p = self.place
        out = []
        for i, (col0, cols, _, zi) in enumerate(self.ranges[to]):
            out.append(self.remote(
                rows_at(self.acc, self.local(int(2 * to >= self.n_t)) * self.size, self.size, col0,
                        cols),
                self.got_z[zi].at[slot, :, pl.ds(0, cols)],
                self.z_base() + i * (self.n_t - 1) + slot, (p.dp, device)))
        return out

    def at_rank(self, act):
        for me in range(self.n_t):
            pl.when(self.place.rank == me)(functools.partial(act, me))

    def z_first(self, me):
        return self.z_copies(me ^ 1, 0, me ^ 1) + self.z_copies(me ^ 3, 1, me ^ 1)

    def z_second(self, me):
        return self.z_copies(me ^ 2, 2, me ^ 2)

    def z_got(self, me, slots):
        for to, slot in ((me, 0), (me ^ 2, 1), (me, 2)):
            if slot in slots:
                for c in self.z_copies(to, slot, me ^ 1):
                    c.wait_recv()

    def z_start(self):
        def act(me):
            for c in self.z_first(me):
                c.start()
        self.at_rank(act)

    def z_turn(self):
        def act(me):
            for c in self.z_first(me):
                c.wait_send()
            self.z_got(me, (0, 1))
            for slot, to in ((1, me ^ 2), (0, me)):
                at = self.local(int(2 * to >= self.n_t)) * self.size
                for col0, cols, _, zi in self.ranges[to]:
                    view = self.acc.at[:, pl.ds(col0, cols)]
                    add_into(view, at, view, at, self.got_z[zi].at[slot, :, pl.ds(0, cols)], 0,
                             self.size)
                if slot == 1:
                    for c in self.z_second(me):
                        c.start()
        self.at_rank(act)

    def z_finish(self):
        def act(me):
            self.z_got(me, (2,))
            way = int(2 * me >= self.n_t)
            for col0, cols, fi, zi in self.ranges[me]:
                add_into(self.final[fi].at[:, pl.ds(0, cols)], self.place.ways[way][1] * self.size,
                         self.acc.at[:, pl.ds(col0, cols)], self.local(way) * self.size,
                         self.got_z[zi].at[2, :, pl.ds(0, cols)], 0, self.size)
            if self.outer:
                self.outer_rounds(me)
        self.at_rank(act)

    def f_base(self):
        return self.z_base() + 2 * (self.n_t - 1)

    def f_copies(self, me, k):
        p = self.place
        out = []
        for i, (_, cols, fi, _) in enumerate(self.ranges[me]):
            size = self.size * (1 << k)
            partner, piece = p.way(me, self.n_t)
            view = rows_at(self.final[fi], (piece // (1 << k)) * size, size, 0, cols)
            out.append(self.remote(view, view, self.f_base() + i * (BITS + 1) + k,
                                   (partner[k], p.rank)))
        return out

    def f_start(self, k):
        for me in range(self.n_t):
            @pl.when(self.place.rank == me)
            def _(me=me):
                for c in self.f_copies(me, k):
                    c.start()

    def f_wait(self, k):
        for me in range(self.n_t):
            @pl.when(self.place.rank == me)
            def _(me=me):
                for c in self.f_copies(me, k):
                    c.wait_recv()

    def n_sems(self):
        return self.f_base() + 2 * (BITS + 1)

    def drain(self):
        self.core_copy().wait_send()
        for k in range(BITS):
            for c in self.bit_copies(k):
                c.wait_send()
        def act(me):
            for c in self.z_second(me):
                c.wait_send()
        self.at_rank(act)
        for me in range(self.n_t):
            @pl.when(self.place.rank == me)
            def _(me=me):
                for k in range(BITS + 1):
                    for c in self.f_copies(me, k):
                        c.wait_send()

    def advance(self, stage):
        if stage == 0:
            self.core_copy().start()
        elif stage == 1:
            self.core_copy().wait_recv()
            self.core_add()
            self.bit_start(BITS - 1)
        elif stage <= BITS:
            k = BITS + 1 - stage
            self.bit_finish(k)
            self.bit_start(k - 1)
        elif stage == BITS + 1:
            self.bit_finish(0)
            self.z_start()
        elif stage == BITS + 2:
            self.z_turn()
        elif stage == BITS + 3:
            self.z_finish()
            self.f_start(0)
        elif stage <= 2 * BITS + 3:
            k = stage - BITS - 4
            self.f_wait(k)
            self.f_start(k + 1)
        elif stage == 2 * BITS + 4:
            self.f_wait(BITS)


def n_outer(n_dp):
    n, step = 0, GROUP
    while step < n_dp:
        n, step = n + 1, step * 2
    return n


def grad_ranges(n_t, unit_live, first):
    ff, at = [], 0
    for r in range(n_t):
        ff.append([(at, unit_live[r], 0, 0)])
        at += unit_live[r]
    early, late = [], []
    for r in range(n_t):
        early.append([(512 * r, 512, 0, 0)] if r < first else [])
        here = [(512 * (r - first), 512, 0, 0)] if r >= first else []
        if 2 * r < n_t:
            here.append((512 * (n_t - first), 512, 1, 1))
        late.append(here)
    return ff, early, late


def dots(a, b, ca, cb):
    return lax.dot_general(a, b, (((ca,), (cb,)), ((), ())), preferred_element_type=F32)


def layer_kernel(n_t, n_dp, unit_live,
                 features, starts, vm_, vo_, vag, vas, vdb, vfg, vfs, qb_in, vb_in, ub_in,
                 gup, wq_in, wk_in, wv_in, wo_in, wu_in, wd_in,
                 out, gin_out, out_d, fu, out_q, lines,
                 wq, wo, wu, wd, feat, fbuf, gb, by, bu, cr, x_s, y_s, p_s, ctx, n1, act,
                 slope, rowf, g2f, rowb, s_ref, gs_ref, tr, slab, grad_d, grad_u,
                 dc, d1, d0, dz, uc, u1, u0, uz, az, bz, sz, fd, fq, fs, bias, small, sgot,
                 wsend, wrecv, local, bsend, brecv, isend, irecv, osend, orecv, gsend, grecv,
                 dsend, drecv, usend, urecv, qsend, qrecv, psend, precv, ssend, srecv,
                 dcred, ucred, qcred, pcred):
    gin = slab
    gc = ctx
    place = Place()
    rank = place.rank
    frames, _, width = features.shape
    part = frames // n_t
    pairs = n_t + 1
    two = 2 * HEAD
    tile = frames // 3
    units = wu.shape[1]
    wide = 256
    bias[...] = jnp.zeros_like(bias)
    bias[0:1, 0 : 3 * HEAD] = qb_in[...].reshape(1, 3 * HEAD)
    bias[1:2, 0 : 3 * HEAD] = vb_in[...].reshape(1, 3 * HEAD)
    bias[2:3, :] = ub_in[...].reshape(1, width)
    place.enter(n_dp)

    regions = weight_regions(n_t, width, unit_live, wq_in, wk_in, wv_in, wo_in, wu_in, wd_in,
                             wq, wo, wu, wd)
    g = Gather(place, n_t, regions, wsend, wrecv)
    n_reg = len(regions)

    def z_pass(src, dst, send, recv, k, incoming=False):
        to = (rank + k) % n_t
        at = (rank + n_t - k) % n_t if incoming else rank
        return pltpu.make_async_remote_copy(
            src_ref=src(to), dst_ref=dst.at[at], send_sem=send.at[k - 1], recv_sem=recv.at[k - 1],
            device_id=(place.dp, to), device_id_type=MESH)

    others = range(1, n_t)

    def bias_to(k, incoming=False):
        return z_pass(lambda to: bias, gb, bsend, brecv, k, incoming)

    def up_to(k, incoming=False):
        return z_pass(lambda to: gup.at[to], gin, isend, irecv, k, incoming)

    def out_to(k, incoming=False):
        return z_pass(lambda to: slab.at[to], out, osend, orecv, k, incoming)

    def gin_to(k, incoming=False):
        return z_pass(lambda to: slab.at[to], gin_out, gsend, grecv, k, incoming)

    g.z_start("pair")
    for k in others:
        bias_to(k).start()
    g.own_start(local, "pair")
    g.own_start(local, "spare")
    g.z_start("up")
    own_bias = pltpu.make_async_copy(bias, gb.at[rank], local.at[n_reg, 0])
    own_up = pltpu.make_async_copy(gup.at[rank], gin.at[rank], local.at[n_reg, 1])
    own_bias.start()
    own_up.start()
    for name in ("out", "up", "down"):
        g.own_start(local, name)

    position = lax.broadcasted_iota(jnp.int32, (frames, 128), 0)
    hit = jnp.zeros((frames, 128), F32)
    for m in range(starts.shape[1]):
        first = starts[rank, m]
        hit = jnp.where((position >= first) & (position < first + SPAN), 1.0, hit)
    cr[...] = hit

    def row(i):
        return (vm_, vo_, vag, vas, vdb, vfg, vfs)[i][...].reshape(1, width)

    def rows(i):
        return pl.ds(pl.multiple_of(i * tile, 16), tile)

    def hidden(at):
        return jnp.where(cr[at, 0:1] > 0.5, row(0), feat[at, :].astype(F32))

    small[...] = jnp.zeros_like(small)
    least = min(unit_live)
    for ref in (fd, fu):
        ref[:, least:] = jnp.zeros((width, ref.shape[1] - least), BF)

    g.z_wait("pair")
    g.start(0, "pair")
    g.z_start("spare")
    g.z_start("out")
    some = fbuf.shape[0]
    for j in range(frames // some):
        c = pltpu.make_async_copy(features.at[pl.ds(some * j, some)], fbuf, local.at[0, 3])
        c.start()
        c.wait()
        for b in range(0, some, some // 3):
            val = fbuf[b : b + some // 3].astype(F32)
            mine = lax.broadcasted_iota(jnp.int32, val.shape, 1) == rank
            rowf[pl.ds(some * j + b, some // 3), :] = jnp.sum(jnp.where(mine, val, 0.0), axis=1)

    g.wait(0, "pair")
    g.start(1, "pair")
    g.z_wait("up")
    g.start(0, "up")
    g.z_start("down")
    @pl.loop(0, 3)
    def _(i):
        at = rows(i)
        feat[at, :] = rowf[at, :].astype(BF)
        x_s[at, :] = hidden(at).astype(BF)

    for k in others:
        bias_to(k, True).wait_recv()
    own_bias.wait()
    for r in range(n_t):
        by[r, 0:1, :] = jnp.zeros((1, 384), F32)
        by[r, 0:1, 0:two] = gb[r, 0:1, 0:two]
        by[r, 0:1, 2 * two : 3 * two] = gb[r, 1:2, 0:two]
    by[n_t, 0:1, :] = jnp.zeros((1, 384), F32)
    for i, c0 in ((0, 0), (1, 2 * two)):
        by[n_t, 0:1, c0 : c0 + two] = jnp.concatenate(
            [gb[r, i : i + 1, two : 3 * HEAD] for r in range(2)], axis=1)
    at = 0
    for r in range(n_t):
        bu[0:1, at : at + unit_live[r]] = gb[r, 2:3, 0 : unit_live[r]]
        at += unit_live[r]
    g.own_wait(local, "pair")
    g.own_wait(local, "spare")
    g.wait(1, "pair")
    g.start(2, "pair")
    g.z_wait("spare")
    g.start(0, "spare")
    g.z_wait("out")
    g.start(0, "out")
    g.wait(0, "up")
    g.start(1, "up")
    g.wait(2, "pair")

    lane3 = lax.broadcasted_iota(jnp.int32, (1, 384), 1)
    shrink = jnp.where(lane3 < two, 0.125, 1.0)

    def project(p):
        at = pl.ds(pl.multiple_of(p * 384, 128), 384)
        val = dots(x_s[...], wq[at, :], 1, 1) + by[p, 0:1, :]
        y_s[:, at] = (val.astype(BF).astype(F32) * shrink).astype(BF)

    pl.loop(0, n_t)(project)
    g.wait(0, "spare")
    g.start(1, "spare")
    g.wait(0, "out")
    g.start(1, "out")
    g.z_wait("down")
    g.start(0, "down")
    for k in others:
        up_to(k).start()
    lane = lax.broadcasted_iota(jnp.int32, (1, two), 1)
    first = lane < HEAD

    half = [jnp.where(lane < HEAD, 1.0, 0.0).astype(BF), jnp.where(lane < HEAD, 0.0, 1.0).astype(BF)]
    strips = [(128 * j, min(128, frames - 128 * j)) for j in range(-(-frames // 128))]

    def qkv_at(p):
        base = p * 384
        return [pl.ds(pl.multiple_of(base + two * j, 128), two) for j in range(3)]

    @pl.loop(0, pairs)
    def _(p):
        @pl.when(p == 2)
        def _():
            g.wait(1, "spare")
            g.start(2, "spare")
            g.wait(1, "out")
            g.start(2, "out")
            g.wait(1, "up")
            g.start(2, "up")

        @pl.when(p == 3)
        def _():
            g.wait(0, "down")
            g.start(1, "down")

        @pl.when(p == n_t)
        def _():
            g.wait(2, "spare")
            project(n_t)

        q_at, k_at, v_at = qkv_at(p)
        q, k, v = y_s[:, q_at], y_s[:, k_at], y_s[:, v_at]
        both = []
        for h in range(2):
            s_ref[...] = dots(k, q * half[h], 1, 1)
            for c0, cn in strips:
                s = s_ref[:, c0 : c0 + cn]
                e = jnp.exp(s - jnp.max(s, axis=0, keepdims=True))
                inv = 1.0 / jnp.sum(e, axis=0, keepdims=True)
                p_s[2 * p + h, :, c0 : c0 + cn] = (e * inv).astype(BF)
            both.append(dots(v, p_s[2 * p + h], 0, 0))
        turned = jnp.concatenate([both[0][:HEAD], both[1][HEAD:]], axis=0).T
        ctx[:, pl.ds(pl.multiple_of(p * two, 128), two)] = turned.astype(BF)

    g.own_wait(local, "out")
    g.wait(2, "out")

    def norm(v):
        center = v - jnp.mean(v, axis=-1, keepdims=True)
        scaled = lax.rsqrt(jnp.mean(center * center, axis=-1, keepdims=True) + EPS)
        return center * scaled, scaled

    def back(e, normed, scaled):
        mean = jnp.mean(e, axis=-1, keepdims=True)
        proj = jnp.mean(e * normed, axis=-1, keepdims=True)
        return scaled * (e - mean - normed * proj)

    def total(v):
        return jnp.sum(v, axis=0, keepdims=True)

    @pl.loop(0, 3)
    def _(i):
        at = rows(i)
        res = hidden(at) + dots(ctx[at, :], wo[...], 1, 0) + row(1)
        normed, scaled = norm(res)
        n1[at, :] = normed
        cr[at, :] = jnp.where(lane < HEAD, cr[at, :], scaled)
        x_s[at, :] = (normed * row(2) + row(3)).astype(BF)

    g.own_wait(local, "up")
    g.wait(2, "up")

    def gelu_tile(at, cols):
        pre = dots(x_s[...], wu[:, at], 1, 0) + bu[0:1, at]
        cdf = 0.5 * (1.0 + lax.erf(pre * 0.7071067811865476))
        act[:, at] = (pre * cdf).astype(BF)
        pdf = jnp.exp(-0.5 * pre * pre) * 0.3989422804014327
        slope[:, at] = (cdf + pre * pdf).astype(BF)

    full = units // wide

    @pl.loop(0, full)
    def _(n):
        gelu_tile(pl.ds(pl.multiple_of(n * wide, 128), wide), wide)

    if units % wide:
        gelu_tile(pl.ds(full * wide, units % wide), units % wide)

    g.wait(1, "down")
    g.start(2, "down")
    for k in others:
        up_to(k, True).wait_recv()
    own_up.wait()
    for j in range(n_t):
        rowf[pl.ds(part * j, part), :] = gin[j].astype(F32)
    g.own_wait(local, "down")
    g.wait(2, "down")

    @pl.loop(0, 3)
    def _(i):
        at = rows(i)
        mid = n1[at, :] * row(2) + row(3)
        res = mid + dots(act[at, :], wd[...], 1, 0) + row(4)
        normed, scaled = norm(res)
        up = rowf[at, :]
        small[2:3, 1536:2304] += total(up * normed)
        small[3:4, 0:768] += total(up)
        grad = back(up * row(5), normed, scaled)
        small[2:3, 768:1536] += total(grad)
        g2f[at, :] = grad
        rowb[at, :] = grad.astype(BF)
        rowf[at, :] = normed * row(5) + row(6)

    for j in range(n_t):
        slab[j] = rowf[pl.ds(part * j, part), :].astype(BF)
    for k in others:
        out_to(k).start()
    own_out = pltpu.make_async_copy(slab.at[rank], out.at[rank], local.at[n_reg, 2])
    own_out.start()

    early = 3
    ff, qa, qb = grad_ranges(n_t, unit_live, early)
    split, end = 512 * early, 512 * pairs

    def sub(ref, start, stop):
        return ref.at[:, pl.ds(start, stop - start)]

    grad_q = sub(wu, 0, end)
    chunk_d = Scatter(place, n_t, n_dp, ff, grad_d, dc, [d0, d1], [dz], [fd], dsend, drecv, dcred)
    chunk_u = Scatter(place, n_t, n_dp, ff, grad_u, uc, [u0, u1], [uz], [fu], usend, urecv, ucred)
    chunk_a = Scatter(place, n_t, n_dp, qa, sub(wu, 0, split), sub(dc, 0, split),
                      [sub(d0, 0, split), sub(d1, 0, split)], [az], [fq], qsend, qrecv, qcred)
    chunk_b = Scatter(place, n_t, n_dp, qb, sub(wu, split, end), sub(dc, split, end),
                      [sub(d0, split, end), sub(d1, split, end)], [bz, sz], [fq, fs], psend, precv,
                      pcred)

    def turn(ref):
        tr[...] = ref[...].astype(F32).T.astype(BF)

    def tiles(f, hook=None):
        @pl.loop(0, full)
        def _(n):
            if hook is not None:
                pl.when(n == hook[0])(hook[1])
            f(pl.ds(pl.multiple_of(n * wide, 128), wide))

        if units % wide:
            f(pl.ds(full * wide, units % wide))

    turn(rowb)

    def down_grad(at):
        grad_d[:, at] = dots(tr[...], act[:, at], 1, 0).astype(BF)

    tiles(down_grad)
    chunk_d.advance(0)
    turn(x_s)

    def up_grad(at):
        grad = dots(rowb[...], wd[at, :], 1, 1) * slope[:, at].astype(F32)
        small[0:1, at] = total(grad)
        low = grad.astype(BF)
        slope[:, at] = low
        grad_u[:, at] = dots(tr[...], low, 1, 0).astype(BF)

    tiles(up_grad, (6, lambda: chunk_d.advance(1)))
    chunk_u.advance(0)

    @pl.loop(0, 3)
    def _(i):
        at = rows(i)
        grad = dots(slope[at, :], wu[...], 1, 1) + g2f[at, :]
        normed = n1[at, :]
        small[1:2, 1536:2304] += total(grad * normed)
        small[2:3, 0:768] += total(grad)
        one = back(grad * row(2), normed, cr[at, HEAD : HEAD + 1])
        small[1:2, 768:1536] += total(one)
        g2f[at, :] = one
        rowb[at, :] = one.astype(BF)

        @pl.when(i == 1)
        def _():
            chunk_d.advance(2)
            chunk_u.advance(1)

    g.drain()
    turn(rowb)
    for p in range(pairs):
        grad_q[:, pl.ds(512 * p + 384, two)] = dots(
            tr[...], ctx[:, two * p : two * p + two], 1, 0).astype(BF)
    gc[...] = dots(rowb[...], wo[...], 1, 1).astype(BF)

    @pl.loop(0, 3)
    def _(i):
        x_s[rows(i), :] = hidden(rows(i)).astype(BF)

    turn(x_s)

    @pl.loop(0, pairs)
    def _(p):
        def hooks(table):
            for i, steps in table.items():
                @pl.when(p == i)
                def _(steps=steps):
                    for chunk, stage in steps:
                        chunk.advance(stage)

        hooks({2: [(chunk_d, 3)], 3: [(chunk_a, 0)], 4: [(chunk_u, 2), (chunk_a, 1)]})
        q_at, k_at, v_at = qkv_at(p)
        c_at = pl.ds(pl.multiple_of(p * two, 128), two)
        q, k, v, gctx = y_s[:, q_at], y_s[:, k_at], y_s[:, v_at], gc[:, c_at]
        gq, gk, gv = [], [], []
        for h in range(2):
            s_ref[...] = dots(v, gctx * half[h], 1, 1)
            for c0, cn in strips:
                gp = s_ref[:, c0 : c0 + cn]
                pr = p_s[2 * p + h, :, c0 : c0 + cn].astype(F32)
                dot = jnp.sum(gp * pr, axis=0, keepdims=True)
                gs_ref[:, c0 : c0 + cn] = (pr * (gp - dot)).astype(BF)
            gk.append(dots(gs_ref[...], q, 1, 0))
            gv.append(dots(p_s[2 * p + h], gctx, 1, 0))
            gq.append(dots(k, gs_ref[...], 0, 0))
        turned = jnp.concatenate([gq[0][:HEAD], gq[1][HEAD:]], axis=0).T * 0.125
        gq_low = turned.astype(BF)
        gv_low = jnp.where(first, gv[0], gv[1]).astype(BF)
        y_s[:, q_at] = gq_low
        y_s[:, k_at] = jnp.where(first, gk[0], gk[1]).astype(BF)
        y_s[:, v_at] = gv_low
        small[3:4, pl.ds(pl.multiple_of(768 + p * two, 128), two)] = total(gq_low.astype(F32))
        small[3:4, pl.ds(pl.multiple_of(768 + two * pairs + p * two, 128), two)] = total(
            gv_low.astype(F32))
        here = pl.ds(pl.multiple_of(p * 384, 128), 384)
        grad_q[:, pl.ds(pl.multiple_of(p * 512, 128), 384)] = dots(
            tr[...], y_s[:, here], 1, 0).astype(BF)

    chunk_b.advance(0)
    chunk_d.advance(4)

    @pl.loop(0, 3)
    def _(i):
        at = rows(i)
        grad = dots(y_s[at, :], wq[...], 1, 0) + g2f[at, :]
        covered = cr[at, 0:1] > 0.5
        small[1:2, 0:768] += total(jnp.where(covered, grad, 0.0))
        rowf[at, :] = 0.1 * jnp.where(covered, 0.0, grad)

    hops = [place.mate] + place.partner + place.outer(n_dp)

    def hop(j):
        return pltpu.make_async_remote_copy(
            src_ref=small, dst_ref=sgot.at[j], send_sem=ssend.at[j], recv_sem=srecv.at[j],
            device_id=(hops[j], place.rank), device_id_type=MESH)

    def zhop(k):
        j = len(hops) + k - 1
        return pltpu.make_async_remote_copy(
            src_ref=small, dst_ref=sgot.at[j], send_sem=ssend.at[j], recv_sem=srecv.at[j],
            device_id=(place.dp, (place.rank + k) % n_t), device_id_type=MESH)

    hop(0).start()
    for k in others:
        out_to(k).wait_send()
        out_to(k, True).wait_recv()
    own_out.wait()
    for j in range(n_t):
        slab[j] = rowf[pl.ds(part * j, part), :].astype(BF)
    for k in others:
        gin_to(k).start()
    own_gin = pltpu.make_async_copy(slab.at[rank], gin_out.at[rank], local.at[n_reg + 1, 0])
    own_gin.start()

    piece = width // 2

    def give_down():
        for block in range(2):
            val = fd[:, block * piece : block * piece + piece].astype(F32).T
            out_d[block * piece : block * piece + piece, :] = val.astype(BF)

    def round_of(j):
        hop(j - 1).wait()
        small[...] = small[...] + sgot[j - 1]
        hop(j).start()

    chunk_d.advance(5)
    chunk_b.advance(1)
    round_of(1)
    chunk_u.advance(3)
    chunk_d.advance(6)
    round_of(2)
    for j in range(3, len(hops)):
        round_of(j)
    chunk_d.advance(7)
    chunk_a.advance(2)
    hop(len(hops) - 1).wait()
    small[...] = small[...] + sgot[len(hops) - 1]
    for k in others:
        zhop(k).start()
    chunk_d.advance(8)
    chunk_b.advance(2)
    chunk_u.advance(4)
    chunk_a.advance(3)
    give_down()
    chunk_b.advance(3)
    chunk_a.advance(4)
    chunk_u.advance(5)
    chunk_b.advance(4)
    chunk_u.advance(6)
    chunk_a.advance(5)
    chunk_u.advance(7)
    chunk_b.advance(5)
    chunk_a.advance(6)
    chunk_u.advance(8)
    chunk_b.advance(6)
    chunk_a.advance(7)
    for k in others:
        zhop(k).wait()
    small[...] = small[...] + sgot[len(hops)] + sgot[len(hops) + 1] + sgot[len(hops) + 2]
    chunk_b.advance(7)
    chunk_a.advance(8)
    chunk_b.advance(8)
    for k in others:
        gin_to(k, True).wait_recv()
        gin_to(k).wait_send()
        up_to(k).wait_send()
        bias_to(k).wait_send()
    own_gin.wait()
    keep = 2 * rank < n_t

    for j in range(4):
        out_q[j, 0:two, :] = fq[:, two * j : two * j + two].astype(F32).T.astype(BF)
        val = fs[:, two * j : two * j + two].astype(F32).T
        val = jnp.where(rank == 0, val[:HEAD], val[HEAD:])
        out_q[j, two : two + HEAD, :] = jnp.where(keep, val, 0.0).astype(BF)
    lines[...] = jnp.zeros_like(lines)
    for i, (r, c) in enumerate(((1, 0), (1, 1), (1, 2), (2, 0), (2, 1), (2, 2), (3, 0))):
        lines[i : i + 1, :] = small[r : r + 1, c * width : c * width + width]
    at = 0
    for r in range(n_t):
        @pl.when(rank == r)
        def _(r=r, at=at):
            for i, base in ((7, width), (8, width + two * pairs)):
                c = base + two * r
                lines[i : i + 1, 0:two] = small[3:4, c : c + two]
                if 2 * r < n_t:
                    c = base + two * n_t + HEAD * r
                    lines[i : i + 1, two : two + HEAD] = small[3:4, c : c + HEAD]
            lines[9:10, 0 : unit_live[r]] = small[0:1, at : at + unit_live[r]]
        at += unit_live[r]
    for chunk in (chunk_d, chunk_u, chunk_a, chunk_b):
        chunk.drain()


def run_layer(n_t, n_dp, unit_live, features, starts, vectors, gup, *weights):
    frames, _, width = features.shape
    units = sum(unit_live)
    wide = max(unit_live)
    pairs = n_t + 1
    heads = 2 * pairs * HEAD
    n_reg = 6 * n_t + 4 * sum(2 * r < n_t for r in range(n_t))
    outer = n_outer(n_dp)
    piece = width // GROUP
    hops = 1 + BITS + outer + n_t - 1
    n_sem = 1 + 2 * BITS + 2 * outer + 2 * (n_t - 1) + 2 * (BITS + 1)
    small = (8, units)

    vm = pl.BlockSpec(memory_space=pltpu.VMEM)
    hb = pl.BlockSpec(memory_space=pl.ANY)
    dma = pltpu.SemaphoreType.DMA
    scratch = dict(
        wq=pltpu.VMEM((384 * pairs, width), BF), wo=pltpu.VMEM((heads, width), BF),
        wu=pltpu.VMEM((width, units), BF), wd=pltpu.VMEM((units, width), BF),
        feat=pltpu.VMEM((frames, width), BF), fbuf=pltpu.VMEM((frames // 8, n_t, width), BF),
        gb=pltpu.VMEM((n_t, 8, width), F32),
        by=pltpu.VMEM((pairs, 8, 384), F32), bu=pltpu.VMEM((8, units), F32),
        cr=pltpu.VMEM((frames, 128), F32), x_s=pltpu.VMEM((frames, width), BF),
        y_s=pltpu.VMEM((frames, 384 * pairs), BF),
        p_s=pltpu.VMEM((2 * pairs, frames, frames), BF), ctx=pltpu.VMEM((frames, heads), BF),
        n1=pltpu.VMEM((frames, width), F32),
        act=pltpu.VMEM((frames, units), BF), slope=pltpu.VMEM((frames, units), BF),
        rowf=pltpu.VMEM((frames, width), F32), g2f=pltpu.VMEM((frames, width), F32),
        rowb=pltpu.VMEM((frames, width), BF),
        s_ref=pltpu.VMEM((frames, frames), F32), gs_ref=pltpu.VMEM((frames, frames), BF),
        tr=pltpu.VMEM((width, frames), BF), slab=pltpu.VMEM((n_t, frames // n_t, width), BF),
        grad_d=pltpu.VMEM((width, units), BF), grad_u=pltpu.VMEM((width, units), BF),
        dc=pltpu.VMEM((width // 2, units), BF), d1=pltpu.VMEM((2 * piece, units), BF),
        d0=pltpu.VMEM((piece, units), BF), dz=pltpu.VMEM((n_t - 1, piece, wide), BF),
        uc=pltpu.VMEM((width // 2, units), BF), u1=pltpu.VMEM((2 * piece, units), BF),
        u0=pltpu.VMEM((piece, units), BF), uz=pltpu.VMEM((n_t - 1, piece, wide), BF),
        az=pltpu.VMEM((n_t - 1, piece, 512), BF), bz=pltpu.VMEM((n_t - 1, piece, 512), BF),
        sz=pltpu.VMEM((n_t - 1, piece, 512), BF),
        fd=pltpu.VMEM((width, wide), BF),
        fq=pltpu.VMEM((width, 512), BF), fs=pltpu.VMEM((width, 512), BF),
        bias=pltpu.VMEM((8, width), F32), small=pltpu.VMEM(small, F32),
        sgot=pltpu.VMEM((hops,) + small, F32),
        wsend=dma((n_reg, 3 * (n_t - 1) + BITS + 1)), wrecv=dma((n_reg, BITS + 4)),
        local=dma((n_reg + 2, 6)), bsend=dma((n_t - 1,)), brecv=dma((n_t - 1,)),
        isend=dma((n_t - 1,)), irecv=dma((n_t - 1,)), osend=dma((n_t - 1,)),
        orecv=dma((n_t - 1,)), gsend=dma((n_t - 1,)), grecv=dma((n_t - 1,)),
        dsend=dma((n_sem,)), drecv=dma((n_sem,)), usend=dma((n_sem,)), urecv=dma((n_sem,)),
        qsend=dma((n_sem,)), qrecv=dma((n_sem,)), psend=dma((n_sem,)), precv=dma((n_sem,)),
        ssend=dma((hops,)), srecv=dma((hops,)),
        **{n: pltpu.SemaphoreType.REGULAR((max(2 * outer, 1),)) for n in ("dc_", "uc_", "qc_", "pc_")},
    )
    slabs = jax.ShapeDtypeStruct((n_t, frames // n_t, width), BF)

    def f32(*shape):
        return jax.ShapeDtypeStruct(shape, F32)

    return pl.pallas_call(
        functools.partial(layer_kernel, n_t, n_dp, unit_live),
        out_shape=[slabs, slabs, jax.ShapeDtypeStruct((wide, width), BF),
                   jax.ShapeDtypeStruct((width, wide), BF),
                   jax.ShapeDtypeStruct((4, 3 * HEAD, width), BF), f32(16, width)],
        in_specs=[hb, pl.BlockSpec(memory_space=pltpu.SMEM)] + [vm] * 10 + [hb] * 7,
        out_specs=[hb] * 2 + [vm] * 4,
        scratch_shapes=list(scratch.values()),
        compiler_params=pltpu.CompilerParams(
            collective_id=0, has_side_effects=True, vmem_limit_bytes=67043328),
        name="layer",
    )(features, starts, *vectors, gup, *weights)


def body(features, mask_starts, mask_vector, query_weight, query_bias, key_weight, value_weight,
         value_bias, output_weight, output_bias, attn_gain, attn_shift, up_weight, up_bias,
         down_weight, down_bias, final_gain, final_shift, grad_output):
    frames, item_count, width = features.shape
    n_t = lax.axis_size("tensor")
    n_d = lax.axis_size("dp")
    rank = lax.axis_index("tensor")
    slots = query_weight.shape[1] // HEAD
    units = up_weight.shape[1]
    unit_live = [units if r == 0 else units * 5 // 6 for r in range(n_t)]
    if n_t != 4 or slots != 3 or item_count != n_t or n_d % GROUP:
        raise ValueError("unsupported sizes")
    vectors = [mask_vector, output_bias, attn_gain, attn_shift, down_bias, final_gain, final_shift,
               query_bias, value_bias, up_bias]
    out, gin, gwd, gwu, gqkvo, lines = run_layer(
        n_t, n_d, unit_live, features, mask_starts, vectors, grad_output.transpose(1, 0, 2),
        query_weight.T, key_weight.T, value_weight.T, output_weight, up_weight, down_weight)
    gm, gob, gag, gas, gdb, gfg, gfs, gqb, gvb, gub = [lines[i] for i in range(10)]
    cols = slots * HEAD
    gq, gk, gv, gwo = [gqkvo[i].astype(F32) for i in range(4)]
    return (out.transpose(1, 0, 2), gin.transpose(1, 0, 2), gm, gq.T, gqb[:cols], gk.T, gv.T,
            gvb[:cols], gwo, gob, gag, gas, gwu.astype(F32), gub, gwd.astype(F32), gdb, gfg, gfs)


def solution(mesh):
    return jax.shard_map(
        body,
        mesh=mesh,
        in_specs=(P(None, "dp", None), P("dp", None), P(), P(None, "tensor"), P("tensor"),
                  P(None, "tensor"), P(None, "tensor"), P("tensor"), P("tensor", None), P(), P(),
                  P(), P(None, "tensor"), P("tensor"), P("tensor", None), P(), P(), P(),
                  P("tensor", "dp", None)),
        out_specs=(P("tensor", "dp", None), P("tensor", "dp", None), P(), P(None, "tensor"),
                   P("tensor"), P(None, "tensor"), P(None, "tensor"), P("tensor"),
                   P("tensor", None), P(), P(), P(), P(None, "tensor"), P("tensor"),
                   P("tensor", None), P(), P(), P()),
        check_vma=False,
    )
```
